32 devices in a mesh: parts: 2 (over y), ctx: 4 (over z), head: 2 (over x), sub: 2 (over core).
Axes of the slice: x: 2, y: 2, z: 4, core: 2. Of those that a mesh axis runs over, the one named last changes fastest.
Arguments:
- queries: bfloat16 [1024, 12288], P(('parts', 'ctx'), ('head', 'sub')), parts along dimension 0, may hold values from -250 to 250
- latent: bfloat16 [1024, 512], P(('parts', 'ctx')), parts along dimension 0, may hold values from -6 to 6
- rope_keys: bfloat16 [1024, 64], P(('parts', 'ctx')), parts along dimension 0, may hold values from -4 to 4
- latent_gain: float32 [512], replicated, may hold values from 0.1 to 1.9
- up_weight: bfloat16 [512, 16384], P(None, ('head', 'sub')), may hold values from -0.25 to 0.25
- prompt_length: int32 [2], P('parts'), parts along dimension 0, may hold values from 256 to 512
Outputs:
- attended: bfloat16 [1024, 8192], P(('parts', 'ctx'), ('head', 'sub')), parts along dimension 0
The draws below stay inside these ranges and needn't reach their ends.
There are 2 independent parts, one for each index of `parts`. The reference program is written for one: setup_inputs(seed, part) draws one part's arguments, and reference() takes and returns one part's arrays. A program takes and returns all parts, laid end to end along the dimension named above; an argument that names none is the same for every part. Nothing has to cross between parts.
All inputs are finite; a program needn't handle non-finite values.
Results may differ from the reference program's by a relative error of at most 0.012.
Values may be sent and summed in bfloat16 or wider, within the bound.
No kernel may reach another device: no remote copies, remote signals or barrier semaphores. Data moves between devices by JAX's collectives and lax.ppermute only.
A program may use at most 128 MiB of HBM per device.

```python
import math
import jax
import jax.numpy as jnp
from jax import lax

HEADS = 64
LATENT = 512
ROPE = 64
NOPE = 128
VDIM = 128
SEQ = 512


def rope_pair(key):
    drawn_key = jax.random.fold_in(key, 11)
    drawn_rope = jnp.clip(jax.random.normal(drawn_key, (SEQ, ROPE), jnp.float32), -4.0, 4.0)
    return drawn_rope


def draw_rope_keys(key, part):
    drawn_rope = rope_pair(key)
    return drawn_rope.astype(jnp.bfloat16)


def draw_queries(key, part):
    background_key = jax.random.fold_in(key, 13)
    background = jnp.clip(2.5 * jax.random.normal(background_key, (SEQ, HEADS, NOPE + ROPE), jnp.float32), -10.0, 10.0)
    return background.reshape(SEQ, HEADS * (NOPE + ROPE)).astype(jnp.bfloat16)


def shard_levels(rng, extent, split, low, largest):
    level = 1.0
    for position, blocks in split:
        draws = jax.random.uniform(jax.random.fold_in(jax.random.fold_in(rng, 6), position), (blocks,), jnp.float32, low / len(split), largest / len(split))
        level = level * jnp.repeat(jnp.exp(draws), extent[position] // blocks).reshape((-1,) + (1,) * (len(extent) - 1 - position))
    return level


def scatter_about(rng, dims, deviation, most, split=(), kind=jnp.bfloat16):
    level = shard_levels(rng, dims, split, -0.22, 0.18) if split else 1.0
    drawn = jax.random.normal(rng, dims, jnp.float32) * deviation * level
    return jnp.minimum(jnp.maximum(drawn, -most), most).astype(kind)


def setup_inputs(seed: int = 0, part: int = 0) -> dict:
    seeds = jax.random.split(jax.random.key(seed), 7)
    own_keys = jax.random.split(jax.random.fold_in(seeds[6], part), 7)
    queries = draw_queries(jax.random.fold_in(jax.random.fold_in(seeds[6], part), 71), part)
    latent = scatter_about(own_keys[1], (SEQ, LATENT), 1.0, 6.0, ((0, 4),))
    rope_keys = draw_rope_keys(jax.random.fold_in(jax.random.fold_in(seeds[6], part), 71), part)
    latent_gain = jnp.clip(1.0 + 0.18 * jax.random.normal(seeds[3], (LATENT,), jnp.float32), 0.1, 1.9)
    up_weight = scatter_about(seeds[4], (LATENT, HEADS * (NOPE + VDIM)), LATENT ** -0.5, 0.25, ((1, 4),))
    prompt_length = jax.random.randint(own_keys[5], (1,), SEQ // 2, SEQ + 1).astype(jnp.int32)
    return dict(queries=queries, latent=latent, rope_keys=rope_keys, latent_gain=latent_gain, up_weight=up_weight, prompt_length=prompt_length)


def rotate(values, positions):
    half_width = values.shape[-1] // 2
    frequency = 10000.0 ** (-jnp.arange(half_width, dtype=jnp.float32) / half_width)
    angles = positions.astype(jnp.float32)[..., None] * frequency
    cosines = jnp.cos(angles)
    sines = jnp.sin(angles)
    lower_half = values[..., :half_width]
    upper_half = values[..., half_width:]
    return jnp.concatenate([lower_half * cosines - upper_half * sines, lower_half * sines + upper_half * cosines], -1)

def reference(queries, latent, rope_keys, latent_gain, up_weight, prompt_length):
    positions = jnp.arange(SEQ, dtype=jnp.int32)
    length = prompt_length[0]
    widened = latent.astype(jnp.float32)
    normed = (widened * lax.rsqrt(lax.optimization_barrier(jnp.mean(widened * widened, -1, keepdims=True)) + 1e-06) * latent_gain.astype(jnp.float32)).astype(jnp.bfloat16)
    key_rope = rotate(rope_keys.astype(jnp.float32), positions).astype(jnp.bfloat16)
    grouped = queries.reshape(SEQ, HEADS, NOPE + ROPE)
    query_nope = grouped[:, :, :NOPE]
    query_rope = rotate(grouped[:, :, NOPE:].astype(jnp.float32), positions[:, None]).astype(jnp.bfloat16)
    expanded = jnp.dot(normed, up_weight, preferred_element_type=jnp.float32).astype(jnp.bfloat16)
    expanded = expanded.reshape(SEQ, HEADS, NOPE + VDIM)
    allowed = (positions[None, :] <= positions[:, None]) & (positions[None, :] < length)
    scale_factor = 1.0 / math.sqrt(NOPE + ROPE)

    def one_head(head_items):
        nope_rows, rope_rows, keys_values = head_items
        scores = jnp.dot(nope_rows, keys_values[:, :NOPE].T, preferred_element_type=jnp.float32)
        scores = scores + jnp.dot(rope_rows, key_rope.T, preferred_element_type=jnp.float32)
        scores = jnp.where(allowed, scores * scale_factor, -1e+30)
        highest = lax.optimization_barrier(jnp.max(scores, -1, keepdims=True))
        raw_weights = jnp.where(allowed, jnp.exp(scores - highest), 0.0)
        running_sum = lax.optimization_barrier(jnp.sum(raw_weights, -1))
        mixed = jnp.dot(raw_weights.astype(jnp.bfloat16), keys_values[:, NOPE:], preferred_element_type=jnp.float32)
        return mixed / running_sum[:, None]
    head_outputs = lax.map(one_head, (query_nope.transpose(1, 0, 2), query_rope.transpose(1, 0, 2), expanded.transpose(1, 0, 2)))
    head_outputs = jnp.where(positions[None, :, None] < length, head_outputs, 0.0)
    return head_outputs.astype(jnp.bfloat16).transpose(1, 0, 2).reshape(SEQ, HEADS * VDIM)
```

```python
import functools
import math

import jax
import jax.numpy as jnp
import numpy as np
from jax import lax
from jax.experimental import pallas as pl
from jax.experimental.pallas import tpu as pltpu
from jax.sharding import PartitionSpec as P

ROPE = 64
NOPE = 128
VDIM = 128
WIDE = 128
FULL = 256
MASKED = -1e30
EXPONENT = math.log2(math.e) / math.sqrt(NOPE + ROPE)

VMEM = pl.BlockSpec(memory_space=pltpu.VMEM)
SMEM = pl.BlockSpec(memory_space=pltpu.SMEM)


def tables(positions):
    half = ROPE // 2
    frequency = np.float32(10000.0) ** (-np.arange(half, dtype=np.float32) / np.float32(half))
    angles = np.arange(positions, dtype=np.float32)[:, None] * frequency.astype(np.float32)
    cosines, sines = np.cos(angles), np.sin(angles)
    rows = np.concatenate([cosines, cosines, -sines, sines], 1).astype(np.float32)
    columns = np.concatenate([cosines, sines], 1).T.astype(np.float32)
    return rows, np.ascontiguousarray(columns)


def pack_kernel(latent, rope, gain, table, length, place, payload, piece):
    rows, width = latent.shape
    half = ROPE // 2
    wide = latent[...].astype(jnp.float32)
    mean = jnp.mean(wide * wide, -1, keepdims=True)
    normed = (wide * lax.rsqrt(mean + 1e-06) * gain[...]).astype(jnp.bfloat16)
    keys = rope[...].astype(jnp.float32)
    low, high = keys[:half], keys[half:]
    cosines, sines = table[:half], table[half:]
    rotated = jnp.concatenate([low * cosines - high * sines, low * sines + high * cosines], 0)
    position = place[0] * rows + lax.broadcasted_iota(jnp.int32, (WIDE - ROPE, rows), 1)
    first = lax.broadcasted_iota(jnp.int32, (WIDE - ROPE, rows), 0) == 0
    bias = jnp.where(first & (position >= length[0]), MASKED, 0.0)
    extra = jnp.concatenate([rotated, bias], 0).T.astype(jnp.bfloat16)
    payload[:, :width] = normed
    payload[:, width:] = extra
    size = piece.shape[0]
    for k in range(rows // size):

        @pl.when(place[1] == k)
        def _():
            piece[:, :width] = normed[k * size : (k + 1) * size]
            piece[:, width:] = extra[k * size : (k + 1) * size]


def own_kernel(heads, queries, payload, weight, table, expanded, full):
    rows = queries.shape[0]
    width = weight.shape[0]
    cosines = jnp.concatenate([table[:, :ROPE]] * 2, 1)
    sines = jnp.concatenate([table[:, ROPE:]] * 2, 1)
    lane = lax.broadcasted_iota(jnp.int32, (rows, 2 * ROPE), 1)
    lower = lane % ROPE < ROPE // 2
    tail = (lax.broadcasted_iota(jnp.int32, (rows, FULL - NOPE - ROPE), 1) == 0).astype(
        jnp.float32
    ).astype(jnp.bfloat16)
    each = NOPE + ROPE
    for i in range(heads // 2):
        pair = queries[:, 2 * each * i : 2 * each * (i + 1)]
        ropes = jnp.concatenate([pair[:, NOPE:each], pair[:, each + NOPE :]], 1).astype(jnp.float32)
        turned = jnp.where(
            lower, pltpu.roll(ropes, 2 * ROPE - ROPE // 2, 1), pltpu.roll(ropes, ROPE // 2, 1)
        )
        ropes = (ropes * cosines + turned * sines).astype(jnp.bfloat16)
        for e in range(2):
            at = FULL * (2 * i + e)
            full[:, at : at + NOPE] = pair[:, each * e : each * e + NOPE]
            full[:, at + NOPE : at + FULL] = jnp.concatenate(
                [ropes[:, ROPE * e : ROPE * (e + 1)], tail], 1
            )
    columns = NOPE + VDIM
    for i in range(heads // 2):
        at = slice(2 * columns * i, 2 * columns * (i + 1))
        expanded[:, at] = jnp.dot(
            payload[:, :width], weight[:, at], preferred_element_type=jnp.float32
        ).astype(jnp.bfloat16)


def attend_kernel(heads, distances, full, own, expanded, weight, *rest):
    count = len(distances)
    pieces, (length, place, out, keys, grown, scores, weights) = rest[:count], rest[count:]
    rows = full.shape[0]
    width = weight.shape[0]
    columns = NOPE + VDIM
    ctx, sub = place[0], place[1]
    keys[:rows, width:] = own[:, width:]
    spare = (lax.broadcasted_iota(jnp.int32, (1, WIDE), 1) == ROPE).astype(jnp.float32)
    spare = (spare * MASKED).astype(jnp.bfloat16)
    at = rows
    for ref, (even, odd) in zip(pieces, distances, strict=True):
        size = ref.shape[0]
        keys[at : at + size, :width] = ref[:, :width]
        there = ctx >= jnp.where(sub == 0, even, odd)
        last = ref[:, width:]
        keys[at : at + size, width:] = jnp.where(there, last, jnp.broadcast_to(spare, last.shape))
        at += size
    total = at
    row = lax.broadcasted_iota(jnp.int32, (rows, rows), 0)
    causal = lax.broadcasted_iota(jnp.int32, (rows, rows), 1) <= row
    live = ctx * rows + lax.broadcasted_iota(jnp.int32, (rows, 1), 0) < length[0]

    def grow(i):
        at = slice(2 * columns * i, 2 * columns * (i + 1))
        grown[i % 3, :rows] = expanded[:, at]
        grown[i % 3, rows:] = jnp.dot(
            keys[rows:, :width], weight[:, at], preferred_element_type=jnp.float32
        ).astype(jnp.bfloat16)

    def score(h):
        i, e = divmod(h, 2)
        nope = grown[i % 3, :, columns * e : columns * e + NOPE]
        whole = jnp.concatenate([nope, keys[:, width:]], 1)
        found = lax.dot_general(
            full[:, FULL * h : FULL * (h + 1)],
            whole,
            (((1,), (1,)), ((), ())),
            preferred_element_type=jnp.float32,
        )
        scores[h % 2, :, :rows] = jnp.where(causal, found[:, :rows], MASKED)
        scores[h % 2, :, rows:] = found[:, rows:]

    def soften(h):
        found = scores[h % 2]
        top = jnp.max(found, 1, keepdims=True)
        raw = jnp.exp2(found * EXPONENT - top * EXPONENT)
        weights[h % 2] = raw.astype(jnp.bfloat16)
        return jnp.sum(raw, 1, keepdims=True)

    def mix(h, total_h):
        i, e = divmod(h, 2)
        values = grown[i % 3, :, columns * e + NOPE : columns * (e + 1)]
        mixed = jnp.dot(weights[h % 2], values, preferred_element_type=jnp.float32)
        out[:, VDIM * h : VDIM * (h + 1)] = jnp.where(live, mixed / total_h, 0.0).astype(
            jnp.bfloat16
        )

    totals = {}
    grow(0)
    for t in range(heads + 2):
        if t % 2 == 0 and t // 2 + 1 < heads // 2:
            grow(t // 2 + 1)
        if t < heads:
            score(t)
        if 0 <= t - 1 < heads:
            totals[t - 1] = soften(t - 1)
        if 0 <= t - 2 < heads:
            mix(t - 2, totals.pop(t - 2))


def in_vmem(x):
    return pltpu.with_memory_space_constraint(x, pltpu.VMEM)


def per_device(
    ctx_size, sub_size, queries, latent, rope_keys, latent_gain, up_weight, prompt_length
):
    rows, width = latent.shape
    heads = up_weight.shape[1] // (NOPE + VDIM)
    ctx = lax.axis_index("ctx")
    sub = lax.axis_index("sub")
    place = jnp.stack([ctx, sub]).astype(jnp.int32)
    by_row, by_column = tables(ctx_size * rows)
    row_table = lax.dynamic_slice_in_dim(jnp.asarray(by_row), ctx * rows, rows, 0)
    column_table = lax.dynamic_slice_in_dim(jnp.asarray(by_column), ctx * rows, rows, 1)

    bf16 = jnp.bfloat16
    wide = width + WIDE
    payload, piece = pl.pallas_call(
        pack_kernel,
        in_specs=[VMEM] * 4 + [SMEM] * 2,
        out_specs=[VMEM] * 2,
        out_shape=[
            jax.ShapeDtypeStruct((rows, wide), bf16),
            jax.ShapeDtypeStruct((rows // sub_size, wide), bf16),
        ],
        name="pack",
    )(latent, rope_keys.T, latent_gain.reshape(1, width), column_table, prompt_length, place)

    cores = ("ctx", "sub")
    whole_sets = (ctx_size - 1) // sub_size
    direct, distances = [], []
    for d in range(whole_sets * sub_size + 1, ctx_size):
        pairs = [
            (c * sub_size + s, (c + d) * sub_size + s)
            for c in range(ctx_size - d)
            for s in range(sub_size)
        ]
        direct.append(lax.ppermute(piece, cores, pairs))
        distances.append([d] * sub_size)
    for k in range(whole_sets):
        pairs = [
            (c * sub_size + s, (c + k * sub_size + 1 + s) * sub_size + s)
            for s in range(sub_size)
            for c in range(ctx_size - (k * sub_size + 1 + s))
        ]
        direct.append(lax.ppermute(payload, cores, pairs))
        distances.append([k * sub_size + 1 + s for s in range(sub_size)])

    expanded, full = pl.pallas_call(
        functools.partial(own_kernel, heads),
        in_specs=[VMEM] * 4,
        out_specs=[VMEM] * 2,
        out_shape=[
            jax.ShapeDtypeStruct((rows, up_weight.shape[1]), bf16),
            jax.ShapeDtypeStruct((rows, heads * FULL), bf16),
        ],
        name="own",
        cost_estimate=pl.CostEstimate(
            flops=2 * rows * width * up_weight.shape[1],
            bytes_accessed=2 * (queries.size + up_weight.size + 2 * rows * up_weight.shape[1]),
            transcendentals=0,
        ),
    )(queries, payload, up_weight, row_table)

    together = jnp.concatenate(direct, 0)
    pieces, both = [together], [distances]
    arrivals = list(zip(direct, distances, strict=True))
    for r in range(1, sub_size):
        swapped = lax.ppermute(together, "sub", [(s, (s + r) % sub_size) for s in range(sub_size)])
        at = 0
        for part, dist in zip(direct, distances, strict=True):
            arrivals.append(
                (
                    swapped[at : at + part.shape[0]],
                    [dist[(s - r) % sub_size] for s in range(sub_size)],
                )
            )
            at += part.shape[0]
    parts = [a for a, _ in arrivals]
    total = rows + sum(p.shape[0] for p in parts)

    return pl.pallas_call(
        functools.partial(attend_kernel, heads, [(d[0], d[-1]) for _, d in arrivals]),
        in_specs=[VMEM] * (4 + len(parts)) + [SMEM] * 2,
        out_specs=VMEM,
        out_shape=jax.ShapeDtypeStruct((rows, heads * VDIM), bf16),
        scratch_shapes=[
            pltpu.VMEM((total, wide), bf16),
            pltpu.VMEM((3, total, 2 * (NOPE + VDIM)), bf16),
            pltpu.VMEM((2, rows, total), jnp.float32),
            pltpu.VMEM((2, rows, total), bf16),
        ],
        name="attend",
        cost_estimate=pl.CostEstimate(
            flops=2 * total * (width + 2 * rows) * up_weight.shape[1],
            bytes_accessed=2 * (up_weight.size + 3 * rows * up_weight.shape[1]),
            transcendentals=heads * rows * total,
        ),
    )(full, payload, expanded, up_weight, *parts, prompt_length, place)


def solution(mesh):
    placed = (
        P(("parts", "ctx"), ("head", "sub")),
        P(("parts", "ctx"), None),
        P(("parts", "ctx"), None),
        P(),
        P(None, ("head", "sub")),
        P("parts"),
    )
    return jax.shard_map(
        functools.partial(per_device, mesh.shape["ctx"], mesh.shape["sub"]),
        mesh=mesh,
        in_specs=placed,
        out_specs=P(("parts", "ctx"), ("head", "sub")),
        check_vma=False,
    )
```

```python
import functools
import math

import jax
import jax.numpy as jnp
import numpy as np
from jax import lax
from jax.experimental import pallas as pl
from jax.experimental.pallas import tpu as pltpu
from jax.sharding import PartitionSpec as P

ROPE = 64
NOPE = 128
VDIM = 128
WIDE = 128
FULL = 256
MASKED = -1e30
MIB = 1024 * 1024
EXPONENT = math.log2(math.e) / math.sqrt(NOPE + ROPE)

VMEM = pl.BlockSpec(memory_space=pltpu.VMEM)
SMEM = pl.BlockSpec(memory_space=pltpu.SMEM)
ANY = pl.BlockSpec(memory_space=pl.ANY)


def tables(positions):
    half = ROPE // 2
    frequency = np.float32(10000.0) ** (-np.arange(half, dtype=np.float32) / np.float32(half))
    angles = np.arange(positions, dtype=np.float32)[:, None] * frequency.astype(np.float32)
    cosines, sines = np.cos(angles), np.sin(angles)
    rows = np.concatenate([cosines, cosines, -sines, sines], 1).astype(np.float32)
    columns = np.concatenate([cosines, sines], 1).T.astype(np.float32)
    return rows, np.ascontiguousarray(columns)


def pack_kernel(latent, rope, gain, tables_hbm, length, payload, piece, table, arrived):
    rows, width = latent.shape
    half = ROPE // 2
    ctx, sub = lax.axis_index("ctx"), lax.axis_index("sub")
    copy = pltpu.make_async_copy(tables_hbm.at[ctx], table, arrived)
    copy.start()
    wide = latent[...].astype(jnp.float32)
    mean = jnp.mean(wide * wide, -1, keepdims=True)
    normed = (wide * lax.rsqrt(mean + 1e-06) * gain[...]).astype(jnp.bfloat16)
    keys = rope[...].astype(jnp.float32)
    low, high = keys[:half], keys[half:]
    copy.wait()
    cosines, sines = table[:half], table[half:]
    rotated = jnp.concatenate([low * cosines - high * sines, low * sines + high * cosines], 0)
    position = ctx * rows + lax.broadcasted_iota(jnp.int32, (WIDE - ROPE, rows), 1)
    first = lax.broadcasted_iota(jnp.int32, (WIDE - ROPE, rows), 0) == 0
    bias = jnp.where(first & (position >= length[0]), MASKED, 0.0)
    extra = jnp.concatenate([rotated, bias], 0).T.astype(jnp.bfloat16)
    payload[:, :width] = normed
    payload[:, width:] = extra
    size = piece.shape[0]
    for k in range(rows // size):

        @pl.when(sub == k)
        def _():
            piece[:, :width] = normed[k * size : (k + 1) * size]
            piece[:, width:] = extra[k * size : (k + 1) * size]


def own_kernel(heads, queries, payload, weight, tables_hbm, expanded, full, table, arrived):
    copy = pltpu.make_async_copy(tables_hbm.at[lax.axis_index("ctx")], table, arrived)
    copy.start()
    copy.wait()
    rows = queries.shape[0]
    width = weight.shape[0]
    cosines = jnp.concatenate([table[:, :ROPE]] * 2, 1)
    sines = jnp.concatenate([table[:, ROPE:]] * 2, 1)
    lane = lax.broadcasted_iota(jnp.int32, (rows, 2 * ROPE), 1)
    lower = lane % ROPE < ROPE // 2
    tail = (lax.broadcasted_iota(jnp.int32, (rows, FULL - NOPE - ROPE), 1) == 0).astype(
        jnp.float32
    ).astype(jnp.bfloat16)
    each = NOPE + ROPE
    for i in range(heads // 2):
        pair = queries[:, 2 * each * i : 2 * each * (i + 1)]
        ropes = jnp.concatenate([pair[:, NOPE:each], pair[:, each + NOPE :]], 1).astype(jnp.float32)
        turned = jnp.where(
            lower, pltpu.roll(ropes, 2 * ROPE - ROPE // 2, 1), pltpu.roll(ropes, ROPE // 2, 1)
        )
        ropes = (ropes * cosines + turned * sines).astype(jnp.bfloat16)
        for e in range(2):
            at = FULL * (2 * i + e)
            full[:, at : at + NOPE] = pair[:, each * e : each * e + NOPE]
            full[:, at + NOPE : at + FULL] = jnp.concatenate(
                [ropes[:, ROPE * e : ROPE * (e + 1)], tail], 1
            )
    columns = NOPE + VDIM
    for i in range(heads // 2):
        at = slice(2 * columns * i, 2 * columns * (i + 1))
        expanded[:, at] = jnp.dot(
            payload[:, :width], weight[:, at], preferred_element_type=jnp.float32
        ).astype(jnp.bfloat16)


def attend_kernel(heads, distances, full, own, expanded, weight, *rest):
    count = len(distances)
    pieces, (length, out, keys, grown, scores, weights) = rest[:count], rest[count:]
    rows = full.shape[0]
    width = weight.shape[0]
    columns = NOPE + VDIM
    ctx, sub = lax.axis_index("ctx"), lax.axis_index("sub")
    keys[:rows, width:] = own[:, width:]
    spare = (lax.broadcasted_iota(jnp.int32, (1, WIDE), 1) == ROPE).astype(jnp.float32)
    spare = (spare * MASKED).astype(jnp.bfloat16)
    at = rows
    for ref, inside in zip(pieces, distances, strict=True):
        begin = 0
        for size, by_core in inside:
            piece = slice(begin, begin + size)
            keys[at : at + size, :width] = ref[piece, :width]
            distance = sum(jnp.where(sub == s, d, 0) for s, d in enumerate(by_core))
            last = ref[piece, width:]
            keys[at : at + size, width:] = jnp.where(
                ctx >= distance, last, jnp.broadcast_to(spare, last.shape)
            )
            at += size
            begin += size
    row = lax.broadcasted_iota(jnp.int32, (rows, rows), 0)
    causal = lax.broadcasted_iota(jnp.int32, (rows, rows), 1) <= row
    live = ctx * rows + lax.broadcasted_iota(jnp.int32, (rows, 1), 0) < length[0]

    def grow(i):
        at = slice(2 * columns * i, 2 * columns * (i + 1))
        grown[i % 3, :rows] = expanded[:, at]
        grown[i % 3, rows:] = jnp.dot(
            keys[rows:, :width], weight[:, at], preferred_element_type=jnp.float32
        ).astype(jnp.bfloat16)

    def score(h):
        i, e = divmod(h, 2)
        nope = grown[i % 3, :, columns * e : columns * e + NOPE]
        whole = jnp.concatenate([nope, keys[:, width:]], 1)
        found = lax.dot_general(
            full[:, FULL * h : FULL * (h + 1)],
            whole,
            (((1,), (1,)), ((), ())),
            preferred_element_type=jnp.float32,
        )
        scores[h % 2, :, :rows] = jnp.where(causal, found[:, :rows], MASKED)
        scores[h % 2, :, rows:] = found[:, rows:]

    def soften(h):
        found = scores[h % 2]
        top = jnp.max(found, 1, keepdims=True)
        raw = jnp.exp2(found * EXPONENT - top * EXPONENT)
        weights[h % 2] = raw.astype(jnp.bfloat16)
        return jnp.sum(raw, 1, keepdims=True)

    def mix(h, total_h):
        i, e = divmod(h, 2)
        values = grown[i % 3, :, columns * e + NOPE : columns * (e + 1)]
        mixed = jnp.dot(weights[h % 2], values, preferred_element_type=jnp.float32)
        out[:, VDIM * h : VDIM * (h + 1)] = jnp.where(live, mixed / total_h, 0.0).astype(
            jnp.bfloat16
        )

    totals = {}
    grow(0)
    for t in range(heads + 2):
        if t % 2 == 0 and t // 2 + 1 < heads // 2:
            grow(t // 2 + 1)
        if t < heads:
            score(t)
        if 0 <= t - 1 < heads:
            totals[t - 1] = soften(t - 1)
        if 0 <= t - 2 < heads:
            mix(t - 2, totals.pop(t - 2))


def per_device(
    ctx_size, sub_size, queries, latent, rope_keys, latent_gain, up_weight, prompt_length
):
    rows, width = latent.shape
    heads = up_weight.shape[1] // (NOPE + VDIM)
    by_row, by_column = tables(ctx_size * rows)
    by_row = by_row.reshape(ctx_size, rows, 2 * ROPE)
    by_column = by_column.reshape(ROPE, ctx_size, rows).transpose(1, 0, 2)

    bf16 = jnp.bfloat16
    wide = width + WIDE
    payload, piece = pl.pallas_call(
        pack_kernel,
        in_specs=[VMEM] * 3 + [ANY, SMEM],
        out_specs=[VMEM] * 2,
        out_shape=[
            jax.ShapeDtypeStruct((rows, wide), bf16),
            jax.ShapeDtypeStruct((rows // sub_size, wide), bf16),
        ],
        scratch_shapes=[pltpu.VMEM((ROPE, rows), jnp.float32), pltpu.SemaphoreType.DMA],
        compiler_params=pltpu.CompilerParams(vmem_limit_bytes=4 * MIB),
        name="pack",
    )(latent, rope_keys.T, latent_gain.reshape(1, width), jnp.asarray(by_column), prompt_length)

    cores = ("ctx", "sub")
    whole_sets = (ctx_size - 1) // sub_size
    direct, distances = [], []
    for d in range(whole_sets * sub_size + 1, ctx_size):
        pairs = [
            (c * sub_size + s, (c + d) * sub_size + s)
            for c in range(ctx_size - d)
            for s in range(sub_size)
        ]
        direct.append(lax.ppermute(piece, cores, pairs))
        distances.append((piece.shape[0], [d] * sub_size))
    for k in range(whole_sets):
        pairs = [
            (c * sub_size + s, (c + k * sub_size + 1 + s) * sub_size + s)
            for s in range(sub_size)
            for c in range(ctx_size - (k * sub_size + 1 + s))
        ]
        direct.append(lax.ppermute(payload, cores, pairs))
        distances.append((rows, [k * sub_size + 1 + s for s in range(sub_size)]))

    expanded, full = pl.pallas_call(
        functools.partial(own_kernel, heads),
        in_specs=[VMEM] * 3 + [ANY],
        out_specs=[VMEM] * 2,
        out_shape=[
            jax.ShapeDtypeStruct((rows, up_weight.shape[1]), bf16),
            jax.ShapeDtypeStruct((rows, heads * FULL), bf16),
        ],
        scratch_shapes=[pltpu.VMEM((rows, 2 * ROPE), jnp.float32), pltpu.SemaphoreType.DMA],
        compiler_params=pltpu.CompilerParams(
            vmem_limit_bytes=4 * MIB
            + 2 * (queries.size + up_weight.size + 2 * rows * up_weight.shape[1])
        ),
        name="own",
        cost_estimate=pl.CostEstimate(
            flops=2 * rows * width * up_weight.shape[1],
            bytes_accessed=2 * (queries.size + up_weight.size + 2 * rows * up_weight.shape[1]),
            transcendentals=0,
        ),
    )(queries, payload, up_weight, jnp.asarray(by_row))

    *direct, expanded, full = lax.optimization_barrier((*direct, expanded, full))
    together = jnp.concatenate(direct, 0)
    pieces, inside = [together], [distances]
    for r in range(1, sub_size):
        pairs = [(s, (s + r) % sub_size) for s in range(sub_size)]
        pieces.append(lax.ppermute(together, "sub", pairs))
        inside.append(
            [(size, [d[(s - r) % sub_size] for s in range(sub_size)]) for size, d in distances]
        )
    total = rows + sum(p.shape[0] for p in pieces)
    held = (full, expanded, up_weight, *pieces)
    scratch = 2 * total * (wide + 6 * (NOPE + VDIM) + 6 * rows)

    return pl.pallas_call(
        functools.partial(attend_kernel, heads, inside),
        in_specs=[VMEM] * (4 + len(pieces)) + [SMEM],
        out_specs=VMEM,
        out_shape=jax.ShapeDtypeStruct((rows, heads * VDIM), bf16),
        scratch_shapes=[
            pltpu.VMEM((total, wide), bf16),
            pltpu.VMEM((3, total, 2 * (NOPE + VDIM)), bf16),
            pltpu.VMEM((2, rows, total), jnp.float32),
            pltpu.VMEM((2, rows, total), bf16),
        ],
        compiler_params=pltpu.CompilerParams(
            vmem_limit_bytes=6 * MIB + 2 * sum(x.size for x in held) + scratch
        ),
        name="attend",
        cost_estimate=pl.CostEstimate(
            flops=2 * total * (width + 2 * rows) * up_weight.shape[1],
            bytes_accessed=2 * (up_weight.size + 3 * rows * up_weight.shape[1]),
            transcendentals=heads * rows * total,
        ),
    )(full, payload, expanded, up_weight, *pieces, prompt_length)


def solution(mesh):
    placed = (
        P(("parts", "ctx"), ("head", "sub")),
        P(("parts", "ctx"), None),
        P(("parts", "ctx"), None),
        P(),
        P(None, ("head", "sub")),
        P("parts"),
    )
    return jax.shard_map(
        functools.partial(per_device, mesh.shape["ctx"], mesh.shape["sub"]),
        mesh=mesh,
        in_specs=placed,
        out_specs=P(("parts", "ctx"), ("head", "sub")),
        check_vma=False,
    )
```

```python
import functools
import math

import jax
import jax.numpy as jnp
import numpy as np
from jax import lax
from jax.experimental import pallas as pl
from jax.experimental.pallas import tpu as pltpu
from jax.sharding import PartitionSpec as P

ROPE = 64
NOPE = 128
VDIM = 128
WIDE = 128
FULL = 256
MASKED = -1e30
MIB = 1024 * 1024
PACK_FLOPS = 4 * 10**9
EXPONENT = math.log2(math.e) / math.sqrt(NOPE + ROPE)

VMEM = pl.BlockSpec(memory_space=pltpu.VMEM)
SMEM = pl.BlockSpec(memory_space=pltpu.SMEM)
HBM = pl.BlockSpec(memory_space=pltpu.HBM)
ANY = pl.BlockSpec(memory_space=pl.ANY)


def tables(positions):
    half = ROPE // 2
    frequency = np.float32(10000.0) ** (-np.arange(half, dtype=np.float32) / np.float32(half))
    angles = np.arange(positions, dtype=np.float32)[:, None] * frequency.astype(np.float32)
    cosines, sines = np.cos(angles), np.sin(angles)
    rows = np.concatenate([cosines, cosines, -sines, sines], 1).astype(np.float32)
    columns = np.concatenate([cosines, sines], 1).T.astype(np.float32)
    return rows, np.ascontiguousarray(columns)


def pack_kernel(
    latent_hbm, rope_hbm, gain_hbm, tables_hbm, length, payload, piece, latent, rope, gain, table, arrived
):
    rows, width = latent.shape
    half = ROPE // 2
    ctx, sub = lax.axis_index("ctx"), lax.axis_index("sub")
    copies = [
        pltpu.make_async_copy(source, target, arrived.at[k])
        for k, (source, target) in enumerate(
            [(latent_hbm, latent), (gain_hbm, gain), (rope_hbm, rope), (tables_hbm.at[ctx], table)]
        )
    ]
    for copy in copies:
        copy.start()
    for copy in copies:
        copy.wait()
    wide = latent[...].astype(jnp.float32)
    mean = jnp.mean(wide * wide, -1, keepdims=True)
    normed = (wide * lax.rsqrt(mean + 1e-06) * gain[...]).astype(jnp.bfloat16)
    keys = rope[...].astype(jnp.float32)
    low, high = keys[:half], keys[half:]
    cosines, sines = table[:half], table[half:]
    rotated = jnp.concatenate([low * cosines - high * sines, low * sines + high * cosines], 0)
    position = ctx * rows + lax.broadcasted_iota(jnp.int32, (WIDE - ROPE, rows), 1)
    first = lax.broadcasted_iota(jnp.int32, (WIDE - ROPE, rows), 0) == 0
    bias = jnp.where(first & (position >= length[0]), MASKED, 0.0)
    extra = jnp.concatenate([rotated, bias], 0).T.astype(jnp.bfloat16)
    payload[:, :width] = normed
    payload[:, width:] = extra
    size = piece.shape[0]
    for k in range(rows // size):

        @pl.when(sub == k)
        def _():
            piece[:, :width] = normed[k * size : (k + 1) * size]
            piece[:, width:] = extra[k * size : (k + 1) * size]


def own_kernel(heads, queries, payload, weight, tables_hbm, expanded, full, table, arrived):
    copy = pltpu.make_async_copy(tables_hbm.at[lax.axis_index("ctx")], table, arrived)
    copy.start()
    copy.wait()
    rows = queries.shape[0]
    width = weight.shape[0]
    cosines = jnp.concatenate([table[:, :ROPE]] * 2, 1)
    sines = jnp.concatenate([table[:, ROPE:]] * 2, 1)
    lane = lax.broadcasted_iota(jnp.int32, (rows, 2 * ROPE), 1)
    lower = lane % ROPE < ROPE // 2
    tail = (lax.broadcasted_iota(jnp.int32, (rows, FULL - NOPE - ROPE), 1) == 0).astype(
        jnp.float32
    ).astype(jnp.bfloat16)
    each = NOPE + ROPE
    for i in range(heads // 2):
        pair = queries[:, 2 * each * i : 2 * each * (i + 1)]
        ropes = jnp.concatenate([pair[:, NOPE:each], pair[:, each + NOPE :]], 1).astype(jnp.float32)
        turned = jnp.where(
            lower, pltpu.roll(ropes, 2 * ROPE - ROPE // 2, 1), pltpu.roll(ropes, ROPE // 2, 1)
        )
        ropes = (ropes * cosines + turned * sines).astype(jnp.bfloat16)
        for e in range(2):
            at = FULL * (2 * i + e)
            full[:, at : at + NOPE] = pair[:, each * e : each * e + NOPE]
            full[:, at + NOPE : at + FULL] = jnp.concatenate(
                [ropes[:, ROPE * e : ROPE * (e + 1)], tail], 1
            )
    columns = NOPE + VDIM
    for i in range(heads // 2):
        at = slice(2 * columns * i, 2 * columns * (i + 1))
        expanded[:, at] = jnp.dot(
            payload[:, :width], weight[:, at], preferred_element_type=jnp.float32
        ).astype(jnp.bfloat16)


def attend_kernel(heads, layout, levels, full, own, expanded, weight, *rest):
    count = len(rest) - 6
    pieces, (length, out, keys, grown, scores, weights) = rest[:count], rest[count:]
    rows = full.shape[0]
    width = weight.shape[0]
    columns = NOPE + VDIM
    ctx, sub = lax.axis_index("ctx"), lax.axis_index("sub")
    row = lax.broadcasted_iota(jnp.int32, (rows, rows), 0)
    causal = lax.broadcasted_iota(jnp.int32, (rows, rows), 1) <= row
    live = ctx * rows + lax.broadcasted_iota(jnp.int32, (rows, 1), 0) < length[0]

    def run(total):
        keys[:rows, width:] = own[:, width:]
        spare = (lax.broadcasted_iota(jnp.int32, (1, WIDE), 1) == ROPE).astype(jnp.float32)
        spare = (spare * MASKED).astype(jnp.bfloat16)
        at = rows
        for which, begin, size, by_core in layout:
            if at >= total:
                break
            ref, piece = pieces[which], slice(begin, begin + size)
            keys[at : at + size, :width] = ref[piece, :width]
            distance = sum(jnp.where(sub == s, d, 0) for s, d in enumerate(by_core))
            last = ref[piece, width:]
            keys[at : at + size, width:] = jnp.where(
                ctx >= distance, last, jnp.broadcast_to(spare, last.shape)
            )
            at += size

        def grow(i):
            at = slice(2 * columns * i, 2 * columns * (i + 1))
            grown[i % 3, :rows] = expanded[:, at]
            if total > rows:
                grown[i % 3, rows:total] = jnp.dot(
                    keys[rows:total, :width], weight[:, at], preferred_element_type=jnp.float32
                ).astype(jnp.bfloat16)

        def score(h):
            i, e = divmod(h, 2)
            nope = grown[i % 3, :total, columns * e : columns * e + NOPE]
            whole = jnp.concatenate([nope, keys[:total, width:]], 1)
            found = lax.dot_general(
                full[:, FULL * h : FULL * (h + 1)],
                whole,
                (((1,), (1,)), ((), ())),
                preferred_element_type=jnp.float32,
            )
            scores[h % 2, :, :rows] = jnp.where(causal, found[:, :rows], MASKED)
            if total > rows:
                scores[h % 2, :, rows:total] = found[:, rows:]

        def soften(h):
            found = scores[h % 2, :, :total]
            top = jnp.max(found, 1, keepdims=True)
            raw = jnp.exp2(found * EXPONENT - top * EXPONENT)
            weights[h % 2, :, :total] = raw.astype(jnp.bfloat16)
            return jnp.sum(raw, 1, keepdims=True)

        def mix(h, total_h):
            i, e = divmod(h, 2)
            values = grown[i % 3, :total, columns * e + NOPE : columns * (e + 1)]
            mixed = jnp.dot(weights[h % 2, :, :total], values, preferred_element_type=jnp.float32)
            out[:, VDIM * h : VDIM * (h + 1)] = jnp.where(live, mixed / total_h, 0.0).astype(
                jnp.bfloat16
            )

        totals = {}
        grow(0)
        for t in range(heads + 2):
            if t % 2 == 0 and t // 2 + 1 < heads // 2:
                grow(t // 2 + 1)
            if t < heads:
                score(t)
            if 0 <= t - 1 < heads:
                totals[t - 1] = soften(t - 1)
            if 0 <= t - 2 < heads:
                mix(t - 2, totals.pop(t - 2))

    above = -1
    for last, total in levels:

        @pl.when((ctx > above) & (ctx <= last))
        def _():
            run(total)

        above = last


def in_hbm(x):
    return pltpu.with_memory_space_constraint(x, pltpu.HBM)


def per_device(
    ctx_size, sub_size, queries, latent, rope_keys, latent_gain, up_weight, prompt_length
):
    rows, width = latent.shape
    heads = up_weight.shape[1] // (NOPE + VDIM)
    by_row, by_column = tables(ctx_size * rows)
    by_row = by_row.reshape(ctx_size, rows, 2 * ROPE)
    by_column = by_column.reshape(ROPE, ctx_size, rows).transpose(1, 0, 2)

    bf16 = jnp.bfloat16
    wide = width + WIDE
    payload, piece = pl.pallas_call(
        pack_kernel,
        in_specs=[HBM] * 4 + [SMEM],
        out_specs=[VMEM] * 2,
        out_shape=[
            jax.ShapeDtypeStruct((rows, wide), bf16),
            jax.ShapeDtypeStruct((rows // sub_size, wide), bf16),
        ],
        scratch_shapes=[
            pltpu.VMEM((rows, width), bf16),
            pltpu.VMEM((ROPE, rows), bf16),
            pltpu.VMEM((1, width), jnp.float32),
            pltpu.VMEM((ROPE, rows), jnp.float32),
            pltpu.SemaphoreType.DMA((4,)),
        ],
        cost_estimate=pl.CostEstimate(
            flops=PACK_FLOPS, bytes_accessed=8 * rows * width, transcendentals=0
        ),
        compiler_params=pltpu.CompilerParams(vmem_limit_bytes=4 * MIB),
        name="pack",
    )(
        in_hbm(latent),
        in_hbm(rope_keys.T),
        in_hbm(latent_gain.reshape(1, width)),
        in_hbm(jnp.asarray(by_column)),
        prompt_length,
    )

    cores = ("ctx", "sub")
    whole_sets = (ctx_size - 1) // sub_size
    direct, distances = [], []
    for k in range(whole_sets):
        pairs = [
            (c * sub_size + s, (c + k * sub_size + 1 + s) * sub_size + s)
            for s in range(sub_size)
            for c in range(ctx_size - (k * sub_size + 1 + s))
        ]
        direct.append(lax.ppermute(payload, cores, pairs))
        distances.append([k * sub_size + 1 + s for s in range(sub_size)])
    for d in range(whole_sets * sub_size + 1, ctx_size):
        pairs = [
            (c * sub_size + s, (c + d) * sub_size + s)
            for c in range(ctx_size - d)
            for s in range(sub_size)
        ]
        direct.append(lax.ppermute(piece, cores, pairs))
        distances.append([d] * sub_size)

    expanded, full = pl.pallas_call(
        functools.partial(own_kernel, heads),
        in_specs=[VMEM] * 3 + [ANY],
        out_specs=[VMEM] * 2,
        out_shape=[
            jax.ShapeDtypeStruct((rows, up_weight.shape[1]), bf16),
            jax.ShapeDtypeStruct((rows, heads * FULL), bf16),
        ],
        scratch_shapes=[pltpu.VMEM((rows, 2 * ROPE), jnp.float32), pltpu.SemaphoreType.DMA],
        compiler_params=pltpu.CompilerParams(
            vmem_limit_bytes=4 * MIB
            + 2 * (queries.size + up_weight.size + 2 * rows * up_weight.shape[1])
        ),
        name="own",
        cost_estimate=pl.CostEstimate(
            flops=2 * rows * width * up_weight.shape[1],
            bytes_accessed=2 * (queries.size + up_weight.size + 2 * rows * up_weight.shape[1]),
            transcendentals=0,
        ),
    )(queries, payload, up_weight, jnp.asarray(by_row))

    *direct, expanded, full = lax.optimization_barrier((*direct, expanded, full))
    together = jnp.concatenate(direct, 0)
    pieces = [together]
    for r in range(1, sub_size):
        pairs = [(s, (s + r) % sub_size) for s in range(sub_size)]
        pieces.append(lax.ppermute(together, "sub", pairs))
    layout, begin = [], 0
    for part, by_core in zip(direct, distances, strict=True):
        for r in range(sub_size):
            turned = [by_core[(s - r) % sub_size] for s in range(sub_size)]
            layout.append((r, begin, part.shape[0], turned))
        begin += part.shape[0]
    total = rows + sum(p.shape[0] for p in pieces)
    levels = [(0, rows)]
    if whole_sets:
        levels.append((sub_size, rows * (1 + sub_size)))
    if levels[-1][0] < ctx_size - 1:
        levels.append((ctx_size - 1, total))
    held = (full, expanded, up_weight, *pieces)
    scratch = 2 * total * (wide + 6 * (NOPE + VDIM) + 6 * rows)

    return pl.pallas_call(
        functools.partial(attend_kernel, heads, layout, levels),
        in_specs=[VMEM] * (4 + len(pieces)) + [SMEM],
        out_specs=VMEM,
        out_shape=jax.ShapeDtypeStruct((rows, heads * VDIM), bf16),
        scratch_shapes=[
            pltpu.VMEM((total, wide), bf16),
            pltpu.VMEM((3, total, 2 * (NOPE + VDIM)), bf16),
            pltpu.VMEM((2, rows, total), jnp.float32),
            pltpu.VMEM((2, rows, total), bf16),
        ],
        compiler_params=pltpu.CompilerParams(
            vmem_limit_bytes=6 * MIB + 2 * sum(x.size for x in held) + scratch
        ),
        name="attend",
        cost_estimate=pl.CostEstimate(
            flops=2 * total * (width + 2 * rows) * up_weight.shape[1],
            bytes_accessed=2 * (up_weight.size + 3 * rows * up_weight.shape[1]),
            transcendentals=heads * rows * total,
        ),
    )(full, payload, expanded, up_weight, *pieces, prompt_length)


def solution(mesh):
    placed = (
        P(("parts", "ctx"), ("head", "sub")),
        P(("parts", "ctx"), None),
        P(("parts", "ctx"), None),
        P(),
        P(None, ("head", "sub")),
        P("parts"),
    )
    return jax.shard_map(
        functools.partial(per_device, mesh.shape["ctx"], mesh.shape["sub"]),
        mesh=mesh,
        in_specs=placed,
        out_specs=P(("parts", "ctx"), ("head", "sub")),
        check_vma=False,
    )
```

```python
import functools
import math

import jax
import jax.numpy as jnp
import numpy as np
from jax import lax
from jax.experimental import pallas as pl
from jax.experimental.pallas import tpu as pltpu
from jax.sharding import PartitionSpec as P

ROPE = 64
NOPE = 128
VDIM = 128
WIDE = 128
FULL = 256
MASKED = -1e30
MIB = 1024 * 1024
PACK_FLOPS = 4 * 10**9
OUT_COPIES = 4
EXPONENT = math.log2(math.e) / math.sqrt(NOPE + ROPE)

VMEM = pl.BlockSpec(memory_space=pltpu.VMEM)
SMEM = pl.BlockSpec(memory_space=pltpu.SMEM)
HBM = pl.BlockSpec(memory_space=pltpu.HBM)
ANY = pl.BlockSpec(memory_space=pl.ANY)


def tables(positions):
    half = ROPE // 2
    frequency = np.float32(10000.0) ** (-np.arange(half, dtype=np.float32) / np.float32(half))
    angles = np.arange(positions, dtype=np.float32)[:, None] * frequency.astype(np.float32)
    cosines, sines = np.cos(angles), np.sin(angles)
    rows = np.concatenate([cosines, cosines, -sines, sines], 1).astype(np.float32)
    columns = np.concatenate([cosines, sines], 1).T.astype(np.float32)
    return rows, np.ascontiguousarray(columns)


def pack_kernel(
    latent_hbm, rope_hbm, gain_hbm, tables_hbm, length, payload, piece, latent, rope, gain, table, arrived
):
    rows, width = latent.shape
    half = ROPE // 2
    ctx, sub = lax.axis_index("ctx"), lax.axis_index("sub")
    copies = [
        pltpu.make_async_copy(source, target, arrived.at[k])
        for k, (source, target) in enumerate(
            [(latent_hbm, latent), (gain_hbm, gain), (rope_hbm, rope), (tables_hbm.at[ctx], table)]
        )
    ]
    for copy in copies:
        copy.start()
    for copy in copies:
        copy.wait()
    wide = latent[...].astype(jnp.float32)
    mean = jnp.mean(wide * wide, -1, keepdims=True)
    normed = (wide * lax.rsqrt(mean + 1e-06) * gain[...]).astype(jnp.bfloat16)
    keys = rope[...].astype(jnp.float32)
    low, high = keys[:half], keys[half:]
    cosines, sines = table[:half], table[half:]
    rotated = jnp.concatenate([low * cosines - high * sines, low * sines + high * cosines], 0)
    position = ctx * rows + lax.broadcasted_iota(jnp.int32, (WIDE - ROPE, rows), 1)
    first = lax.broadcasted_iota(jnp.int32, (WIDE - ROPE, rows), 0) == 0
    bias = jnp.where(first & (position >= length[0]), MASKED, 0.0)
    extra = jnp.concatenate([rotated, bias], 0).T.astype(jnp.bfloat16)
    payload[:, :width] = normed
    payload[:, width:] = extra
    size = piece.shape[0]
    for k in range(rows // size):

        @pl.when(sub == k)
        def _():
            piece[:, :width] = normed[k * size : (k + 1) * size]
            piece[:, width:] = extra[k * size : (k + 1) * size]


def own_kernel(heads, queries, payload, weight, tables_hbm, expanded, full, table, arrived):
    copy = pltpu.make_async_copy(tables_hbm.at[lax.axis_index("ctx")], table, arrived)
    copy.start()
    copy.wait()
    rows = queries.shape[0]
    width = weight.shape[0]
    cosines = jnp.concatenate([table[:, :ROPE]] * 2, 1)
    sines = jnp.concatenate([table[:, ROPE:]] * 2, 1)
    lane = lax.broadcasted_iota(jnp.int32, (rows, 2 * ROPE), 1)
    lower = lane % ROPE < ROPE // 2
    tail = (lax.broadcasted_iota(jnp.int32, (rows, FULL - NOPE - ROPE), 1) == 0).astype(
        jnp.float32
    ).astype(jnp.bfloat16)
    each = NOPE + ROPE
    for i in range(heads // 2):
        pair = queries[:, 2 * each * i : 2 * each * (i + 1)]
        ropes = jnp.concatenate([pair[:, NOPE:each], pair[:, each + NOPE :]], 1).astype(jnp.float32)
        turned = jnp.where(
            lower, pltpu.roll(ropes, 2 * ROPE - ROPE // 2, 1), pltpu.roll(ropes, ROPE // 2, 1)
        )
        ropes = (ropes * cosines + turned * sines).astype(jnp.bfloat16)
        for e in range(2):
            at = FULL * (2 * i + e)
            full[:, at : at + NOPE] = pair[:, each * e : each * e + NOPE]
            full[:, at + NOPE : at + FULL] = jnp.concatenate(
                [ropes[:, ROPE * e : ROPE * (e + 1)], tail], 1
            )
    columns = NOPE + VDIM
    for i in range(heads // 2):
        at = slice(2 * columns * i, 2 * columns * (i + 1))
        expanded[:, at] = jnp.dot(
            payload[:, :width], weight[:, at], preferred_element_type=jnp.float32
        ).astype(jnp.bfloat16)


def attend_kernel(heads, layout, levels, full, own, expanded, weight, *rest):
    count = len(rest) - 8
    pieces, (length, out_hbm, keys, grown, scores, weights, out, sent) = rest[:count], rest[count:]
    rows = full.shape[0]
    width = weight.shape[0]
    columns = NOPE + VDIM
    ctx, sub = lax.axis_index("ctx"), lax.axis_index("sub")
    row = lax.broadcasted_iota(jnp.int32, (rows, rows), 0)
    causal = lax.broadcasted_iota(jnp.int32, (rows, rows), 1) <= row
    live = ctx * rows + lax.broadcasted_iota(jnp.int32, (rows, 1), 0) < length[0]
    stage, buffers = 2, 4
    block = VDIM * heads // OUT_COPIES

    def leave(k):
        at = pl.ds(k * block, block)
        return pltpu.make_async_copy(out.at[:, at], out_hbm.at[:, at], sent.at[k])

    def run(total):
        keys[:rows, width:] = own[:, width:]
        spare = (lax.broadcasted_iota(jnp.int32, (1, WIDE), 1) == ROPE).astype(jnp.float32)
        spare = (spare * MASKED).astype(jnp.bfloat16)
        at = rows
        for which, begin, size, masks in layout:
            if at >= total:
                break
            ref, piece = pieces[which], slice(begin, begin + size)
            keys[at : at + size, :width] = ref[piece, :width]
            holders = sum(jnp.where(sub == s, mask, 0) for s, mask in enumerate(masks))
            last = ref[piece, width:]
            keys[at : at + size, width:] = jnp.where(
                lax.shift_right_logical(holders, ctx) & 1 == 1,
                last,
                jnp.broadcast_to(spare, last.shape),
            )
            at += size

        def grow(i):
            at = slice(2 * columns * i, 2 * columns * (i + 1))
            grown[i % 4, :rows] = expanded[:, at]
            if total > rows:
                grown[i % 4, rows:total] = jnp.dot(
                    keys[rows:total, :width], weight[:, at], preferred_element_type=jnp.float32
                ).astype(jnp.bfloat16)

        def score(h):
            i, e = divmod(h, 2)
            nope = grown[i % 4, :total, columns * e : columns * e + NOPE]
            whole = jnp.concatenate([nope, keys[:total, width:]], 1)
            found = lax.dot_general(
                full[:, FULL * h : FULL * (h + 1)],
                whole,
                (((1,), (1,)), ((), ())),
                preferred_element_type=jnp.float32,
            )
            scores[h % buffers, :, :rows] = jnp.where(causal, found[:, :rows], MASKED)
            if total > rows:
                scores[h % buffers, :, rows:total] = found[:, rows:]

        def soften(h):
            found = scores[h % buffers, :, :total]
            top = jnp.max(found, 1, keepdims=True)
            raw = jnp.exp2(found * EXPONENT - top * EXPONENT)
            weights[h % buffers, :, :total] = raw.astype(jnp.bfloat16)
            return jnp.sum(raw, 1, keepdims=True)

        def mix(h, total_h):
            i, e = divmod(h, 2)
            values = grown[i % 4, :total, columns * e + NOPE : columns * (e + 1)]
            mixed = jnp.dot(
                weights[h % buffers, :, :total], values, preferred_element_type=jnp.float32
            )
            out[:, VDIM * h : VDIM * (h + 1)] = jnp.where(live, mixed / total_h, 0.0).astype(
                jnp.bfloat16
            )
            if (h + 1) % (heads // OUT_COPIES) == 0:
                leave(h // (heads // OUT_COPIES)).start()

        totals = {}
        steps = heads // stage
        grow(0)
        for t in range(steps + 2):
            if t + 1 < heads // 2:
                grow(t + 1)
            for h in range(stage * t, stage * (t + 1)):
                if t < steps:
                    score(h)
            for h in range(stage * (t - 1), stage * t):
                if 0 <= t - 1 < steps:
                    totals[h] = soften(h)
            for h in range(stage * (t - 2), stage * (t - 1)):
                if 0 <= t - 2 < steps:
                    mix(h, totals.pop(h))

    for total, places in levels:

        @pl.when(functools.reduce(jnp.logical_or, [ctx == c for c in places]))
        def _():
            run(total)

    for k in range(OUT_COPIES):
        leave(k).wait()


def plan(shards, cores):
    colours = []
    for distance in range(shards - 1, 0, -1):
        for source in range(shards - distance):
            target = source + distance
            for colour in colours:
                if all(source != i and target != j for i, j in colour):
                    colour.append((source, target))
                    break
            else:
                colours.append([(source, target)])
    whole = len(colours) // cores * cores
    sets = [colours[k : k + cores] for k in range(0, whole, cores)]
    return sets, colours[whole:]


def signed(mask):
    return mask - (1 << 32) if mask >= 1 << 31 else mask


def in_hbm(x):
    return pltpu.with_memory_space_constraint(x, pltpu.HBM)


def per_device(
    ctx_size, sub_size, queries, latent, rope_keys, latent_gain, up_weight, prompt_length
):
    rows, width = latent.shape
    heads = up_weight.shape[1] // (NOPE + VDIM)
    by_row, by_column = tables(ctx_size * rows)
    by_row = by_row.reshape(ctx_size, rows, 2 * ROPE)
    by_column = by_column.reshape(ROPE, ctx_size, rows).transpose(1, 0, 2)

    bf16 = jnp.bfloat16
    wide = width + WIDE
    payload, piece = pl.pallas_call(
        pack_kernel,
        in_specs=[HBM] * 4 + [SMEM],
        out_specs=[VMEM] * 2,
        out_shape=[
            jax.ShapeDtypeStruct((rows, wide), bf16),
            jax.ShapeDtypeStruct((rows // sub_size, wide), bf16),
        ],
        scratch_shapes=[
            pltpu.VMEM((rows, width), bf16),
            pltpu.VMEM((ROPE, rows), bf16),
            pltpu.VMEM((1, width), jnp.float32),
            pltpu.VMEM((ROPE, rows), jnp.float32),
            pltpu.SemaphoreType.DMA((4,)),
        ],
        cost_estimate=pl.CostEstimate(
            flops=PACK_FLOPS, bytes_accessed=8 * rows * width, transcendentals=0
        ),
        compiler_params=pltpu.CompilerParams(vmem_limit_bytes=4 * MIB),
        name="pack",
    )(
        in_hbm(latent),
        in_hbm(rope_keys.T),
        in_hbm(latent_gain.reshape(1, width)),
        in_hbm(jnp.asarray(by_column)),
        prompt_length,
    )

    cores = ("ctx", "sub")
    sets, rest = plan(ctx_size, sub_size)
    sends = [(payload, by_core) for by_core in sets]
    sends += [(piece, [edges] * sub_size) for edges in rest]
    direct, holders = [], []
    for data, by_core in sends:
        pairs = [
            (i * sub_size + s, j * sub_size + s) for s, edges in enumerate(by_core) for i, j in edges
        ]
        direct.append(lax.ppermute(data, cores, pairs))
        holders.append([sum(1 << j for _, j in edges) for edges in by_core])

    expanded, full = pl.pallas_call(
        functools.partial(own_kernel, heads),
        in_specs=[VMEM] * 3 + [ANY],
        out_specs=[VMEM] * 2,
        out_shape=[
            jax.ShapeDtypeStruct((rows, up_weight.shape[1]), bf16),
            jax.ShapeDtypeStruct((rows, heads * FULL), bf16),
        ],
        scratch_shapes=[pltpu.VMEM((rows, 2 * ROPE), jnp.float32), pltpu.SemaphoreType.DMA],
        compiler_params=pltpu.CompilerParams(
            vmem_limit_bytes=4 * MIB
            + 2 * (queries.size + up_weight.size + 2 * rows * up_weight.shape[1])
        ),
        name="own",
        cost_estimate=pl.CostEstimate(
            flops=2 * rows * width * up_weight.shape[1],
            bytes_accessed=2 * (queries.size + up_weight.size + 2 * rows * up_weight.shape[1]),
            transcendentals=0,
        ),
    )(queries, payload, up_weight, jnp.asarray(by_row))

    *direct, expanded, full = lax.optimization_barrier((*direct, expanded, full))
    together = jnp.concatenate(direct, 0)
    pieces = [together]
    for r in range(1, sub_size):
        pairs = [(s, (s + r) % sub_size) for s in range(sub_size)]
        pieces.append(lax.ppermute(together, "sub", pairs))
    layout, begin = [], 0
    total, need = rows, [rows] * ctx_size
    for part, masks in zip(direct, holders, strict=True):
        size = part.shape[0]
        for r in range(sub_size):
            turned = [signed(masks[(s - r) % sub_size]) for s in range(sub_size)]
            layout.append((r, begin, size, turned))
        total += size * sub_size
        begin += size
        need = [total if any(m >> c & 1 for m in masks) else n for c, n in enumerate(need)]
    if len(set(need)) > 3:
        need = [rows] + [total] * (ctx_size - 1)
    levels = [(t, [c for c in range(ctx_size) if need[c] == t]) for t in sorted(set(need))]
    held = (full, expanded, up_weight, *pieces)
    scratch = 2 * total * (wide + 8 * (NOPE + VDIM) + 12 * rows)

    return pl.pallas_call(
        functools.partial(attend_kernel, heads, layout, levels),
        in_specs=[VMEM] * (4 + len(pieces)) + [SMEM],
        out_specs=ANY,
        out_shape=jax.ShapeDtypeStruct((rows, heads * VDIM), bf16),
        scratch_shapes=[
            pltpu.VMEM((total, wide), bf16),
            pltpu.VMEM((4, total, 2 * (NOPE + VDIM)), bf16),
            pltpu.VMEM((4, rows, total), jnp.float32),
            pltpu.VMEM((4, rows, total), bf16),
            pltpu.VMEM((rows, heads * VDIM), bf16),
            pltpu.SemaphoreType.DMA((OUT_COPIES,)),
        ],
        compiler_params=pltpu.CompilerParams(
            vmem_limit_bytes=6 * MIB + 2 * sum(x.size for x in held) + scratch
        ),
        name="attend",
        cost_estimate=pl.CostEstimate(
            flops=2 * total * (width + 2 * rows) * up_weight.shape[1],
            bytes_accessed=2 * (up_weight.size + 3 * rows * up_weight.shape[1]),
            transcendentals=heads * rows * total,
        ),
    )(full, payload, expanded, up_weight, *pieces, prompt_length)


def solution(mesh):
    placed = (
        P(("parts", "ctx"), ("head", "sub")),
        P(("parts", "ctx"), None),
        P(("parts", "ctx"), None),
        P(),
        P(None, ("head", "sub")),
        P("parts"),
    )
    return jax.shard_map(
        functools.partial(per_device, mesh.shape["ctx"], mesh.shape["sub"]),
        mesh=mesh,
        in_specs=placed,
        out_specs=P(("parts", "ctx"), ("head", "sub")),
        check_vma=False,
    )
```

```python
import functools
import math

import jax
import jax.numpy as jnp
import numpy as np
from jax import lax
from jax.experimental import pallas as pl
from jax.experimental.pallas import tpu as pltpu
from jax.sharding import PartitionSpec as P

ROPE = 64
NOPE = 128
VDIM = 128
WIDE = 128
FULL = 256
MASKED = -1e30
MIB = 1024 * 1024
PACK_FLOPS = 4 * 10**9
OUT_COPIES = 4
EXPONENT = math.log2(math.e) / math.sqrt(NOPE + ROPE)

VMEM = pl.BlockSpec(memory_space=pltpu.VMEM)
SMEM = pl.BlockSpec(memory_space=pltpu.SMEM)
HBM = pl.BlockSpec(memory_space=pltpu.HBM)
ANY = pl.BlockSpec(memory_space=pl.ANY)


def tables(positions):
    half = ROPE // 2
    frequency = np.float32(10000.0) ** (-np.arange(half, dtype=np.float32) / np.float32(half))
    angles = np.arange(positions, dtype=np.float32)[:, None] * frequency.astype(np.float32)
    cosines, sines = np.cos(angles), np.sin(angles)
    rows = np.concatenate([cosines, cosines, -sines, sines], 1).astype(np.float32)
    columns = np.concatenate([cosines, sines], 1).T.astype(np.float32)
    return rows, np.ascontiguousarray(columns)


def normalise(latent, gain):
    wide = latent.astype(jnp.float32)
    mean = jnp.mean(wide * wide, -1, keepdims=True)
    return (wide * lax.rsqrt(mean + 1e-06) * gain).astype(jnp.bfloat16)


def last_tile(rope, table, start, live):
    half = ROPE // 2
    keys = rope.astype(jnp.float32)
    low, high = keys[:half], keys[half:]
    cosines, sines = table[:half], table[half:]
    rotated = jnp.concatenate([low * cosines - high * sines, low * sines + high * cosines], 0)
    shape = (WIDE - ROPE, rope.shape[1])
    position = start + lax.broadcasted_iota(jnp.int32, shape, 1)
    first = lax.broadcasted_iota(jnp.int32, shape, 0) == 0
    bias = jnp.where(first & (position >= live), MASKED, 0.0)
    return jnp.concatenate([rotated, bias], 0).T.astype(jnp.bfloat16)


def spare_tile(rows):
    lane = lax.broadcasted_iota(jnp.int32, (rows, WIDE), 1)
    return jnp.where(lane == ROPE, MASKED, 0.0).astype(jnp.bfloat16)


def pack_kernel(
    latent_hbm, rope_hbm, gain_hbm, tables_hbm, length, payload, piece, latent, rope, gain, table, arrived
):
    rows, width = latent.shape
    ctx, sub = lax.axis_index("ctx"), lax.axis_index("sub")
    copies = [
        pltpu.make_async_copy(source, target, arrived.at[k])
        for k, (source, target) in enumerate(
            [(latent_hbm, latent), (gain_hbm, gain), (rope_hbm, rope), (tables_hbm.at[ctx], table)]
        )
    ]
    for copy in copies:
        copy.start()
    for copy in copies:
        copy.wait()
    normed = normalise(latent[...], gain[...])
    extra = last_tile(rope[...], table[...], ctx * rows, length[0])
    payload[:, :width] = normed
    payload[:, width:] = extra
    size = piece.shape[0]
    for k in range(rows // size):

        @pl.when(sub == k)
        def _():
            piece[:, :width] = normed[k * size : (k + 1) * size]
            piece[:, width:] = extra[k * size : (k + 1) * size]


def pick(sub, values):
    return sum(jnp.where(sub == s, value, 0) for s, value in enumerate(values))


def holds(sub, ctx, masks):
    return lax.shift_right_logical(pick(sub, masks), ctx) & 1 == 1


def mid_kernel(sources, masks, piece_masks, gain, tables, length, *rest):
    count = len(sources)
    latents, ropes, pieces = rest[:count], rest[count : 2 * count], rest[2 * count : -1]
    together = rest[-1]
    ctx, sub = lax.axis_index("ctx"), lax.axis_index("sub")
    at = 0
    for latent, rope, source, mask in zip(latents, ropes, sources, masks, strict=True):
        rows, width = latent.shape
        origin = sum(
            jnp.where((sub == s) & (ctx == j), i, 0)
            for s, edges in enumerate(source)
            for i, j in edges
        )
        together[at : at + rows, :width] = normalise(latent[...], gain[...])
        tile = last_tile(rope[...], tables[origin], origin * rows, length[0])
        together[at : at + rows, width:] = jnp.where(holds(sub, ctx, mask), tile, spare_tile(rows))
        at += rows
    for piece, mask in zip(pieces, piece_masks, strict=True):
        size, width = piece.shape[0], piece.shape[1] - WIDE
        together[at : at + size, :width] = piece[:, :width]
        together[at : at + size, width:] = jnp.where(
            holds(sub, ctx, mask), piece[:, width:], spare_tile(size)
        )
        at += size


def grow_kernel(step, together, weight, grown):
    width = weight.shape[0]

    @pl.when(lax.axis_index("ctx") > 0)
    def _():
        for k in range(weight.shape[1] // step):
            at = slice(k * step, (k + 1) * step)
            grown[:, at] = jnp.dot(
                together[:, :width], weight[:, at], preferred_element_type=jnp.float32
            ).astype(jnp.bfloat16)


def own_kernel(heads, queries, payload, weight, tables_hbm, expanded, full, table, arrived):
    copy = pltpu.make_async_copy(tables_hbm.at[lax.axis_index("ctx")], table, arrived)
    copy.start()
    copy.wait()
    rows = queries.shape[0]
    width = weight.shape[0]
    cosines = jnp.concatenate([table[:, :ROPE]] * 2, 1)
    sines = jnp.concatenate([table[:, ROPE:]] * 2, 1)
    lane = lax.broadcasted_iota(jnp.int32, (rows, 2 * ROPE), 1)
    lower = lane % ROPE < ROPE // 2
    tail = (lax.broadcasted_iota(jnp.int32, (rows, FULL - NOPE - ROPE), 1) == 0).astype(
        jnp.float32
    ).astype(jnp.bfloat16)
    each = NOPE + ROPE
    for i in range(heads // 2):
        pair = queries[:, 2 * each * i : 2 * each * (i + 1)]
        ropes = jnp.concatenate([pair[:, NOPE:each], pair[:, each + NOPE :]], 1).astype(jnp.float32)
        turned = jnp.where(
            lower, pltpu.roll(ropes, 2 * ROPE - ROPE // 2, 1), pltpu.roll(ropes, ROPE // 2, 1)
        )
        ropes = (ropes * cosines + turned * sines).astype(jnp.bfloat16)
        for e in range(2):
            at = FULL * (2 * i + e)
            full[:, at : at + NOPE] = pair[:, each * e : each * e + NOPE]
            full[:, at + NOPE : at + FULL] = jnp.concatenate(
                [ropes[:, ROPE * e : ROPE * (e + 1)], tail], 1
            )
    columns = NOPE + VDIM
    for i in range(heads // 2):
        at = slice(2 * columns * i, 2 * columns * (i + 1))
        expanded[:, at] = jnp.dot(
            payload[:, :width], weight[:, at], preferred_element_type=jnp.float32
        ).astype(jnp.bfloat16)


def attend_kernel(heads, sets, levels, full, own, expanded, weight, together, fetched, *rest):
    swapped = rest[:-7]
    length, out_hbm, grown, scores, weights, out, sent = rest[-7:]
    rows = full.shape[0]
    width = weight.shape[0]
    columns = NOPE + VDIM
    ctx = lax.axis_index("ctx")
    row = lax.broadcasted_iota(jnp.int32, (rows, rows), 0)
    causal = lax.broadcasted_iota(jnp.int32, (rows, rows), 1) <= row
    live = ctx * rows + lax.broadcasted_iota(jnp.int32, (rows, 1), 0) < length[0]
    stage, buffers = 2, 4
    block = VDIM * heads // OUT_COPIES

    def leave(k):
        at = pl.ds(k * block, block)
        return pltpu.make_async_copy(out.at[:, at], out_hbm.at[:, at], sent.at[k])

    def run(level):
        every = together.shape[0]
        part = (0, sets, every)[level]
        total = rows + part * (1 + len(swapped))

        def rows_of(own_part, direct_part, swapped_part):
            found = [own_part()]
            for begin, end in ((0, sets), (sets, every)):
                if begin < end <= part:
                    found.append(direct_part(slice(begin, end)))
                    for r in range(len(swapped)):
                        found.append(swapped_part(r, slice(begin, end)))
            return found[0] if len(found) == 1 else jnp.concatenate(found, 0)

        def grow(i):
            at = slice(2 * columns * i, 2 * columns * (i + 1))
            for r, ref in enumerate(swapped):
                if part:
                    grown[i % 4, r, :part] = jnp.dot(
                        ref[:part, :width], weight[:, at], preferred_element_type=jnp.float32
                    ).astype(jnp.bfloat16)

        def column(h, begin, end):
            i, e = divmod(h, 2)
            return rows_of(
                lambda: expanded[:, columns * h + begin : columns * h + end],
                lambda piece: fetched[piece, columns * h + begin : columns * h + end],
                lambda r, piece: grown[i % 4, r, piece, columns * e + begin : columns * e + end],
            )

        def score(h):
            last = rows_of(
                lambda: own[:, width:],
                lambda piece: together[piece, width:],
                lambda r, piece: swapped[r][piece, width:],
            )
            found = lax.dot_general(
                full[:, FULL * h : FULL * (h + 1)],
                jnp.concatenate([column(h, 0, NOPE), last], 1),
                (((1,), (1,)), ((), ())),
                preferred_element_type=jnp.float32,
            )
            scores[h % buffers, :, :rows] = jnp.where(causal, found[:, :rows], MASKED)
            if total > rows:
                scores[h % buffers, :, rows:total] = found[:, rows:]

        def soften(h):
            found = scores[h % buffers, :, :total]
            top = jnp.max(found, 1, keepdims=True)
            raw = jnp.exp2(found * EXPONENT - top * EXPONENT)
            weights[h % buffers, :, :total] = raw.astype(jnp.bfloat16)
            return jnp.sum(raw, 1, keepdims=True)

        def mix(h, total_h):
            mixed = jnp.dot(
                weights[h % buffers, :, :total],
                column(h, NOPE, columns),
                preferred_element_type=jnp.float32,
            )
            out[:, VDIM * h : VDIM * (h + 1)] = jnp.where(live, mixed / total_h, 0.0).astype(
                jnp.bfloat16
            )
            if (h + 1) % (heads // OUT_COPIES) == 0:
                leave(h // (heads // OUT_COPIES)).start()

        totals = {}
        steps = heads // stage
        grow(0)
        for t in range(steps + 2):
            if t + 1 < heads // 2:
                grow(t + 1)
            for h in range(stage * t, stage * (t + 1)):
                if t < steps:
                    score(h)
            for h in range(stage * (t - 1), stage * t):
                if 0 <= t - 1 < steps:
                    totals[h] = soften(h)
            for h in range(stage * (t - 2), stage * (t - 1)):
                if 0 <= t - 2 < steps:
                    mix(h, totals.pop(h))

    for level, places in levels:

        @pl.when(functools.reduce(jnp.logical_or, [ctx == c for c in places]))
        def _():
            run(level)

    for k in range(OUT_COPIES):
        leave(k).wait()


def plan(shards, cores):
    colours = []
    for distance in range(shards - 1, 0, -1):
        for source in range(shards - distance):
            target = source + distance
            for colour in colours:
                if all(source != i and target != j for i, j in colour):
                    colour.append((source, target))
                    break
            else:
                colours.append([(source, target)])
    whole = len(colours) // cores * cores
    sets = [colours[k : k + cores] for k in range(0, whole, cores)]
    return sets, colours[whole:]


def signed(mask):
    return mask - (1 << 32) if mask >= 1 << 31 else mask


def in_hbm(x):
    return pltpu.with_memory_space_constraint(x, pltpu.HBM)


def grant(*arrays):
    return pltpu.CompilerParams(vmem_limit_bytes=4 * MIB + 2 * sum(x.size for x in arrays))


def per_device(
    ctx_size, sub_size, queries, latent, rope_keys, latent_gain, up_weight, prompt_length
):
    rows, width = latent.shape
    heads = up_weight.shape[1] // (NOPE + VDIM)
    by_row, by_column = tables(ctx_size * rows)
    by_row = jnp.asarray(by_row.reshape(ctx_size, rows, 2 * ROPE))
    by_column = jnp.asarray(by_column.reshape(ROPE, ctx_size, rows).transpose(1, 0, 2))
    gain = latent_gain.reshape(1, width)
    turned = rope_keys.T
    bf16 = jnp.bfloat16
    wide = width + WIDE

    cores = ("ctx", "sub")
    sets, rest = plan(ctx_size, sub_size)

    def send(data, by_core):
        pairs = [
            (i * sub_size + s, j * sub_size + s) for s, edges in enumerate(by_core) for i, j in edges
        ]
        return lax.ppermute(data, cores, pairs)

    def receivers(by_core):
        return [signed(sum(1 << j for _, j in edges)) for edges in by_core]

    latents = [send(latent, by_core) for by_core in sets]
    ropes = [send(turned, by_core) for by_core in sets]

    payload, piece = pl.pallas_call(
        pack_kernel,
        in_specs=[HBM] * 4 + [SMEM],
        out_specs=[VMEM] * 2,
        out_shape=[
            jax.ShapeDtypeStruct((rows, wide), bf16),
            jax.ShapeDtypeStruct((rows // sub_size, wide), bf16),
        ],
        scratch_shapes=[
            pltpu.VMEM((rows, width), bf16),
            pltpu.VMEM((ROPE, rows), bf16),
            pltpu.VMEM((1, width), jnp.float32),
            pltpu.VMEM((ROPE, rows), jnp.float32),
            pltpu.SemaphoreType.DMA((4,)),
        ],
        cost_estimate=pl.CostEstimate(
            flops=PACK_FLOPS, bytes_accessed=8 * rows * width, transcendentals=0
        ),
        compiler_params=grant(),
        name="pack",
    )(in_hbm(latent), in_hbm(turned), in_hbm(gain), in_hbm(by_column), prompt_length)

    pieces = [send(piece, [edges] * sub_size) for edges in rest]

    expanded, full = pl.pallas_call(
        functools.partial(own_kernel, heads),
        in_specs=[VMEM] * 3 + [ANY],
        out_specs=[VMEM] * 2,
        out_shape=[
            jax.ShapeDtypeStruct((rows, up_weight.shape[1]), bf16),
            jax.ShapeDtypeStruct((rows, heads * FULL), bf16),
        ],
        scratch_shapes=[pltpu.VMEM((rows, 2 * ROPE), jnp.float32), pltpu.SemaphoreType.DMA],
        compiler_params=grant(queries, up_weight, payload, up_weight[:rows], up_weight[:rows]),
        name="own",
        cost_estimate=pl.CostEstimate(
            flops=2 * rows * width * up_weight.shape[1],
            bytes_accessed=2 * (queries.size + up_weight.size + 2 * rows * up_weight.shape[1]),
            transcendentals=0,
        ),
    )(queries, payload, up_weight, by_row)

    latents, ropes, pieces, expanded, full = lax.optimization_barrier(
        (latents, ropes, pieces, expanded, full)
    )
    reach = sum(x.shape[0] for x in (*latents, *pieces))
    whole = sum(x.shape[0] for x in latents)
    together = pl.pallas_call(
        functools.partial(
            mid_kernel,
            sets,
            [receivers(by_core) for by_core in sets],
            [receivers([edges] * sub_size) for edges in rest],
        ),
        in_specs=[VMEM] * 2 + [SMEM] + [VMEM] * (2 * len(latents) + len(pieces)),
        out_specs=VMEM,
        out_shape=jax.ShapeDtypeStruct((reach, wide), bf16),
        compiler_params=grant(by_column, by_column, *latents, *ropes, *pieces, *pieces, *latents),
        name="mid",
    )(gain, by_column, prompt_length, *latents, *ropes, *pieces)

    swapped = []
    for r in range(1, sub_size):
        pairs = [(s, (s + r) % sub_size) for s in range(sub_size)]
        swapped.append(lax.ppermute(together, "sub", pairs))

    fetched = pl.pallas_call(
        functools.partial(grow_kernel, 4 * (NOPE + VDIM)),
        in_specs=[VMEM] * 2,
        out_specs=VMEM,
        out_shape=jax.ShapeDtypeStruct((reach, up_weight.shape[1]), bf16),
        compiler_params=pltpu.CompilerParams(
            vmem_limit_bytes=4 * MIB
            + 2 * (up_weight.size + reach * (wide + up_weight.shape[1]))
        ),
        name="grow",
        cost_estimate=pl.CostEstimate(
            flops=2 * reach * width * up_weight.shape[1],
            bytes_accessed=2 * (up_weight.size + reach * up_weight.shape[1]),
            transcendentals=0,
        ),
    )(together, up_weight)

    needs = [0] * ctx_size
    for level, groups in ((1, [e for by_core in sets for e in by_core]), (2, rest)):
        for edges in groups:
            for _, j in edges:
                needs[j] = level
    levels = [(k, [c for c in range(ctx_size) if needs[c] == k]) for k in sorted(set(needs))]
    total = rows + sub_size * reach
    held = 2 * (up_weight.size + (reach + 2 * rows) * up_weight.shape[1] + total * wide)
    scratch = 8 * total * (NOPE + VDIM) * 2 + 24 * rows * total + 2 * rows * heads * VDIM
    return pl.pallas_call(
        functools.partial(attend_kernel, heads, whole, levels),
        in_specs=[VMEM] * (6 + len(swapped)) + [SMEM],
        out_specs=ANY,
        out_shape=jax.ShapeDtypeStruct((rows, heads * VDIM), bf16),
        scratch_shapes=[
            pltpu.VMEM((4, len(swapped), reach, 2 * (NOPE + VDIM)), bf16),
            pltpu.VMEM((4, rows, total), jnp.float32),
            pltpu.VMEM((4, rows, total), bf16),
            pltpu.VMEM((rows, heads * VDIM), bf16),
            pltpu.SemaphoreType.DMA((OUT_COPIES,)),
        ],
        compiler_params=pltpu.CompilerParams(vmem_limit_bytes=6 * MIB + held + scratch),
        name="attend",
        cost_estimate=pl.CostEstimate(
            flops=2 * total * (width + 2 * rows) * up_weight.shape[1],
            bytes_accessed=2 * (up_weight.size + 3 * rows * up_weight.shape[1]),
            transcendentals=heads * rows * total,
        ),
    )(full, payload, expanded, up_weight, together, fetched, *swapped, prompt_length)


def solution(mesh):
    placed = (
        P(("parts", "ctx"), ("head", "sub")),
        P(("parts", "ctx"), None),
        P(("parts", "ctx"), None),
        P(),
        P(None, ("head", "sub")),
        P("parts"),
    )
    return jax.shard_map(
        functools.partial(per_device, mesh.shape["ctx"], mesh.shape["sub"]),
        mesh=mesh,
        in_specs=placed,
        out_specs=P(("parts", "ctx"), ("head", "sub")),
        check_vma=False,
    )
```

```python
import functools
import math

import jax
import jax.numpy as jnp
import numpy as np
from jax import lax
from jax.experimental import pallas as pl
from jax.experimental.pallas import tpu as pltpu
from jax.sharding import PartitionSpec as P

ROPE = 64
NOPE = 128
VDIM = 128
WIDE = 128
FULL = 256
MASKED = -1e30
MIB = 1024 * 1024
PACK_FLOPS = 4 * 10**9
OUT_COPIES = 4
EXPONENT = math.log2(math.e) / math.sqrt(NOPE + ROPE)

VMEM = pl.BlockSpec(memory_space=pltpu.VMEM)
SMEM = pl.BlockSpec(memory_space=pltpu.SMEM)
HBM = pl.BlockSpec(memory_space=pltpu.HBM)
ANY = pl.BlockSpec(memory_space=pl.ANY)


def tables(positions):
    half = ROPE // 2
    frequency = np.float32(10000.0) ** (-np.arange(half, dtype=np.float32) / np.float32(half))
    angles = np.arange(positions, dtype=np.float32)[:, None] * frequency.astype(np.float32)
    cosines, sines = np.cos(angles), np.sin(angles)
    rows = np.concatenate([cosines, cosines, -sines, sines], 1).astype(np.float32)
    columns = np.concatenate([cosines, sines], 1).T.astype(np.float32)
    return rows, np.ascontiguousarray(columns)


def normalise(latent, gain):
    wide = latent.astype(jnp.float32)
    mean = jnp.mean(wide * wide, -1, keepdims=True)
    return (wide * lax.rsqrt(mean + 1e-06) * gain).astype(jnp.bfloat16)


def last_tile(rope, table):
    half = ROPE // 2
    keys = rope.astype(jnp.float32)
    low, high = keys[:half], keys[half:]
    cosines, sines = table[:half], table[half:]
    zeros = jnp.zeros((WIDE - ROPE, rope.shape[1]), jnp.float32)
    rotated = [low * cosines - high * sines, low * sines + high * cosines, zeros]
    return jnp.concatenate(rotated, 0).T.astype(jnp.bfloat16)


def masked_tile(tile, allowed):
    lane = lax.broadcasted_iota(jnp.int32, tile.shape, 1)
    token = lax.broadcasted_iota(jnp.int32, tile.shape, 0)
    bias = jnp.where((lane == ROPE) & ~allowed(token), MASKED, 0.0)
    return tile + bias.astype(jnp.bfloat16)


def pack_kernel(
    latent_hbm,
    rope_hbm,
    gain_hbm,
    tables_hbm,
    payload,
    piece,
    latent,
    rope,
    gain,
    table,
    arrived,
):
    rows, width = latent.shape
    ctx, sub = lax.axis_index("ctx"), lax.axis_index("sub")
    copies = [
        pltpu.make_async_copy(source, target, arrived.at[k])
        for k, (source, target) in enumerate(
            [
                (latent_hbm, latent),
                (gain_hbm, gain),
                (rope_hbm, rope),
                (tables_hbm.at[ctx], table),
            ]
        )
    ]
    for copy in copies:
        copy.start()
    for copy in copies:
        copy.wait()
    normed = normalise(latent[...], gain[...])
    extra = last_tile(rope[...], table[...])
    payload[:, :width] = normed
    payload[:, width:] = extra
    size = piece.shape[0]
    for k in range(rows // size):

        @pl.when(sub == k)
        def _():
            piece[:, :width] = normed[k * size : (k + 1) * size]
            piece[:, width:] = extra[k * size : (k + 1) * size]


def mid_kernel(sources, piece_sources, gain, tables, length, *rest):
    count = len(sources)
    latents, ropes, pieces = rest[:count], rest[count : 2 * count], rest[2 * count : -1]
    together = rest[-1]
    ctx, sub = lax.axis_index("ctx"), lax.axis_index("sub")

    def origin(source):
        picked = [
            jnp.where((sub == s) & (ctx == j), i + 1, 0)
            for s, edges in enumerate(source)
            for i, j in edges
        ]
        return sum(picked) - 1

    def allowed(start, there):
        return lambda token: (start + token < length[0]) & there

    at = 0
    for latent, rope, source in zip(latents, ropes, sources, strict=True):
        rows, width = latent.shape
        shard = origin(source)
        start = jnp.maximum(shard, 0)
        together[at : at + rows, :width] = normalise(latent[...], gain[...])
        together[at : at + rows, width:] = masked_tile(
            last_tile(rope[...], tables[start]), allowed(start * rows, shard >= 0)
        )
        at += rows
    for piece, edges in zip(pieces, piece_sources, strict=True):
        size, width = piece.shape[0], piece.shape[1] - WIDE
        cores = lax.axis_size("sub")
        shard = origin([edges] * cores)
        together[at : at + size, :width] = piece[:, :width]
        together[at : at + size, width:] = masked_tile(
            piece[:, width:], allowed((shard * cores + sub) * size, shard >= 0)
        )
        at += size


def grow_kernel(step, together, weight, grown):
    width = weight.shape[0]

    @pl.when(lax.axis_index("ctx") > 0)
    def _():
        for k in range(weight.shape[1] // step):
            at = slice(k * step, (k + 1) * step)
            grown[:, at] = jnp.dot(
                together[:, :width], weight[:, at], preferred_element_type=jnp.float32
            ).astype(jnp.bfloat16)


def own_kernel(heads, queries, payload, weight, tables_hbm, expanded, full, table, arrived):
    copy = pltpu.make_async_copy(tables_hbm.at[lax.axis_index("ctx")], table, arrived)
    copy.start()
    copy.wait()
    rows = queries.shape[0]
    width = weight.shape[0]
    cosines = jnp.concatenate([table[:, :ROPE]] * 2, 1)
    sines = jnp.concatenate([table[:, ROPE:]] * 2, 1)
    lane = lax.broadcasted_iota(jnp.int32, (rows, 2 * ROPE), 1)
    lower = lane % ROPE < ROPE // 2
    tail = (lax.broadcasted_iota(jnp.int32, (rows, FULL - NOPE - ROPE), 1) == 0).astype(
        jnp.float32
    ).astype(jnp.bfloat16)
    each = NOPE + ROPE
    for i in range(heads // 2):
        pair = queries[:, 2 * each * i : 2 * each * (i + 1)]
        ropes = jnp.concatenate([pair[:, NOPE:each], pair[:, each + NOPE :]], 1).astype(jnp.float32)
        turned = jnp.where(
            lower, pltpu.roll(ropes, 2 * ROPE - ROPE // 2, 1), pltpu.roll(ropes, ROPE // 2, 1)
        )
        ropes = (ropes * cosines + turned * sines).astype(jnp.bfloat16)
        for e in range(2):
            at = FULL * (2 * i + e)
            full[:, at : at + NOPE] = pair[:, each * e : each * e + NOPE]
            full[:, at + NOPE : at + FULL] = jnp.concatenate(
                [ropes[:, ROPE * e : ROPE * (e + 1)], tail], 1
            )
    columns = NOPE + VDIM
    for i in range(heads // 2):
        at = slice(2 * columns * i, 2 * columns * (i + 1))
        expanded[:, at] = jnp.dot(
            payload[:, :width], weight[:, at], preferred_element_type=jnp.float32
        ).astype(jnp.bfloat16)


def attend_kernel(heads, sets, levels, full, own, expanded, weight, together, fetched, *rest):
    swapped = rest[:-8]
    length, out_hbm, last_own, grown, scores, weights, out, sent = rest[-8:]
    rows = full.shape[0]
    width = weight.shape[0]
    columns = NOPE + VDIM
    ctx = lax.axis_index("ctx")
    row = lax.broadcasted_iota(jnp.int32, (rows, rows), 0)
    causal = lax.broadcasted_iota(jnp.int32, (rows, rows), 1) <= row
    live = ctx * rows + lax.broadcasted_iota(jnp.int32, (rows, 1), 0) < length[0]
    last_own[...] = masked_tile(own[:, width:], lambda token: ctx * rows + token < length[0])
    stage, buffers = 2, 4
    block = VDIM * heads // OUT_COPIES

    def leave(k):
        at = pl.ds(k * block, block)
        return pltpu.make_async_copy(out.at[:, at], out_hbm.at[:, at], sent.at[k])

    def run(level):
        every = together.shape[0]
        part = (0, sets, every)[level]
        total = rows + part * (1 + len(swapped))

        def rows_of(own_part, direct_part, swapped_part):
            found = [own_part()]
            for begin, end in ((0, sets), (sets, every)):
                if begin < end <= part:
                    found.append(direct_part(slice(begin, end)))
                    for r in range(len(swapped)):
                        found.append(swapped_part(r, slice(begin, end)))
            return found[0] if len(found) == 1 else jnp.concatenate(found, 0)

        def grow(i):
            at = slice(2 * columns * i, 2 * columns * (i + 1))
            for r, ref in enumerate(swapped):
                if part:
                    grown[i % 4, r, :part] = jnp.dot(
                        ref[:part, :width], weight[:, at], preferred_element_type=jnp.float32
                    ).astype(jnp.bfloat16)

        def column(h, begin, end):
            i, e = divmod(h, 2)
            return rows_of(
                lambda: expanded[:, columns * h + begin : columns * h + end],
                lambda piece: fetched[piece, columns * h + begin : columns * h + end],
                lambda r, piece: grown[i % 4, r, piece, columns * e + begin : columns * e + end],
            )

        def score(h):
            last = rows_of(
                lambda: last_own[...],
                lambda piece: together[piece, width:],
                lambda r, piece: swapped[r][piece, width:],
            )
            found = lax.dot_general(
                full[:, FULL * h : FULL * (h + 1)],
                jnp.concatenate([column(h, 0, NOPE), last], 1),
                (((1,), (1,)), ((), ())),
                preferred_element_type=jnp.float32,
            )
            scores[h % buffers, :, :rows] = jnp.where(causal, found[:, :rows], MASKED)
            if total > rows:
                scores[h % buffers, :, rows:total] = found[:, rows:]

        def soften(h):
            found = scores[h % buffers, :, :total]
            top = jnp.max(found, 1, keepdims=True)
            raw = jnp.exp2(found * EXPONENT - top * EXPONENT)
            weights[h % buffers, :, :total] = raw.astype(jnp.bfloat16)
            return jnp.sum(raw, 1, keepdims=True)

        def mix(h, total_h):
            mixed = jnp.dot(
                weights[h % buffers, :, :total],
                column(h, NOPE, columns),
                preferred_element_type=jnp.float32,
            )
            out[:, VDIM * h : VDIM * (h + 1)] = jnp.where(live, mixed / total_h, 0.0).astype(
                jnp.bfloat16
            )
            if (h + 1) % (heads // OUT_COPIES) == 0:
                leave(h // (heads // OUT_COPIES)).start()

        totals = {}
        steps = heads // stage
        grow(0)
        for t in range(steps + 2):
            if t + 1 < heads // 2:
                grow(t + 1)
            for h in range(stage * t, stage * (t + 1)):
                if t < steps:
                    score(h)
            for h in range(stage * (t - 1), stage * t):
                if 0 <= t - 1 < steps:
                    totals[h] = soften(h)
            for h in range(stage * (t - 2), stage * (t - 1)):
                if 0 <= t - 2 < steps:
                    mix(h, totals.pop(h))

    for level, places in levels:

        @pl.when(functools.reduce(jnp.logical_or, [ctx == c for c in places]))
        def _():
            run(level)

    for k in range(OUT_COPIES):
        leave(k).wait()


def plan(shards, cores):
    colours = []
    for distance in range(shards - 1, 0, -1):
        for source in range(shards - distance):
            target = source + distance
            for colour in colours:
                if all(source != i and target != j for i, j in colour):
                    colour.append((source, target))
                    break
            else:
                colours.append([(source, target)])
    whole = len(colours) // cores * cores
    sets = [colours[k : k + cores] for k in range(0, whole, cores)]
    return sets, colours[whole:]


def in_hbm(x):
    return pltpu.with_memory_space_constraint(x, pltpu.HBM)


def grant(*arrays):
    return pltpu.CompilerParams(vmem_limit_bytes=4 * MIB + 2 * sum(x.size for x in arrays))


def per_device(
    ctx_size, sub_size, queries, latent, rope_keys, latent_gain, up_weight, prompt_length
):
    rows, width = latent.shape
    heads = up_weight.shape[1] // (NOPE + VDIM)
    by_row, by_column = tables(ctx_size * rows)
    by_row = jnp.asarray(by_row.reshape(ctx_size, rows, 2 * ROPE))
    by_column = jnp.asarray(by_column.reshape(ROPE, ctx_size, rows).transpose(1, 0, 2))
    gain = latent_gain.reshape(1, width)
    turned = rope_keys.T
    bf16 = jnp.bfloat16
    wide = width + WIDE

    cores = ("ctx", "sub")
    sets, rest = plan(ctx_size, sub_size)

    def send(data, by_core):
        pairs = [
            (i * sub_size + s, j * sub_size + s) for s, edges in enumerate(by_core) for i, j in edges
        ]
        return lax.ppermute(data, cores, pairs)

    latents = [send(latent, by_core) for by_core in sets]
    ropes = [send(turned, by_core) for by_core in sets]

    payload, piece = pl.pallas_call(
        pack_kernel,
        in_specs=[HBM] * 4,
        out_specs=[VMEM] * 2,
        out_shape=[
            jax.ShapeDtypeStruct((rows, wide), bf16),
            jax.ShapeDtypeStruct((rows // sub_size, wide), bf16),
        ],
        scratch_shapes=[
            pltpu.VMEM((rows, width), bf16),
            pltpu.VMEM((ROPE, rows), bf16),
            pltpu.VMEM((1, width), jnp.float32),
            pltpu.VMEM((ROPE, rows), jnp.float32),
            pltpu.SemaphoreType.DMA((4,)),
        ],
        cost_estimate=pl.CostEstimate(
            flops=PACK_FLOPS, bytes_accessed=8 * rows * width, transcendentals=0
        ),
        compiler_params=grant(),
        name="pack",
    )(in_hbm(latent), in_hbm(turned), in_hbm(gain), in_hbm(by_column))

    pieces = [send(piece, [edges] * sub_size) for edges in rest]

    expanded, full = pl.pallas_call(
        functools.partial(own_kernel, heads),
        in_specs=[VMEM] * 3 + [ANY],
        out_specs=[VMEM] * 2,
        out_shape=[
            jax.ShapeDtypeStruct((rows, up_weight.shape[1]), bf16),
            jax.ShapeDtypeStruct((rows, heads * FULL), bf16),
        ],
        scratch_shapes=[pltpu.VMEM((rows, 2 * ROPE), jnp.float32), pltpu.SemaphoreType.DMA],
        compiler_params=grant(queries, up_weight, payload, up_weight[:rows], up_weight[:rows]),
        name="own",
        cost_estimate=pl.CostEstimate(
            flops=2 * rows * width * up_weight.shape[1],
            bytes_accessed=2 * (queries.size + up_weight.size + 2 * rows * up_weight.shape[1]),
            transcendentals=0,
        ),
    )(queries, payload, up_weight, by_row)

    expanded, prompt_length = lax.optimization_barrier((expanded, prompt_length))
    latents, ropes, pieces, expanded, full = lax.optimization_barrier(
        (latents, ropes, pieces, expanded, full)
    )
    reach = sum(x.shape[0] for x in (*latents, *pieces))
    whole = sum(x.shape[0] for x in latents)
    together = pl.pallas_call(
        functools.partial(mid_kernel, sets, rest),
        in_specs=[VMEM] * 2 + [SMEM] + [VMEM] * (2 * len(latents) + len(pieces)),
        out_specs=VMEM,
        out_shape=jax.ShapeDtypeStruct((reach, wide), bf16),
        compiler_params=grant(by_column, by_column, *latents, *ropes, *pieces, *pieces, *latents),
        name="mid",
    )(gain, by_column, prompt_length, *latents, *ropes, *pieces)

    swapped = []
    for r in range(1, sub_size):
        pairs = [(s, (s + r) % sub_size) for s in range(sub_size)]
        swapped.append(lax.ppermute(together, "sub", pairs))

    fetched = pl.pallas_call(
        functools.partial(grow_kernel, 4 * (NOPE + VDIM)),
        in_specs=[VMEM] * 2,
        out_specs=VMEM,
        out_shape=jax.ShapeDtypeStruct((reach, up_weight.shape[1]), bf16),
        compiler_params=pltpu.CompilerParams(
            vmem_limit_bytes=4 * MIB
            + 2 * (up_weight.size + reach * (wide + up_weight.shape[1]))
        ),
        name="grow",
        cost_estimate=pl.CostEstimate(
            flops=2 * reach * width * up_weight.shape[1],
            bytes_accessed=2 * (up_weight.size + reach * up_weight.shape[1]),
            transcendentals=0,
        ),
    )(together, up_weight)

    needs = [0] * ctx_size
    for level, groups in ((1, [e for by_core in sets for e in by_core]), (2, rest)):
        for edges in groups:
            for _, j in edges:
                needs[j] = level
    levels = [(k, [c for c in range(ctx_size) if needs[c] == k]) for k in sorted(set(needs))]
    total = rows + sub_size * reach
    held = 2 * (up_weight.size + (reach + 2 * rows) * up_weight.shape[1] + total * wide)
    scratch = 8 * total * (NOPE + VDIM) * 2 + 24 * rows * total + 2 * rows * heads * VDIM
    return pl.pallas_call(
        functools.partial(attend_kernel, heads, whole, levels),
        in_specs=[VMEM] * (6 + len(swapped)) + [SMEM],
        out_specs=ANY,
        out_shape=jax.ShapeDtypeStruct((rows, heads * VDIM), bf16),
        scratch_shapes=[
            pltpu.VMEM((rows, WIDE), bf16),
            pltpu.VMEM((4, len(swapped), reach, 2 * (NOPE + VDIM)), bf16),
            pltpu.VMEM((4, rows, total), jnp.float32),
            pltpu.VMEM((4, rows, total), bf16),
            pltpu.VMEM((rows, heads * VDIM), bf16),
            pltpu.SemaphoreType.DMA((OUT_COPIES,)),
        ],
        compiler_params=pltpu.CompilerParams(vmem_limit_bytes=6 * MIB + held + scratch),
        name="attend",
        cost_estimate=pl.CostEstimate(
            flops=2 * total * (width + 2 * rows) * up_weight.shape[1],
            bytes_accessed=2 * (up_weight.size + 3 * rows * up_weight.shape[1]),
            transcendentals=heads * rows * total,
        ),
    )(full, payload, expanded, up_weight, together, fetched, *swapped, prompt_length)


def solution(mesh):
    placed = (
        P(("parts", "ctx"), ("head", "sub")),
        P(("parts", "ctx"), None),
        P(("parts", "ctx"), None),
        P(),
        P(None, ("head", "sub")),
        P("parts"),
    )
    step = jax.shard_map(
        functools.partial(per_device, mesh.shape["ctx"], mesh.shape["sub"]),
        mesh=mesh,
        in_specs=placed,
        out_specs=P(("parts", "ctx"), ("head", "sub")),
        check_vma=False,
    )
    if len(plan(mesh.shape["ctx"], mesh.shape["sub"])[0]) > 1:
        return step
    return step
```

```python
import functools
import math

import jax
import jax.numpy as jnp
import numpy as np
from jax import lax
from jax.experimental import pallas as pl
from jax.experimental.pallas import tpu as pltpu
from jax.sharding import PartitionSpec as P

ROPE = 64
NOPE = 128
VDIM = 128
WIDE = 128
FULL = 256
MASKED = -1e30
MIB = 1024 * 1024
PACK_FLOPS = 4 * 10**9
OUT_COPIES = 4
EXPONENT = math.log2(math.e) / math.sqrt(NOPE + ROPE)

VMEM = pl.BlockSpec(memory_space=pltpu.VMEM)
SMEM = pl.BlockSpec(memory_space=pltpu.SMEM)
HBM = pl.BlockSpec(memory_space=pltpu.HBM)
ANY = pl.BlockSpec(memory_space=pl.ANY)


def tables(positions):
    half = ROPE // 2
    frequency = np.float32(10000.0) ** (-np.arange(half, dtype=np.float32) / np.float32(half))
    angles = np.arange(positions, dtype=np.float32)[:, None] * frequency.astype(np.float32)
    cosines, sines = np.cos(angles), np.sin(angles)
    rows = np.concatenate([cosines, cosines, -sines, sines], 1).astype(np.float32)
    columns = np.concatenate([cosines, sines], 1).T.astype(np.float32)
    return rows, np.ascontiguousarray(columns)


def normalise(latent, gain):
    wide = latent.astype(jnp.float32)
    mean = jnp.mean(wide * wide, -1, keepdims=True)
    return (wide * lax.rsqrt(mean + 1e-06) * gain).astype(jnp.bfloat16)


def last_tile(rope, table):
    half = ROPE // 2
    keys = rope.astype(jnp.float32)
    low, high = keys[:half], keys[half:]
    cosines, sines = table[:half], table[half:]
    zeros = jnp.zeros((WIDE - ROPE, rope.shape[1]), jnp.float32)
    rotated = [low * cosines - high * sines, low * sines + high * cosines, zeros]
    return jnp.concatenate(rotated, 0).T.astype(jnp.bfloat16)


def masked_tile(tile, allowed):
    lane = lax.broadcasted_iota(jnp.int32, tile.shape, 1)
    token = lax.broadcasted_iota(jnp.int32, tile.shape, 0)
    bias = jnp.where((lane == ROPE) & ~allowed(token), MASKED, 0.0)
    return tile + bias.astype(jnp.bfloat16)


def pack_kernel(
    latent_hbm,
    rope_hbm,
    gain_hbm,
    tables_hbm,
    payload,
    piece,
    latent,
    rope,
    gain,
    table,
    arrived,
):
    rows, width = latent.shape
    ctx, sub = lax.axis_index("ctx"), lax.axis_index("sub")
    copies = [
        pltpu.make_async_copy(source, target, arrived.at[k])
        for k, (source, target) in enumerate(
            [
                (latent_hbm, latent),
                (gain_hbm, gain),
                (rope_hbm, rope),
                (tables_hbm.at[ctx], table),
            ]
        )
    ]
    for copy in copies:
        copy.start()
    for copy in copies:
        copy.wait()
    normed = normalise(latent[...], gain[...])
    extra = last_tile(rope[...], table[...])
    payload[:, :width] = normed
    payload[:, width:] = extra
    size = piece.shape[0]
    for k in range(rows // size):

        @pl.when(sub == k)
        def _():
            piece[:, :width] = normed[k * size : (k + 1) * size]
            piece[:, width:] = extra[k * size : (k + 1) * size]


def mid_kernel(sources, piece_sources, gain, tables, length, *rest):
    count = len(sources)
    latents, ropes, pieces = rest[:count], rest[count : 2 * count], rest[2 * count : -1]
    together = rest[-1]
    ctx, sub = lax.axis_index("ctx"), lax.axis_index("sub")

    def origin(source):
        picked = [
            jnp.where((sub == s) & (ctx == j), i + 1, 0)
            for s, edges in enumerate(source)
            for i, j in edges
        ]
        return sum(picked) - 1

    def allowed(start, there):
        return lambda token: (start + token < length[0]) & there

    at = 0
    for latent, rope, source in zip(latents, ropes, sources, strict=True):
        rows, width = latent.shape
        shard = origin(source)
        start = jnp.maximum(shard, 0)
        together[at : at + rows, :width] = normalise(latent[...], gain[...])
        together[at : at + rows, width:] = masked_tile(
            last_tile(rope[...], tables[start]), allowed(start * rows, shard >= 0)
        )
        at += rows
    for piece, edges in zip(pieces, piece_sources, strict=True):
        size, width = piece.shape[0], piece.shape[1] - WIDE
        cores = lax.axis_size("sub")
        shard = origin([edges] * cores)
        together[at : at + size, :width] = piece[:, :width]
        together[at : at + size, width:] = masked_tile(
            piece[:, width:], allowed((shard * cores + sub) * size, shard >= 0)
        )
        at += size


def grow_kernel(step, together, weight, grown):
    width = weight.shape[0]

    @pl.when(lax.axis_index("ctx") > 0)
    def _():
        for k in range(weight.shape[1] // step):
            at = slice(k * step, (k + 1) * step)
            grown[:, at] = jnp.dot(
                together[:, :width], weight[:, at], preferred_element_type=jnp.float32
            ).astype(jnp.bfloat16)


def own_kernel(heads, queries, payload, weight, tables_hbm, expanded, full, table, arrived):
    copy = pltpu.make_async_copy(tables_hbm.at[lax.axis_index("ctx")], table, arrived)
    copy.start()
    copy.wait()
    rows = queries.shape[0]
    width = weight.shape[0]
    cosines = jnp.concatenate([table[:, :ROPE]] * 2, 1)
    sines = jnp.concatenate([table[:, ROPE:]] * 2, 1)
    lane = lax.broadcasted_iota(jnp.int32, (rows, 2 * ROPE), 1)
    lower = lane % ROPE < ROPE // 2
    tail = (lax.broadcasted_iota(jnp.int32, (rows, FULL - NOPE - ROPE), 1) == 0).astype(
        jnp.float32
    ).astype(jnp.bfloat16)
    each = NOPE + ROPE
    for i in range(heads // 2):
        pair = queries[:, 2 * each * i : 2 * each * (i + 1)]
        ropes = jnp.concatenate([pair[:, NOPE:each], pair[:, each + NOPE :]], 1).astype(jnp.float32)
        turned = jnp.where(
            lower, pltpu.roll(ropes, 2 * ROPE - ROPE // 2, 1), pltpu.roll(ropes, ROPE // 2, 1)
        )
        ropes = (ropes * cosines + turned * sines).astype(jnp.bfloat16)
        for e in range(2):
            at = FULL * (2 * i + e)
            full[:, at : at + NOPE] = pair[:, each * e : each * e + NOPE]
            full[:, at + NOPE : at + FULL] = jnp.concatenate(
                [ropes[:, ROPE * e : ROPE * (e + 1)], tail], 1
            )
    columns = NOPE + VDIM
    for i in range(heads // 2):
        at = slice(2 * columns * i, 2 * columns * (i + 1))
        expanded[:, at] = jnp.dot(
            payload[:, :width], weight[:, at], preferred_element_type=jnp.float32
        ).astype(jnp.bfloat16)


def attend_kernel(heads, sets, levels, full, own, expanded, weight, together, fetched, *rest):
    swapped = rest[:-8]
    length, out_hbm, last_own, grown, scores, weights, out, sent = rest[-8:]
    rows = full.shape[0]
    width = weight.shape[0]
    columns = NOPE + VDIM
    ctx = lax.axis_index("ctx")
    row = lax.broadcasted_iota(jnp.int32, (rows, rows), 0)
    causal = lax.broadcasted_iota(jnp.int32, (rows, rows), 1) <= row
    live = ctx * rows + lax.broadcasted_iota(jnp.int32, (rows, 1), 0) < length[0]
    last_own[...] = masked_tile(own[:, width:], lambda token: ctx * rows + token < length[0])
    stage, buffers = 2, 4
    block = VDIM * heads // OUT_COPIES

    def leave(k):
        at = pl.ds(k * block, block)
        return pltpu.make_async_copy(out.at[:, at], out_hbm.at[:, at], sent.at[k])

    def run(used):
        every = together.shape[0]
        both = ((0, sets), (sets, every))
        spans = [span for span, use in zip(both, used, strict=True) if use]
        extent = slice(spans[0][0], spans[-1][1]) if spans else slice(0, 0)
        total = rows + sum(end - begin for begin, end in spans) * (1 + len(swapped))

        def rows_of(own_part, direct_part, swapped_part):
            found = [own_part()]
            for begin, end in spans:
                found.append(direct_part(slice(begin, end)))
                for r in range(len(swapped)):
                    found.append(swapped_part(r, slice(begin, end)))
            return found[0] if len(found) == 1 else jnp.concatenate(found, 0)

        def grow(i):
            at = slice(2 * columns * i, 2 * columns * (i + 1))
            for r, ref in enumerate(swapped):
                if spans:
                    grown[i % 4, r, extent] = jnp.dot(
                        ref[extent, :width], weight[:, at], preferred_element_type=jnp.float32
                    ).astype(jnp.bfloat16)

        def column(h, begin, end):
            i, e = divmod(h, 2)
            return rows_of(
                lambda: expanded[:, columns * h + begin : columns * h + end],
                lambda piece: fetched[piece, columns * h + begin : columns * h + end],
                lambda r, piece: grown[i % 4, r, piece, columns * e + begin : columns * e + end],
            )

        def score(h):
            last = rows_of(
                lambda: last_own[...],
                lambda piece: together[piece, width:],
                lambda r, piece: swapped[r][piece, width:],
            )
            found = lax.dot_general(
                full[:, FULL * h : FULL * (h + 1)],
                jnp.concatenate([column(h, 0, NOPE), last], 1),
                (((1,), (1,)), ((), ())),
                preferred_element_type=jnp.float32,
            )
            scores[h % buffers, :, :rows] = jnp.where(causal, found[:, :rows], MASKED)
            if total > rows:
                scores[h % buffers, :, rows:total] = found[:, rows:]

        def soften(h):
            found = scores[h % buffers, :, :total]
            top = jnp.max(found, 1, keepdims=True)
            raw = jnp.exp2(found * EXPONENT - top * EXPONENT)
            weights[h % buffers, :, :total] = raw.astype(jnp.bfloat16)
            return jnp.sum(raw, 1, keepdims=True)

        def mix(h, total_h):
            mixed = jnp.dot(
                weights[h % buffers, :, :total],
                column(h, NOPE, columns),
                preferred_element_type=jnp.float32,
            )
            out[:, VDIM * h : VDIM * (h + 1)] = jnp.where(live, mixed / total_h, 0.0).astype(
                jnp.bfloat16
            )
            if (h + 1) % (heads // OUT_COPIES) == 0:
                leave(h // (heads // OUT_COPIES)).start()

        totals = {}
        steps = heads // stage
        grow(0)
        for t in range(steps + 2):
            if t + 1 < heads // 2:
                grow(t + 1)
            for h in range(stage * t, stage * (t + 1)):
                if t < steps:
                    score(h)
            for h in range(stage * (t - 1), stage * t):
                if 0 <= t - 1 < steps:
                    totals[h] = soften(h)
            for h in range(stage * (t - 2), stage * (t - 1)):
                if 0 <= t - 2 < steps:
                    mix(h, totals.pop(h))

    for used, places in levels:

        @pl.when(functools.reduce(jnp.logical_or, [ctx == c for c in places]))
        def _():
            run(used)

    for k in range(OUT_COPIES):
        leave(k).wait()


def plan(shards, cores):
    colours = []
    for distance in range(shards - 1, 0, -1):
        for source in range(shards - distance):
            target = source + distance
            for colour in colours:
                if all(source != i and target != j for i, j in colour):
                    colour.append((source, target))
                    break
            else:
                colours.append([(source, target)])
    whole = len(colours) // cores * cores
    sets = [colours[k : k + cores] for k in range(0, whole, cores)]
    return sets, colours[whole:]


def in_hbm(x):
    return pltpu.with_memory_space_constraint(x, pltpu.HBM)


def grant(*arrays):
    return pltpu.CompilerParams(vmem_limit_bytes=4 * MIB + 2 * sum(x.size for x in arrays))


def per_device(
    ctx_size, sub_size, queries, latent, rope_keys, latent_gain, up_weight, prompt_length
):
    rows, width = latent.shape
    heads = up_weight.shape[1] // (NOPE + VDIM)
    by_row, by_column = tables(ctx_size * rows)
    by_row = jnp.asarray(by_row.reshape(ctx_size, rows, 2 * ROPE))
    by_column = jnp.asarray(by_column.reshape(ROPE, ctx_size, rows).transpose(1, 0, 2))
    gain = latent_gain.reshape(1, width)
    turned = rope_keys.T
    bf16 = jnp.bfloat16
    wide = width + WIDE

    cores = ("ctx", "sub")
    sets, rest = plan(ctx_size, sub_size)

    def send(data, by_core):
        pairs = [
            (i * sub_size + s, j * sub_size + s) for s, edges in enumerate(by_core) for i, j in edges
        ]
        return lax.ppermute(data, cores, pairs)

    latents = [send(latent, by_core) for by_core in sets]
    ropes = [send(turned, by_core) for by_core in sets]

    payload, piece = pl.pallas_call(
        pack_kernel,
        in_specs=[HBM] * 4,
        out_specs=[VMEM] * 2,
        out_shape=[
            jax.ShapeDtypeStruct((rows, wide), bf16),
            jax.ShapeDtypeStruct((rows // sub_size, wide), bf16),
        ],
        scratch_shapes=[
            pltpu.VMEM((rows, width), bf16),
            pltpu.VMEM((ROPE, rows), bf16),
            pltpu.VMEM((1, width), jnp.float32),
            pltpu.VMEM((ROPE, rows), jnp.float32),
            pltpu.SemaphoreType.DMA((4,)),
        ],
        cost_estimate=pl.CostEstimate(
            flops=PACK_FLOPS, bytes_accessed=8 * rows * width, transcendentals=0
        ),
        compiler_params=grant(),
        name="pack",
    )(in_hbm(latent), in_hbm(turned), in_hbm(gain), in_hbm(by_column))

    pieces = [send(piece, [edges] * sub_size) for edges in rest]

    expanded, full = pl.pallas_call(
        functools.partial(own_kernel, heads),
        in_specs=[VMEM] * 3 + [ANY],
        out_specs=[VMEM] * 2,
        out_shape=[
            jax.ShapeDtypeStruct((rows, up_weight.shape[1]), bf16),
            jax.ShapeDtypeStruct((rows, heads * FULL), bf16),
        ],
        scratch_shapes=[pltpu.VMEM((rows, 2 * ROPE), jnp.float32), pltpu.SemaphoreType.DMA],
        compiler_params=grant(queries, up_weight, payload, up_weight[:rows], up_weight[:rows]),
        name="own",
        cost_estimate=pl.CostEstimate(
            flops=2 * rows * width * up_weight.shape[1],
            bytes_accessed=2 * (queries.size + up_weight.size + 2 * rows * up_weight.shape[1]),
            transcendentals=0,
        ),
    )(queries, payload, up_weight, by_row)

    expanded, prompt_length = lax.optimization_barrier((expanded, prompt_length))
    latents, ropes, pieces, expanded, full = lax.optimization_barrier(
        (latents, ropes, pieces, expanded, full)
    )
    reach = sum(x.shape[0] for x in (*latents, *pieces))
    whole = sum(x.shape[0] for x in latents)
    together = pl.pallas_call(
        functools.partial(mid_kernel, sets, rest),
        in_specs=[VMEM] * 2 + [SMEM] + [VMEM] * (2 * len(latents) + len(pieces)),
        out_specs=VMEM,
        out_shape=jax.ShapeDtypeStruct((reach, wide), bf16),
        compiler_params=grant(by_column, by_column, *latents, *ropes, *pieces, *pieces, *latents),
        name="mid",
    )(gain, by_column, prompt_length, *latents, *ropes, *pieces)

    swapped = []
    for r in range(1, sub_size):
        pairs = [(s, (s + r) % sub_size) for s in range(sub_size)]
        swapped.append(lax.ppermute(together, "sub", pairs))

    fetched = pl.pallas_call(
        functools.partial(grow_kernel, 4 * (NOPE + VDIM)),
        in_specs=[VMEM] * 2,
        out_specs=VMEM,
        out_shape=jax.ShapeDtypeStruct((reach, up_weight.shape[1]), bf16),
        compiler_params=pltpu.CompilerParams(
            vmem_limit_bytes=4 * MIB
            + 2 * (up_weight.size + reach * (wide + up_weight.shape[1]))
        ),
        name="grow",
        cost_estimate=pl.CostEstimate(
            flops=2 * reach * width * up_weight.shape[1],
            bytes_accessed=2 * (up_weight.size + reach * up_weight.shape[1]),
            transcendentals=0,
        ),
    )(together, up_weight)

    parts = [[e for by_core in sets for e in by_core], rest]
    needs = [
        tuple(any(j == c for edges in part for _, j in edges) for part in parts)
        for c in range(ctx_size)
    ]
    levels = [(u, [c for c in range(ctx_size) if needs[c] == u]) for u in sorted(set(needs))]
    total = rows + sub_size * reach
    held = 2 * (up_weight.size + (reach + 2 * rows) * up_weight.shape[1] + total * wide)
    scratch = 8 * total * (NOPE + VDIM) * 2 + 24 * rows * total + 2 * rows * heads * VDIM
    return pl.pallas_call(
        functools.partial(attend_kernel, heads, whole, levels),
        in_specs=[VMEM] * (6 + len(swapped)) + [SMEM],
        out_specs=ANY,
        out_shape=jax.ShapeDtypeStruct((rows, heads * VDIM), bf16),
        scratch_shapes=[
            pltpu.VMEM((rows, WIDE), bf16),
            pltpu.VMEM((4, len(swapped), reach, 2 * (NOPE + VDIM)), bf16),
            pltpu.VMEM((4, rows, total), jnp.float32),
            pltpu.VMEM((4, rows, total), bf16),
            pltpu.VMEM((rows, heads * VDIM), bf16),
            pltpu.SemaphoreType.DMA((OUT_COPIES,)),
        ],
        compiler_params=pltpu.CompilerParams(vmem_limit_bytes=6 * MIB + held + scratch),
        name="attend",
        cost_estimate=pl.CostEstimate(
            flops=2 * total * (width + 2 * rows) * up_weight.shape[1],
            bytes_accessed=2 * (up_weight.size + 3 * rows * up_weight.shape[1]),
            transcendentals=heads * rows * total,
        ),
    )(full, payload, expanded, up_weight, together, fetched, *swapped, prompt_length)


def solution(mesh):
    placed = (
        P(("parts", "ctx"), ("head", "sub")),
        P(("parts", "ctx"), None),
        P(("parts", "ctx"), None),
        P(),
        P(None, ("head", "sub")),
        P("parts"),
    )
    step = jax.shard_map(
        functools.partial(per_device, mesh.shape["ctx"], mesh.shape["sub"]),
        mesh=mesh,
        in_specs=placed,
        out_specs=P(("parts", "ctx"), ("head", "sub")),
        check_vma=False,
    )
    if len(plan(mesh.shape["ctx"], mesh.shape["sub"])[0]) > 1:
        return step
    return step
```

```python
import functools
import math

import jax
import jax.numpy as jnp
import numpy as np
from jax import lax
from jax.experimental import pallas as pl
from jax.experimental.pallas import tpu as pltpu
from jax.sharding import PartitionSpec as P

ROPE = 64
NOPE = 128
VDIM = 128
WIDE = 128
FULL = 256
MASKED = -1e30
MIB = 1024 * 1024
PACK_FLOPS = 4 * 10**9
OUT_COPIES = 4
EXPONENT = math.log2(math.e) / math.sqrt(NOPE + ROPE)

VMEM = pl.BlockSpec(memory_space=pltpu.VMEM)
SMEM = pl.BlockSpec(memory_space=pltpu.SMEM)
HBM = pl.BlockSpec(memory_space=pltpu.HBM)
ANY = pl.BlockSpec(memory_space=pl.ANY)


def tables(positions):
    half = ROPE // 2
    frequency = np.float32(10000.0) ** (-np.arange(half, dtype=np.float32) / np.float32(half))
    angles = np.arange(positions, dtype=np.float32)[:, None] * frequency.astype(np.float32)
    cosines, sines = np.cos(angles), np.sin(angles)
    rows = np.concatenate([cosines, cosines, -sines, sines], 1).astype(np.float32)
    columns = np.concatenate([cosines, sines], 1).T.astype(np.float32)
    return rows, np.ascontiguousarray(columns)


def normalise(latent, gain):
    wide = latent.astype(jnp.float32)
    mean = jnp.mean(wide * wide, -1, keepdims=True)
    return (wide * lax.rsqrt(mean + 1e-06) * gain).astype(jnp.bfloat16)


def last_tile(rope, table):
    half = ROPE // 2
    keys = rope.astype(jnp.float32)
    low, high = keys[:half], keys[half:]
    cosines, sines = table[:half], table[half:]
    zeros = jnp.zeros((WIDE - ROPE, rope.shape[1]), jnp.float32)
    rotated = [low * cosines - high * sines, low * sines + high * cosines, zeros]
    return jnp.concatenate(rotated, 0).T.astype(jnp.bfloat16)


def masked_tile(tile, allowed):
    lane = lax.broadcasted_iota(jnp.int32, tile.shape, 1)
    token = lax.broadcasted_iota(jnp.int32, tile.shape, 0)
    bias = jnp.where((lane == ROPE) & ~allowed(token), MASKED, 0.0)
    return tile + bias.astype(jnp.bfloat16)


def pack_kernel(
    latent_hbm,
    rope_hbm,
    gain_hbm,
    tables_hbm,
    payload,
    piece,
    latent,
    rope,
    gain,
    table,
    arrived,
):
    rows, width = latent.shape
    ctx, sub = lax.axis_index("ctx"), lax.axis_index("sub")
    copies = [
        pltpu.make_async_copy(source, target, arrived.at[k])
        for k, (source, target) in enumerate(
            [
                (latent_hbm, latent),
                (gain_hbm, gain),
                (rope_hbm, rope),
                (tables_hbm.at[ctx], table),
            ]
        )
    ]
    for copy in copies:
        copy.start()
    for copy in copies:
        copy.wait()
    normed = normalise(latent[...], gain[...])
    extra = last_tile(rope[...], table[...])
    payload[:, :width] = normed
    payload[:, width:] = extra
    size = piece.shape[0]
    for k in range(rows // size):

        @pl.when(sub == k)
        def _():
            piece[:, :width] = normed[k * size : (k + 1) * size]
            piece[:, width:] = extra[k * size : (k + 1) * size]


def mid_kernel(sources, piece_sources, gain, tables, length, *rest):
    count = len(sources)
    latents, ropes, pieces = rest[:count], rest[count : 2 * count], rest[2 * count : -1]
    together = rest[-1]
    ctx, sub = lax.axis_index("ctx"), lax.axis_index("sub")

    def origin(source):
        picked = [
            jnp.where((sub == s) & (ctx == j), i + 1, 0)
            for s, edges in enumerate(source)
            for i, j in edges
        ]
        return sum(picked) - 1

    def allowed(start, there):
        return lambda token: (start + token < length[0]) & there

    at = 0
    for latent, rope, source in zip(latents, ropes, sources, strict=True):
        rows, width = latent.shape
        shard = origin(source)
        start = jnp.maximum(shard, 0)
        together[at : at + rows, :width] = normalise(latent[...], gain[...])
        together[at : at + rows, width:] = masked_tile(
            last_tile(rope[...], tables[start]), allowed(start * rows, shard >= 0)
        )
        at += rows
    for piece, edges in zip(pieces, piece_sources, strict=True):
        size, width = piece.shape[0], piece.shape[1] - WIDE
        cores = lax.axis_size("sub")
        shard = origin([edges] * cores)
        together[at : at + size, :width] = piece[:, :width]
        together[at : at + size, width:] = masked_tile(
            piece[:, width:], allowed((shard * cores + sub) * size, shard >= 0)
        )
        at += size


def grow_kernel(heads, together, weight, turned, straight, values):
    width = weight.shape[0]

    @pl.when(lax.axis_index("ctx") > 0)
    def _():
        for i in range(heads // 2):
            project(together[:, :width], weight, i, turned, values, straight)


def project(rows, weight, pair, turned, values, straight=None):
    columns = NOPE + VDIM
    at = slice(2 * columns * pair, 2 * columns * (pair + 1))
    expanded = jnp.dot(rows, weight[:, at], preferred_element_type=jnp.float32).astype(jnp.bfloat16)
    tokens = turned.shape[1]
    for e in range(2):
        h = 2 * pair + e
        keys = expanded[:, columns * e : columns * e + NOPE]
        turned[NOPE * h : NOPE * (h + 1)] = keys[:tokens].T
        if straight is not None:
            straight[:, NOPE * h : NOPE * (h + 1)] = keys[tokens:]
        values[:, VDIM * h : VDIM * (h + 1)] = expanded[:, columns * e + NOPE : columns * (e + 1)]


def own_kernel(heads, queries, payload, weight, tables_hbm, keys, values, full, table, arrived):
    copy = pltpu.make_async_copy(tables_hbm.at[lax.axis_index("ctx")], table, arrived)
    copy.start()
    copy.wait()
    rows = queries.shape[0]
    width = weight.shape[0]
    cosines = jnp.concatenate([table[:, :ROPE]] * 2, 1)
    sines = jnp.concatenate([table[:, ROPE:]] * 2, 1)
    lane = lax.broadcasted_iota(jnp.int32, (rows, 2 * ROPE), 1)
    lower = lane % ROPE < ROPE // 2
    tail = (lax.broadcasted_iota(jnp.int32, (rows, FULL - NOPE - ROPE), 1) == 0).astype(
        jnp.float32
    ).astype(jnp.bfloat16)
    each = NOPE + ROPE
    for i in range(heads // 2):
        pair = queries[:, 2 * each * i : 2 * each * (i + 1)]
        ropes = jnp.concatenate([pair[:, NOPE:each], pair[:, each + NOPE :]], 1).astype(jnp.float32)
        turned = jnp.where(
            lower, pltpu.roll(ropes, 2 * ROPE - ROPE // 2, 1), pltpu.roll(ropes, ROPE // 2, 1)
        )
        ropes = (ropes * cosines + turned * sines).astype(jnp.bfloat16)
        for e in range(2):
            at = FULL * (2 * i + e)
            full[:, at : at + NOPE] = pair[:, each * e : each * e + NOPE]
            full[:, at + NOPE : at + FULL] = jnp.concatenate(
                [ropes[:, ROPE * e : ROPE * (e + 1)], tail], 1
            )
    for i in range(heads // 2):
        project(payload[:, :width], weight, i, keys, values)


def attend_kernel(
    heads,
    sets,
    levels,
    full,
    own,
    own_keys,
    own_values,
    weight,
    together,
    turned,
    straight,
    fetched,
    *rest,
):
    swapped = rest[:-9]
    length, out_hbm, last_own, last_turned, grown, scores, weights, out, sent = rest[-9:]
    rows = full.shape[0]
    width = weight.shape[0]
    columns = NOPE + VDIM
    ctx = lax.axis_index("ctx")
    row = lax.broadcasted_iota(jnp.int32, (rows, rows), 0)
    causal = lax.broadcasted_iota(jnp.int32, (rows, rows), 1) <= row
    live = ctx * rows + lax.broadcasted_iota(jnp.int32, (rows, 1), 0) < length[0]
    last_own[...] = masked_tile(own[:, width:], lambda token: ctx * rows + token < length[0])
    stage, buffers = 2, 4
    block = VDIM * heads // OUT_COPIES

    def leave(k):
        at = pl.ds(k * block, block)
        return pltpu.make_async_copy(out.at[:, at], out_hbm.at[:, at], sent.at[k])

    def run(used):
        every = together.shape[0]
        both = ((0, sets), (sets, every))
        spans = [span for span, use in zip(both, used, strict=True) if use]
        extent = slice(spans[0][0], spans[-1][1]) if spans else slice(0, 0)
        total = rows + sum(end - begin for begin, end in spans) * (1 + len(swapped))

        def rows_of(own_part, direct_part, swapped_part):
            found = [own_part()]
            for begin, end in spans:
                found.append(direct_part(slice(begin, end)))
                for r in range(len(swapped)):
                    found.append(swapped_part(r, slice(begin, end)))
            return found[0] if len(found) == 1 else jnp.concatenate(found, 0)

        def grow(i):
            at = slice(2 * columns * i, 2 * columns * (i + 1))
            for r, ref in enumerate(swapped):
                if spans:
                    grown[i % 4, r, extent] = jnp.dot(
                        ref[extent, :width], weight[:, at], preferred_element_type=jnp.float32
                    ).astype(jnp.bfloat16)

        last = rows_of(
            lambda: last_own[...],
            lambda piece: together[piece, width:],
            lambda r, piece: swapped[r][piece, width:],
        )
        last_turned[:, :total] = last.T

        def keys_of(h):
            i, e = divmod(h, 2)
            at, head = slice(columns * e, columns * e + NOPE), slice(NOPE * h, NOPE * (h + 1))
            found = [own_keys[head]]
            if used[0]:
                found.append(turned[head])
                found += [grown[i % 4, r, :sets, at].T for r in range(len(swapped))]
            if used[1]:
                pieces = [grown[i % 4, r, sets:, at] for r in range(len(swapped))]
                found.append(jnp.concatenate([straight[:, head], *pieces], 0).T)
            return found[0] if len(found) == 1 else jnp.concatenate(found, 1)

        def values_of(h):
            i, e = divmod(h, 2)
            at = slice(columns * e + NOPE, columns * (e + 1))
            return rows_of(
                lambda: own_values[:, VDIM * h : VDIM * (h + 1)],
                lambda piece: fetched[piece, VDIM * h : VDIM * (h + 1)],
                lambda r, piece: grown[i % 4, r, piece, at],
            )

        def score(h):
            found = jnp.dot(
                full[:, FULL * h : FULL * (h + 1)],
                jnp.concatenate([keys_of(h), last_turned[:, :total]], 0),
                preferred_element_type=jnp.float32,
            )
            scores[h % buffers, :, :rows] = jnp.where(causal, found[:, :rows], MASKED)
            if total > rows:
                scores[h % buffers, :, rows:total] = found[:, rows:]

        def soften(h):
            found = scores[h % buffers, :, :total]
            top = jnp.max(found, 1, keepdims=True)
            raw = jnp.exp2(found * EXPONENT - top * EXPONENT)
            weights[h % buffers, :, :total] = raw.astype(jnp.bfloat16)
            return jnp.sum(raw, 1, keepdims=True)

        def mix(h, total_h):
            mixed = jnp.dot(
                weights[h % buffers, :, :total],
                values_of(h),
                preferred_element_type=jnp.float32,
            )
            out[:, VDIM * h : VDIM * (h + 1)] = jnp.where(live, mixed / total_h, 0.0).astype(
                jnp.bfloat16
            )
            if (h + 1) % (heads // OUT_COPIES) == 0:
                leave(h // (heads // OUT_COPIES)).start()

        totals = {}
        steps = heads // stage
        grow(0)
        for t in range(steps + 2):
            if t + 1 < heads // 2:
                grow(t + 1)
            for h in range(stage * t, stage * (t + 1)):
                if t < steps:
                    score(h)
            for h in range(stage * (t - 1), stage * t):
                if 0 <= t - 1 < steps:
                    totals[h] = soften(h)
            for h in range(stage * (t - 2), stage * (t - 1)):
                if 0 <= t - 2 < steps:
                    mix(h, totals.pop(h))

    for used, places in levels:

        @pl.when(functools.reduce(jnp.logical_or, [ctx == c for c in places]))
        def _():
            run(used)

    for k in range(OUT_COPIES):
        leave(k).wait()


def plan(shards, cores):
    colours = []
    for distance in range(shards - 1, 0, -1):
        for source in range(shards - distance):
            target = source + distance
            for colour in colours:
                if all(source != i and target != j for i, j in colour):
                    colour.append((source, target))
                    break
            else:
                colours.append([(source, target)])
    whole = len(colours) // cores * cores
    sets = [colours[k : k + cores] for k in range(0, whole, cores)]
    return sets, colours[whole:]


def in_hbm(x):
    return pltpu.with_memory_space_constraint(x, pltpu.HBM)


def grant(*arrays):
    return pltpu.CompilerParams(vmem_limit_bytes=4 * MIB + 2 * sum(x.size for x in arrays))


def per_device(
    ctx_size, sub_size, queries, latent, rope_keys, latent_gain, up_weight, prompt_length
):
    rows, width = latent.shape
    heads = up_weight.shape[1] // (NOPE + VDIM)
    by_row, by_column = tables(ctx_size * rows)
    by_row = jnp.asarray(by_row.reshape(ctx_size, rows, 2 * ROPE))
    by_column = jnp.asarray(by_column.reshape(ROPE, ctx_size, rows).transpose(1, 0, 2))
    gain = latent_gain.reshape(1, width)
    turned = rope_keys.T
    bf16 = jnp.bfloat16
    wide = width + WIDE

    cores = ("ctx", "sub")
    sets, rest = plan(ctx_size, sub_size)

    def send(data, by_core):
        pairs = [
            (i * sub_size + s, j * sub_size + s) for s, edges in enumerate(by_core) for i, j in edges
        ]
        return lax.ppermute(data, cores, pairs)

    latents = [send(latent, by_core) for by_core in sets]
    ropes = [send(turned, by_core) for by_core in sets]

    payload, piece = pl.pallas_call(
        pack_kernel,
        in_specs=[HBM] * 4,
        out_specs=[VMEM] * 2,
        out_shape=[
            jax.ShapeDtypeStruct((rows, wide), bf16),
            jax.ShapeDtypeStruct((rows // sub_size, wide), bf16),
        ],
        scratch_shapes=[
            pltpu.VMEM((rows, width), bf16),
            pltpu.VMEM((ROPE, rows), bf16),
            pltpu.VMEM((1, width), jnp.float32),
            pltpu.VMEM((ROPE, rows), jnp.float32),
            pltpu.SemaphoreType.DMA((4,)),
        ],
        cost_estimate=pl.CostEstimate(
            flops=PACK_FLOPS, bytes_accessed=8 * rows * width, transcendentals=0
        ),
        compiler_params=grant(),
        name="pack",
    )(in_hbm(latent), in_hbm(turned), in_hbm(gain), in_hbm(by_column))

    pieces = [send(piece, [edges] * sub_size) for edges in rest]

    own_keys, own_values, full = pl.pallas_call(
        functools.partial(own_kernel, heads),
        in_specs=[VMEM] * 3 + [ANY],
        out_specs=[VMEM] * 3,
        out_shape=[
            jax.ShapeDtypeStruct((heads * NOPE, rows), bf16),
            jax.ShapeDtypeStruct((rows, heads * VDIM), bf16),
            jax.ShapeDtypeStruct((rows, heads * FULL), bf16),
        ],
        scratch_shapes=[pltpu.VMEM((rows, 2 * ROPE), jnp.float32), pltpu.SemaphoreType.DMA],
        compiler_params=grant(queries, up_weight, payload, up_weight[:rows], up_weight[:rows]),
        name="own",
        cost_estimate=pl.CostEstimate(
            flops=2 * rows * width * up_weight.shape[1],
            bytes_accessed=2 * (queries.size + up_weight.size + 2 * rows * up_weight.shape[1]),
            transcendentals=0,
        ),
    )(queries, payload, up_weight, by_row)

    own_keys, prompt_length = lax.optimization_barrier((own_keys, prompt_length))
    latents, ropes, pieces, own_keys, own_values, full = lax.optimization_barrier(
        (latents, ropes, pieces, own_keys, own_values, full)
    )
    reach = sum(x.shape[0] for x in (*latents, *pieces))
    whole = sum(x.shape[0] for x in latents)
    together = pl.pallas_call(
        functools.partial(mid_kernel, sets, rest),
        in_specs=[VMEM] * 2 + [SMEM] + [VMEM] * (2 * len(latents) + len(pieces)),
        out_specs=VMEM,
        out_shape=jax.ShapeDtypeStruct((reach, wide), bf16),
        compiler_params=grant(by_column, by_column, *latents, *ropes, *pieces, *pieces, *latents),
        name="mid",
    )(gain, by_column, prompt_length, *latents, *ropes, *pieces)

    swapped = []
    for r in range(1, sub_size):
        pairs = [(s, (s + r) % sub_size) for s in range(sub_size)]
        swapped.append(lax.ppermute(together, "sub", pairs))

    fetched = pl.pallas_call(
        functools.partial(grow_kernel, heads),
        in_specs=[VMEM] * 2,
        out_specs=[VMEM] * 3,
        out_shape=[
            jax.ShapeDtypeStruct((heads * NOPE, whole), bf16),
            jax.ShapeDtypeStruct((reach - whole, heads * NOPE), bf16),
            jax.ShapeDtypeStruct((reach, heads * VDIM), bf16),
        ],
        compiler_params=pltpu.CompilerParams(
            vmem_limit_bytes=4 * MIB
            + 2 * (up_weight.size + reach * (wide + up_weight.shape[1]))
        ),
        name="grow",
        cost_estimate=pl.CostEstimate(
            flops=2 * reach * width * up_weight.shape[1],
            bytes_accessed=2 * (up_weight.size + reach * up_weight.shape[1]),
            transcendentals=0,
        ),
    )(together, up_weight)

    parts = [[e for by_core in sets for e in by_core], rest]
    needs = [
        tuple(any(j == c for edges in part for _, j in edges) for part in parts)
        for c in range(ctx_size)
    ]
    levels = [(u, [c for c in range(ctx_size) if needs[c] == u]) for u in sorted(set(needs))]
    total = rows + sub_size * reach
    held = 2 * (up_weight.size + (reach + 2 * rows) * up_weight.shape[1] + total * wide)
    scratch = 8 * total * (NOPE + VDIM) * 2 + 24 * rows * total + 2 * rows * heads * VDIM
    return pl.pallas_call(
        functools.partial(attend_kernel, heads, whole, levels),
        in_specs=[VMEM] * (9 + len(swapped)) + [SMEM],
        out_specs=ANY,
        out_shape=jax.ShapeDtypeStruct((rows, heads * VDIM), bf16),
        scratch_shapes=[
            pltpu.VMEM((rows, WIDE), bf16),
            pltpu.VMEM((WIDE, total), bf16),
            pltpu.VMEM((4, len(swapped), reach, 2 * (NOPE + VDIM)), bf16),
            pltpu.VMEM((4, rows, total), jnp.float32),
            pltpu.VMEM((4, rows, total), bf16),
            pltpu.VMEM((rows, heads * VDIM), bf16),
            pltpu.SemaphoreType.DMA((OUT_COPIES,)),
        ],
        compiler_params=pltpu.CompilerParams(vmem_limit_bytes=6 * MIB + held + scratch),
        name="attend",
        cost_estimate=pl.CostEstimate(
            flops=2 * total * (width + 2 * rows) * up_weight.shape[1],
            bytes_accessed=2 * (up_weight.size + 3 * rows * up_weight.shape[1]),
            transcendentals=heads * rows * total,
        ),
    )(full, payload, own_keys, own_values, up_weight, together, *fetched, *swapped, prompt_length)


def solution(mesh):
    placed = (
        P(("parts", "ctx"), ("head", "sub")),
        P(("parts", "ctx"), None),
        P(("parts", "ctx"), None),
        P(),
        P(None, ("head", "sub")),
        P("parts"),
    )
    step = jax.shard_map(
        functools.partial(per_device, mesh.shape["ctx"], mesh.shape["sub"]),
        mesh=mesh,
        in_specs=placed,
        out_specs=P(("parts", "ctx"), ("head", "sub")),
        check_vma=False,
    )
    if len(plan(mesh.shape["ctx"], mesh.shape["sub"])[0]) > 1:
        return step
    return step
```

```python
import functools
import math

import jax
import jax.numpy as jnp
import numpy as np
from jax import lax
from jax.experimental import pallas as pl
from jax.experimental.pallas import tpu as pltpu
from jax.sharding import PartitionSpec as P

ROPE = 64
NOPE = 128
VDIM = 128
WIDE = 128
FULL = 256
MASKED = -1e30
MIB = 1024 * 1024
PACK_FLOPS = 4 * 10**9
OUT_COPIES = 4
EXPONENT = math.log2(math.e) / math.sqrt(NOPE + ROPE)

VMEM = pl.BlockSpec(memory_space=pltpu.VMEM)
SMEM = pl.BlockSpec(memory_space=pltpu.SMEM)
HBM = pl.BlockSpec(memory_space=pltpu.HBM)
ANY = pl.BlockSpec(memory_space=pl.ANY)


def tables(positions):
    half = ROPE // 2
    frequency = np.float32(10000.0) ** (-np.arange(half, dtype=np.float32) / np.float32(half))
    angles = np.arange(positions, dtype=np.float32)[:, None] * frequency.astype(np.float32)
    cosines, sines = np.cos(angles), np.sin(angles)
    rows = np.concatenate([cosines, cosines, -sines, sines], 1).astype(np.float32)
    columns = np.concatenate([cosines, sines], 1).T.astype(np.float32)
    return rows, np.ascontiguousarray(columns)


def normalise(latent, gain):
    wide = latent.astype(jnp.float32)
    mean = jnp.mean(wide * wide, -1, keepdims=True)
    return (wide * lax.rsqrt(mean + 1e-06) * gain).astype(jnp.bfloat16)


def last_tile(rope, table):
    half = ROPE // 2
    keys = rope.astype(jnp.float32)
    low, high = keys[:half], keys[half:]
    cosines, sines = table[:half], table[half:]
    zeros = jnp.zeros((WIDE - ROPE, rope.shape[1]), jnp.float32)
    rotated = [low * cosines - high * sines, low * sines + high * cosines, zeros]
    return jnp.concatenate(rotated, 0).T.astype(jnp.bfloat16)


def masked_tile(tile, allowed):
    lane = lax.broadcasted_iota(jnp.int32, tile.shape, 1)
    token = lax.broadcasted_iota(jnp.int32, tile.shape, 0)
    bias = jnp.where((lane == ROPE) & ~allowed(token), MASKED, 0.0)
    return tile + bias.astype(jnp.bfloat16)


def pack_kernel(
    latent_hbm,
    rope_hbm,
    gain_hbm,
    tables_hbm,
    payload,
    piece,
    latent,
    rope,
    gain,
    table,
    arrived,
):
    rows, width = latent.shape
    ctx, sub = lax.axis_index("ctx"), lax.axis_index("sub")
    copies = [
        pltpu.make_async_copy(source, target, arrived.at[k])
        for k, (source, target) in enumerate(
            [
                (latent_hbm, latent),
                (gain_hbm, gain),
                (rope_hbm, rope),
                (tables_hbm.at[ctx], table),
            ]
        )
    ]
    for copy in copies:
        copy.start()
    for copy in copies:
        copy.wait()
    normed = normalise(latent[...], gain[...])
    extra = last_tile(rope[...], table[...])
    payload[:, :width] = normed
    payload[:, width:] = extra
    size = piece.shape[0]
    for k in range(rows // size):

        @pl.when(sub == k)
        def _():
            piece[:, :width] = normed[k * size : (k + 1) * size]
            piece[:, width:] = extra[k * size : (k + 1) * size]


def mid_kernel(sources, piece_sources, gain, tables, length, *rest):
    count = len(sources)
    latents, ropes, pieces = rest[:count], rest[count : 2 * count], rest[2 * count : -1]
    together = rest[-1]
    ctx, sub = lax.axis_index("ctx"), lax.axis_index("sub")

    def origin(source):
        picked = [
            jnp.where((sub == s) & (ctx == j), i + 1, 0)
            for s, edges in enumerate(source)
            for i, j in edges
        ]
        return sum(picked) - 1

    def allowed(start, there):
        return lambda token: (start + token < length[0]) & there

    at = 0
    for latent, rope, source in zip(latents, ropes, sources, strict=True):
        rows, width = latent.shape
        shard = origin(source)
        start = jnp.maximum(shard, 0)
        together[at : at + rows, :width] = normalise(latent[...], gain[...])
        together[at : at + rows, width:] = masked_tile(
            last_tile(rope[...], tables[start]), allowed(start * rows, shard >= 0)
        )
        at += rows
    for piece, edges in zip(pieces, piece_sources, strict=True):
        size, width = piece.shape[0], piece.shape[1] - WIDE
        cores = lax.axis_size("sub")
        shard = origin([edges] * cores)
        together[at : at + size, :width] = piece[:, :width]
        together[at : at + size, width:] = masked_tile(
            piece[:, width:], allowed((shard * cores + sub) * size, shard >= 0)
        )
        at += size


def grow_kernel(heads, together, weight, full, own, expanded, length, grown, early):
    rows, width = own.shape[0], weight.shape[0]
    columns = NOPE + VDIM
    ctx = lax.axis_index("ctx")

    @pl.when(ctx > 0)
    def _():
        row = lax.broadcasted_iota(jnp.int32, (rows, rows), 0)
        causal = lax.broadcasted_iota(jnp.int32, (rows, rows), 1) <= row
        last_own = masked_tile(own[:, width:], lambda token: ctx * rows + token < length[0])
        last = jnp.concatenate([last_own, together[:rows, width:]], 0)
        for i in range(heads // 2):
            at = slice(2 * columns * i, 2 * columns * (i + 1))
            grown[:, at] = jnp.dot(
                together[:, :width], weight[:, at], preferred_element_type=jnp.float32
            ).astype(jnp.bfloat16)
            if i > 0:
                score_early(i - 1, causal, last, full, expanded, grown, early)
        score_early(heads // 2 - 1, causal, last, full, expanded, grown, early)


def score_early(pair, causal, last, full, expanded, grown, early):
    rows = full.shape[0]
    for h in (2 * pair, 2 * pair + 1):
        at = slice((NOPE + VDIM) * h, (NOPE + VDIM) * h + NOPE)
        keys = jnp.concatenate([expanded[:, at], grown[:rows, at]], 0)
        found = lax.dot_general(
            full[:, FULL * h : FULL * (h + 1)],
            jnp.concatenate([keys, last], 1),
            (((1,), (1,)), ((), ())),
            preferred_element_type=jnp.float32,
        )
        early[h, :, :rows] = jnp.where(causal, found[:, :rows], MASKED)
        early[h, :, rows:] = found[:, rows:]


def own_kernel(heads, queries, payload, weight, tables_hbm, expanded, full, table, arrived):
    copy = pltpu.make_async_copy(tables_hbm.at[lax.axis_index("ctx")], table, arrived)
    copy.start()
    copy.wait()
    rows = queries.shape[0]
    width = weight.shape[0]
    cosines = jnp.concatenate([table[:, :ROPE]] * 2, 1)
    sines = jnp.concatenate([table[:, ROPE:]] * 2, 1)
    lane = lax.broadcasted_iota(jnp.int32, (rows, 2 * ROPE), 1)
    lower = lane % ROPE < ROPE // 2
    tail = (lax.broadcasted_iota(jnp.int32, (rows, FULL - NOPE - ROPE), 1) == 0).astype(
        jnp.float32
    ).astype(jnp.bfloat16)
    each = NOPE + ROPE
    for i in range(heads // 2):
        pair = queries[:, 2 * each * i : 2 * each * (i + 1)]
        ropes = jnp.concatenate([pair[:, NOPE:each], pair[:, each + NOPE :]], 1).astype(jnp.float32)
        turned = jnp.where(
            lower, pltpu.roll(ropes, 2 * ROPE - ROPE // 2, 1), pltpu.roll(ropes, ROPE // 2, 1)
        )
        ropes = (ropes * cosines + turned * sines).astype(jnp.bfloat16)
        for e in range(2):
            at = FULL * (2 * i + e)
            full[:, at : at + NOPE] = pair[:, each * e : each * e + NOPE]
            full[:, at + NOPE : at + FULL] = jnp.concatenate(
                [ropes[:, ROPE * e : ROPE * (e + 1)], tail], 1
            )
    columns = NOPE + VDIM
    for i in range(heads // 2):
        at = slice(2 * columns * i, 2 * columns * (i + 1))
        expanded[:, at] = jnp.dot(
            payload[:, :width], weight[:, at], preferred_element_type=jnp.float32
        ).astype(jnp.bfloat16)


def attend_kernel(heads, sets, levels, full, own, expanded, weight, together, fetched, early, *rest):
    swapped = rest[:-8]
    length, out_hbm, last_own, grown, scores, weights, out, sent = rest[-8:]
    rows = full.shape[0]
    width = weight.shape[0]
    columns = NOPE + VDIM
    ctx = lax.axis_index("ctx")
    row = lax.broadcasted_iota(jnp.int32, (rows, rows), 0)
    causal = lax.broadcasted_iota(jnp.int32, (rows, rows), 1) <= row
    live = ctx * rows + lax.broadcasted_iota(jnp.int32, (rows, 1), 0) < length[0]
    last_own[...] = masked_tile(own[:, width:], lambda token: ctx * rows + token < length[0])
    stage, buffers = 2, 4
    block = VDIM * heads // OUT_COPIES

    def leave(k):
        at = pl.ds(k * block, block)
        return pltpu.make_async_copy(out.at[:, at], out_hbm.at[:, at], sent.at[k])

    def run(used, high):
        every = together.shape[0]
        both = ((0, sets), (sets, every))
        spans = [span for span, use in zip(both, used, strict=True) if use]
        extent = slice(spans[0][0], spans[-1][1]) if spans else slice(0, 0)
        total = rows + sum(end - begin for begin, end in spans) * (1 + len(swapped))

        def rows_of(own_part, direct_part, swapped_part):
            found = [own_part()]
            for begin, end in spans:
                found.append(direct_part(slice(begin, end)))
                for r in range(len(swapped)):
                    found.append(swapped_part(r, slice(begin, end)))
            return found[0] if len(found) == 1 else jnp.concatenate(found, 0)

        def grow(i):
            at = slice(2 * columns * i, 2 * columns * (i + 1))
            for r, ref in enumerate(swapped):
                if spans:
                    grown[i % 4, r, extent] = jnp.dot(
                        ref[extent, :width], weight[:, at], preferred_element_type=jnp.float32
                    ).astype(jnp.bfloat16)

        known = 2 * rows if used[0] else 0

        def column(h, begin, end):
            i, e = divmod(h, 2)
            return rows_of(
                lambda: expanded[:, columns * h + begin : columns * h + end],
                lambda piece: fetched[piece, columns * h + begin : columns * h + end],
                lambda r, piece: grown[i % 4, r, piece, columns * e + begin : columns * e + end],
            )

        def score(h):
            last = rows_of(
                lambda: last_own[...],
                lambda piece: together[piece, width:],
                lambda r, piece: swapped[r][piece, width:],
            )
            found = lax.dot_general(
                full[:high, FULL * h : FULL * (h + 1)],
                jnp.concatenate([column(h, 0, NOPE)[known:], last[known:]], 1),
                (((1,), (1,)), ((), ())),
                preferred_element_type=jnp.float32,
            )
            if known:
                scores[h % buffers, :high, known:total] = found
                return
            scores[h % buffers, :high, :rows] = jnp.where(causal[:high], found[:, :rows], MASKED)
            if total > rows:
                scores[h % buffers, :high, rows:total] = found[:, rows:]

        def soften(h):
            found = scores[h % buffers, :high, known:total]
            if known:
                found = jnp.concatenate([early[h, :high], found], 1)
            top = jnp.max(found, 1, keepdims=True)
            raw = jnp.exp2(found * EXPONENT - top * EXPONENT)
            weights[h % buffers, :high, :total] = raw.astype(jnp.bfloat16)
            return jnp.sum(raw, 1, keepdims=True)

        def mix(h, total_h):
            mixed = jnp.dot(
                weights[h % buffers, :high, :total],
                column(h, NOPE, columns),
                preferred_element_type=jnp.float32,
            )
            at = slice(VDIM * h, VDIM * (h + 1))
            out[:high, at] = jnp.where(live[:high], mixed / total_h, 0.0).astype(jnp.bfloat16)
            if high < rows:
                out[high:, at] = jnp.zeros((rows - high, VDIM), jnp.bfloat16)
            if (h + 1) % (heads // OUT_COPIES) == 0:
                leave(h // (heads // OUT_COPIES)).start()

        totals = {}
        steps = heads // stage
        grow(0)
        for t in range(steps + 2):
            if t + 1 < heads // 2:
                grow(t + 1)
            for h in range(stage * t, stage * (t + 1)):
                if t < steps:
                    score(h)
            for h in range(stage * (t - 1), stage * t):
                if 0 <= t - 1 < steps:
                    totals[h] = soften(h)
            for h in range(stage * (t - 2), stage * (t - 1)):
                if 0 <= t - 2 < steps:
                    mix(h, totals.pop(h))

    left = length[0] - ctx * rows

    @pl.when(left <= 0)
    def _():
        out[...] = jnp.zeros_like(out)
        for k in range(OUT_COPIES):
            leave(k).start()

    for used, places in levels:
        here = functools.reduce(jnp.logical_or, [ctx == c for c in places])
        bounds = [0, rows // 2, rows] if all(used) else [0, rows]
        for low, high in zip(bounds[:-1], bounds[1:], strict=True):
            fits = (left > low) if high == rows else (left > low) & (left <= high)

            @pl.when(here & fits)
            def _():
                run(used, high)

    for k in range(OUT_COPIES):
        leave(k).wait()


def plan(shards, cores):
    colours = []
    for distance in range(shards - 1, 0, -1):
        for source in range(shards - distance):
            target = source + distance
            for colour in colours:
                if all(source != i and target != j for i, j in colour):
                    colour.append((source, target))
                    break
            else:
                colours.append([(source, target)])
    whole = len(colours) // cores * cores
    sets = [colours[k : k + cores] for k in range(0, whole, cores)]
    return sets, colours[whole:]


def in_hbm(x):
    return pltpu.with_memory_space_constraint(x, pltpu.HBM)


def grant(*arrays):
    return pltpu.CompilerParams(vmem_limit_bytes=4 * MIB + 2 * sum(x.size for x in arrays))


def per_device(
    ctx_size, sub_size, queries, latent, rope_keys, latent_gain, up_weight, prompt_length
):
    rows, width = latent.shape
    heads = up_weight.shape[1] // (NOPE + VDIM)
    by_row, by_column = tables(ctx_size * rows)
    by_row = jnp.asarray(by_row.reshape(ctx_size, rows, 2 * ROPE))
    by_column = jnp.asarray(by_column.reshape(ROPE, ctx_size, rows).transpose(1, 0, 2))
    gain = latent_gain.reshape(1, width)
    turned = rope_keys.T
    bf16 = jnp.bfloat16
    wide = width + WIDE

    cores = ("ctx", "sub")
    sets, rest = plan(ctx_size, sub_size)

    def send(data, by_core):
        pairs = [
            (i * sub_size + s, j * sub_size + s) for s, edges in enumerate(by_core) for i, j in edges
        ]
        return lax.ppermute(data, cores, pairs)

    latents = [send(latent, by_core) for by_core in sets]
    ropes = [send(turned, by_core) for by_core in sets]

    payload, piece = pl.pallas_call(
        pack_kernel,
        in_specs=[HBM] * 4,
        out_specs=[VMEM] * 2,
        out_shape=[
            jax.ShapeDtypeStruct((rows, wide), bf16),
            jax.ShapeDtypeStruct((rows // sub_size, wide), bf16),
        ],
        scratch_shapes=[
            pltpu.VMEM((rows, width), bf16),
            pltpu.VMEM((ROPE, rows), bf16),
            pltpu.VMEM((1, width), jnp.float32),
            pltpu.VMEM((ROPE, rows), jnp.float32),
            pltpu.SemaphoreType.DMA((4,)),
        ],
        cost_estimate=pl.CostEstimate(
            flops=PACK_FLOPS, bytes_accessed=8 * rows * width, transcendentals=0
        ),
        compiler_params=grant(),
        name="pack",
    )(in_hbm(latent), in_hbm(turned), in_hbm(gain), in_hbm(by_column))

    pieces = [send(piece, [edges] * sub_size) for edges in rest]

    expanded, full = pl.pallas_call(
        functools.partial(own_kernel, heads),
        in_specs=[VMEM] * 3 + [ANY],
        out_specs=[VMEM] * 2,
        out_shape=[
            jax.ShapeDtypeStruct((rows, up_weight.shape[1]), bf16),
            jax.ShapeDtypeStruct((rows, heads * FULL), bf16),
        ],
        scratch_shapes=[pltpu.VMEM((rows, 2 * ROPE), jnp.float32), pltpu.SemaphoreType.DMA],
        compiler_params=grant(queries, up_weight, payload, up_weight[:rows], up_weight[:rows]),
        name="own",
        cost_estimate=pl.CostEstimate(
            flops=2 * rows * width * up_weight.shape[1],
            bytes_accessed=2 * (queries.size + up_weight.size + 2 * rows * up_weight.shape[1]),
            transcendentals=0,
        ),
    )(queries, payload, up_weight, by_row)

    expanded, prompt_length = lax.optimization_barrier((expanded, prompt_length))
    latents, ropes, pieces, expanded, full = lax.optimization_barrier(
        (latents, ropes, pieces, expanded, full)
    )
    reach = sum(x.shape[0] for x in (*latents, *pieces))
    whole = sum(x.shape[0] for x in latents)
    together = pl.pallas_call(
        functools.partial(mid_kernel, sets, rest),
        in_specs=[VMEM] * 2 + [SMEM] + [VMEM] * (2 * len(latents) + len(pieces)),
        out_specs=VMEM,
        out_shape=jax.ShapeDtypeStruct((reach, wide), bf16),
        compiler_params=grant(by_column, by_column, *latents, *ropes, *pieces, *pieces, *latents),
        name="mid",
    )(gain, by_column, prompt_length, *latents, *ropes, *pieces)

    swapped = []
    for r in range(1, sub_size):
        pairs = [(s, (s + r) % sub_size) for s in range(sub_size)]
        swapped.append(lax.ppermute(together, "sub", pairs))

    fetched, early = pl.pallas_call(
        functools.partial(grow_kernel, heads),
        in_specs=[VMEM] * 5 + [SMEM],
        out_specs=[VMEM] * 2,
        out_shape=[
            jax.ShapeDtypeStruct((reach, up_weight.shape[1]), bf16),
            jax.ShapeDtypeStruct((heads, rows, 2 * rows), jnp.float32),
        ],
        compiler_params=pltpu.CompilerParams(
            vmem_limit_bytes=4 * MIB
            + 2 * (up_weight.size + reach * (wide + up_weight.shape[1]))
            + 2 * (full.size + expanded.size + payload.size)
            + 8 * heads * rows * rows
        ),
        name="grow",
        cost_estimate=pl.CostEstimate(
            flops=2 * reach * width * up_weight.shape[1],
            bytes_accessed=2 * (up_weight.size + reach * up_weight.shape[1]),
            transcendentals=0,
        ),
    )(together, up_weight, full, payload, expanded, prompt_length)

    parts = [[e for by_core in sets for e in by_core], rest]
    needs = [
        tuple(any(j == c for edges in part for _, j in edges) for part in parts)
        for c in range(ctx_size)
    ]
    levels = [(u, [c for c in range(ctx_size) if needs[c] == u]) for u in sorted(set(needs))]
    total = rows + sub_size * reach
    held = 8 * heads * rows * rows + 2 * (up_weight.size + (reach + 2 * rows) * up_weight.shape[1] + total * wide)
    scratch = 8 * total * (NOPE + VDIM) * 2 + 24 * rows * total + 2 * rows * heads * VDIM
    return pl.pallas_call(
        functools.partial(attend_kernel, heads, whole, levels),
        in_specs=[VMEM] * (7 + len(swapped)) + [SMEM],
        out_specs=ANY,
        out_shape=jax.ShapeDtypeStruct((rows, heads * VDIM), bf16),
        scratch_shapes=[
            pltpu.VMEM((rows, WIDE), bf16),
            pltpu.VMEM((4, len(swapped), reach, 2 * (NOPE + VDIM)), bf16),
            pltpu.VMEM((4, rows, total), jnp.float32),
            pltpu.VMEM((4, rows, total), bf16),
            pltpu.VMEM((rows, heads * VDIM), bf16),
            pltpu.SemaphoreType.DMA((OUT_COPIES,)),
        ],
        compiler_params=pltpu.CompilerParams(vmem_limit_bytes=6 * MIB + held + scratch),
        name="attend",
        cost_estimate=pl.CostEstimate(
            flops=2 * total * (width + 2 * rows) * up_weight.shape[1],
            bytes_accessed=2 * (up_weight.size + 3 * rows * up_weight.shape[1]),
            transcendentals=heads * rows * total,
        ),
    )(full, payload, expanded, up_weight, together, fetched, early, *swapped, prompt_length)


def solution(mesh):
    placed = (
        P(("parts", "ctx"), ("head", "sub")),
        P(("parts", "ctx"), None),
        P(("parts", "ctx"), None),
        P(),
        P(None, ("head", "sub")),
        P("parts"),
    )
    step = jax.shard_map(
        functools.partial(per_device, mesh.shape["ctx"], mesh.shape["sub"]),
        mesh=mesh,
        in_specs=placed,
        out_specs=P(("parts", "ctx"), ("head", "sub")),
        check_vma=False,
    )
    if len(plan(mesh.shape["ctx"], mesh.shape["sub"])[0]) > 1:
        return step
    return step
```

```python
import functools
import math

import jax
import jax.numpy as jnp
import numpy as np
from jax import lax
from jax.experimental import pallas as pl
from jax.experimental.pallas import tpu as pltpu
from jax.sharding import PartitionSpec as P

ROPE = 64
NOPE = 128
VDIM = 128
WIDE = 128
FULL = 256
MASKED = -1e30
MIB = 1024 * 1024
PACK_FLOPS = 4 * 10**9
OUT_COPIES = 4
EXPONENT = math.log2(math.e) / math.sqrt(NOPE + ROPE)

VMEM = pl.BlockSpec(memory_space=pltpu.VMEM)
SMEM = pl.BlockSpec(memory_space=pltpu.SMEM)
HBM = pl.BlockSpec(memory_space=pltpu.HBM)
ANY = pl.BlockSpec(memory_space=pl.ANY)


def tables(positions):
    half = ROPE // 2
    frequency = np.float32(10000.0) ** (-np.arange(half, dtype=np.float32) / np.float32(half))
    angles = np.arange(positions, dtype=np.float32)[:, None] * frequency.astype(np.float32)
    cosines, sines = np.cos(angles), np.sin(angles)
    rows = np.concatenate([cosines, cosines, -sines, sines], 1).astype(np.float32)
    columns = np.concatenate([cosines, sines], 1).T.astype(np.float32)
    return rows, np.ascontiguousarray(columns)


def normalise(latent, gain):
    wide = latent.astype(jnp.float32)
    mean = jnp.mean(wide * wide, -1, keepdims=True)
    return (wide * lax.rsqrt(mean + 1e-06) * gain).astype(jnp.bfloat16)


def last_tile(rope, table):
    half = ROPE // 2
    keys = rope.astype(jnp.float32)
    low, high = keys[:half], keys[half:]
    cosines, sines = table[:half], table[half:]
    zeros = jnp.zeros((WIDE - ROPE, rope.shape[1]), jnp.float32)
    rotated = [low * cosines - high * sines, low * sines + high * cosines, zeros]
    return jnp.concatenate(rotated, 0).T.astype(jnp.bfloat16)


def masked_tile(tile, allowed):
    lane = lax.broadcasted_iota(jnp.int32, tile.shape, 1)
    token = lax.broadcasted_iota(jnp.int32, tile.shape, 0)
    bias = jnp.where((lane == ROPE) & ~allowed(token), MASKED, 0.0)
    return tile + bias.astype(jnp.bfloat16)


def pack_kernel(
    latent_hbm,
    rope_hbm,
    gain_hbm,
    tables_hbm,
    payload,
    piece,
    latent,
    rope,
    gain,
    table,
    arrived,
):
    rows, width = latent.shape
    ctx, sub = lax.axis_index("ctx"), lax.axis_index("sub")
    copies = [
        pltpu.make_async_copy(source, target, arrived.at[k])
        for k, (source, target) in enumerate(
            [
                (latent_hbm, latent),
                (gain_hbm, gain),
                (rope_hbm, rope),
                (tables_hbm.at[ctx], table),
            ]
        )
    ]
    for copy in copies:
        copy.start()
    for copy in copies:
        copy.wait()
    normed = normalise(latent[...], gain[...])
    extra = last_tile(rope[...], table[...])
    payload[:, :width] = normed
    payload[:, width:] = extra
    size = piece.shape[0]
    for k in range(rows // size):

        @pl.when(sub == k)
        def _():
            piece[:, :width] = normed[k * size : (k + 1) * size]
            piece[:, width:] = extra[k * size : (k + 1) * size]


def mid_kernel(sources, piece_sources, gain, tables, length, *rest):
    count = len(sources)
    latents, ropes, pieces = rest[:count], rest[count : 2 * count], rest[2 * count : -1]
    together = rest[-1]
    ctx, sub = lax.axis_index("ctx"), lax.axis_index("sub")

    def origin(source):
        picked = [
            jnp.where((sub == s) & (ctx == j), i + 1, 0)
            for s, edges in enumerate(source)
            for i, j in edges
        ]
        return sum(picked) - 1

    def allowed(start, there):
        return lambda token: (start + token < length[0]) & there

    at = 0
    for latent, rope, source in zip(latents, ropes, sources, strict=True):
        rows, width = latent.shape
        shard = origin(source)
        start = jnp.maximum(shard, 0)
        together[at : at + rows, :width] = normalise(latent[...], gain[...])
        together[at : at + rows, width:] = masked_tile(
            last_tile(rope[...], tables[start]), allowed(start * rows, shard >= 0)
        )
        at += rows
    for piece, edges in zip(pieces, piece_sources, strict=True):
        size, width = piece.shape[0], piece.shape[1] - WIDE
        cores = lax.axis_size("sub")
        shard = origin([edges] * cores)
        together[at : at + size, :width] = piece[:, :width]
        together[at : at + size, width:] = masked_tile(
            piece[:, width:], allowed((shard * cores + sub) * size, shard >= 0)
        )
        at += size


def grow_kernel(heads, takers, together, weight, full, own, expanded, length, grown, early):
    rows, width = own.shape[0], weight.shape[0]
    columns = NOPE + VDIM
    ctx = lax.axis_index("ctx")
    takes = functools.reduce(jnp.logical_or, [ctx == c for c in takers], ctx < 0)

    def run(scored):
        row = lax.broadcasted_iota(jnp.int32, (rows, rows), 0)
        causal = lax.broadcasted_iota(jnp.int32, (rows, rows), 1) <= row
        last_own = masked_tile(own[:, width:], lambda token: ctx * rows + token < length[0])
        last = jnp.concatenate([last_own, together[:rows, width:]], 0)
        for i in range(heads // 2 + 1):
            if i < heads // 2:
                at = slice(2 * columns * i, 2 * columns * (i + 1))
                grown[:, at] = jnp.dot(
                    together[:, :width], weight[:, at], preferred_element_type=jnp.float32
                ).astype(jnp.bfloat16)
            if scored and i > 0:
                score_early(i - 1, causal, last, full, expanded, grown, early)

    @pl.when(takes)
    def _():
        run(True)

    @pl.when((ctx > 0) & ~takes)
    def _():
        run(False)


def score_early(pair, causal, last, full, expanded, grown, early):
    rows = full.shape[0]
    for h in (2 * pair, 2 * pair + 1):
        at = slice((NOPE + VDIM) * h, (NOPE + VDIM) * h + NOPE)
        keys = jnp.concatenate([expanded[:, at], grown[:rows, at]], 0)
        found = lax.dot_general(
            full[:, FULL * h : FULL * (h + 1)],
            jnp.concatenate([keys, last], 1),
            (((1,), (1,)), ((), ())),
            preferred_element_type=jnp.float32,
        )
        early[h, :, :rows] = jnp.where(causal, found[:, :rows], MASKED)
        early[h, :, rows:] = found[:, rows:]


def own_kernel(heads, queries, payload, weight, tables_hbm, expanded, full, table, arrived):
    copy = pltpu.make_async_copy(tables_hbm.at[lax.axis_index("ctx")], table, arrived)
    copy.start()
    copy.wait()
    rows = queries.shape[0]
    width = weight.shape[0]
    cosines = jnp.concatenate([table[:, :ROPE]] * 2, 1)
    sines = jnp.concatenate([table[:, ROPE:]] * 2, 1)
    lane = lax.broadcasted_iota(jnp.int32, (rows, 2 * ROPE), 1)
    lower = lane % ROPE < ROPE // 2
    tail = (lax.broadcasted_iota(jnp.int32, (rows, FULL - NOPE - ROPE), 1) == 0).astype(
        jnp.float32
    ).astype(jnp.bfloat16)
    each = NOPE + ROPE
    for i in range(heads // 2):
        pair = queries[:, 2 * each * i : 2 * each * (i + 1)]
        ropes = jnp.concatenate([pair[:, NOPE:each], pair[:, each + NOPE :]], 1).astype(jnp.float32)
        turned = jnp.where(
            lower, pltpu.roll(ropes, 2 * ROPE - ROPE // 2, 1), pltpu.roll(ropes, ROPE // 2, 1)
        )
        ropes = (ropes * cosines + turned * sines).astype(jnp.bfloat16)
        for e in range(2):
            at = FULL * (2 * i + e)
            full[:, at : at + NOPE] = pair[:, each * e : each * e + NOPE]
            full[:, at + NOPE : at + FULL] = jnp.concatenate(
                [ropes[:, ROPE * e : ROPE * (e + 1)], tail], 1
            )
    columns = NOPE + VDIM
    for i in range(heads // 2):
        at = slice(2 * columns * i, 2 * columns * (i + 1))
        expanded[:, at] = jnp.dot(
            payload[:, :width], weight[:, at], preferred_element_type=jnp.float32
        ).astype(jnp.bfloat16)


def attend_kernel(heads, sets, levels, full, own, expanded, weight, together, fetched, early, *rest):
    swapped = rest[:-8]
    length, out_hbm, last_own, grown, scores, weights, out, sent = rest[-8:]
    rows = full.shape[0]
    width = weight.shape[0]
    columns = NOPE + VDIM
    ctx = lax.axis_index("ctx")
    row = lax.broadcasted_iota(jnp.int32, (rows, rows), 0)
    causal = lax.broadcasted_iota(jnp.int32, (rows, rows), 1) <= row
    live = ctx * rows + lax.broadcasted_iota(jnp.int32, (rows, 1), 0) < length[0]
    last_own[...] = masked_tile(own[:, width:], lambda token: ctx * rows + token < length[0])
    stage, buffers = 2, 4
    block = VDIM * heads // OUT_COPIES

    def leave(k):
        at = pl.ds(k * block, block)
        return pltpu.make_async_copy(out.at[:, at], out_hbm.at[:, at], sent.at[k])

    def run(used, high):
        every = together.shape[0]
        both = ((0, sets), (sets, every))
        spans = [span for span, use in zip(both, used, strict=True) if use]
        extent = slice(spans[0][0], spans[-1][1]) if spans else slice(0, 0)
        total = rows + sum(end - begin for begin, end in spans) * (1 + len(swapped))

        def rows_of(own_part, direct_part, swapped_part):
            found = [own_part()]
            for begin, end in spans:
                found.append(direct_part(slice(begin, end)))
                for r in range(len(swapped)):
                    found.append(swapped_part(r, slice(begin, end)))
            return found[0] if len(found) == 1 else jnp.concatenate(found, 0)

        def grow(i):
            at = slice(2 * columns * i, 2 * columns * (i + 1))
            for r, ref in enumerate(swapped):
                if spans:
                    grown[i % 4, r, extent] = jnp.dot(
                        ref[extent, :width], weight[:, at], preferred_element_type=jnp.float32
                    ).astype(jnp.bfloat16)

        known = 2 * rows if used[0] else 0

        def column(h, begin, end):
            i, e = divmod(h, 2)
            return rows_of(
                lambda: expanded[:, columns * h + begin : columns * h + end],
                lambda piece: fetched[piece, columns * h + begin : columns * h + end],
                lambda r, piece: grown[i % 4, r, piece, columns * e + begin : columns * e + end],
            )

        def score(h):
            last = rows_of(
                lambda: last_own[...],
                lambda piece: together[piece, width:],
                lambda r, piece: swapped[r][piece, width:],
            )
            found = lax.dot_general(
                full[:high, FULL * h : FULL * (h + 1)],
                jnp.concatenate([column(h, 0, NOPE)[known:], last[known:]], 1),
                (((1,), (1,)), ((), ())),
                preferred_element_type=jnp.float32,
            )
            if known:
                scores[h % buffers, :high, known:total] = found
                return
            scores[h % buffers, :high, :rows] = jnp.where(causal[:high], found[:, :rows], MASKED)
            if total > rows:
                scores[h % buffers, :high, rows:total] = found[:, rows:]

        def soften(h):
            found = scores[h % buffers, :high, known:total]
            if known:
                found = jnp.concatenate([early[h, :high], found], 1)
            top = jnp.max(found, 1, keepdims=True)
            raw = jnp.exp2(found * EXPONENT - top * EXPONENT)
            weights[h % buffers, :high, :total] = raw.astype(jnp.bfloat16)
            return jnp.sum(raw, 1, keepdims=True)

        def mix(h, total_h):
            mixed = jnp.dot(
                weights[h % buffers, :high, :total],
                column(h, NOPE, columns),
                preferred_element_type=jnp.float32,
            )
            at = slice(VDIM * h, VDIM * (h + 1))
            out[:high, at] = jnp.where(live[:high], mixed / total_h, 0.0).astype(jnp.bfloat16)
            if high < rows:
                out[high:, at] = jnp.zeros((rows - high, VDIM), jnp.bfloat16)
            if (h + 1) % (heads // OUT_COPIES) == 0:
                leave(h // (heads // OUT_COPIES)).start()

        totals = {}
        steps = heads // stage
        grow(0)
        for t in range(steps + 2):
            if t + 1 < heads // 2:
                grow(t + 1)
            for h in range(stage * t, stage * (t + 1)):
                if t < steps:
                    score(h)
            for h in range(stage * (t - 1), stage * t):
                if 0 <= t - 1 < steps:
                    totals[h] = soften(h)
            for h in range(stage * (t - 2), stage * (t - 1)):
                if 0 <= t - 2 < steps:
                    mix(h, totals.pop(h))

    left = length[0] - ctx * rows

    @pl.when(left <= 0)
    def _():
        out[...] = jnp.zeros_like(out)
        for k in range(OUT_COPIES):
            leave(k).start()

    for used, places in levels:
        here = functools.reduce(jnp.logical_or, [ctx == c for c in places])
        bounds = [0, rows // 2, rows] if all(used) else [0, rows]
        for low, high in zip(bounds[:-1], bounds[1:], strict=True):
            fits = (left > low) if high == rows else (left > low) & (left <= high)

            @pl.when(here & fits)
            def _():
                run(used, high)

    for k in range(OUT_COPIES):
        leave(k).wait()


def plan(shards, cores):
    colours = []
    for distance in range(shards - 1, 0, -1):
        for source in range(shards - distance):
            target = source + distance
            for colour in colours:
                if all(source != i and target != j for i, j in colour):
                    colour.append((source, target))
                    break
            else:
                colours.append([(source, target)])
    whole = len(colours) // cores * cores
    sets = [colours[k : k + cores] for k in range(0, whole, cores)]
    return sets, colours[whole:]


def in_hbm(x):
    return pltpu.with_memory_space_constraint(x, pltpu.HBM)


def grant(*arrays):
    return pltpu.CompilerParams(vmem_limit_bytes=4 * MIB + 2 * sum(x.size for x in arrays))


def per_device(
    ctx_size, sub_size, queries, latent, rope_keys, latent_gain, up_weight, prompt_length
):
    rows, width = latent.shape
    heads = up_weight.shape[1] // (NOPE + VDIM)
    by_row, by_column = tables(ctx_size * rows)
    by_row = jnp.asarray(by_row.reshape(ctx_size, rows, 2 * ROPE))
    by_column = jnp.asarray(by_column.reshape(ROPE, ctx_size, rows).transpose(1, 0, 2))
    gain = latent_gain.reshape(1, width)
    turned = rope_keys.T
    bf16 = jnp.bfloat16
    wide = width + WIDE

    cores = ("ctx", "sub")
    sets, rest = plan(ctx_size, sub_size)

    def send(data, by_core):
        pairs = [
            (i * sub_size + s, j * sub_size + s) for s, edges in enumerate(by_core) for i, j in edges
        ]
        return lax.ppermute(data, cores, pairs)

    latents = [send(latent, by_core) for by_core in sets]
    ropes = [send(turned, by_core) for by_core in sets]

    payload, piece = pl.pallas_call(
        pack_kernel,
        in_specs=[HBM] * 4,
        out_specs=[VMEM] * 2,
        out_shape=[
            jax.ShapeDtypeStruct((rows, wide), bf16),
            jax.ShapeDtypeStruct((rows // sub_size, wide), bf16),
        ],
        scratch_shapes=[
            pltpu.VMEM((rows, width), bf16),
            pltpu.VMEM((ROPE, rows), bf16),
            pltpu.VMEM((1, width), jnp.float32),
            pltpu.VMEM((ROPE, rows), jnp.float32),
            pltpu.SemaphoreType.DMA((4,)),
        ],
        cost_estimate=pl.CostEstimate(
            flops=PACK_FLOPS, bytes_accessed=8 * rows * width, transcendentals=0
        ),
        compiler_params=grant(),
        name="pack",
    )(in_hbm(latent), in_hbm(turned), in_hbm(gain), in_hbm(by_column))

    pieces = [send(piece, [edges] * sub_size) for edges in rest]

    expanded, full = pl.pallas_call(
        functools.partial(own_kernel, heads),
        in_specs=[VMEM] * 3 + [ANY],
        out_specs=[VMEM] * 2,
        out_shape=[
            jax.ShapeDtypeStruct((rows, up_weight.shape[1]), bf16),
            jax.ShapeDtypeStruct((rows, heads * FULL), bf16),
        ],
        scratch_shapes=[pltpu.VMEM((rows, 2 * ROPE), jnp.float32), pltpu.SemaphoreType.DMA],
        compiler_params=grant(queries, up_weight, payload, up_weight[:rows], up_weight[:rows]),
        name="own",
        cost_estimate=pl.CostEstimate(
            flops=2 * rows * width * up_weight.shape[1],
            bytes_accessed=2 * (queries.size + up_weight.size + 2 * rows * up_weight.shape[1]),
            transcendentals=0,
        ),
    )(queries, payload, up_weight, by_row)

    expanded, prompt_length = lax.optimization_barrier((expanded, prompt_length))
    latents, ropes, pieces, expanded, full = lax.optimization_barrier(
        (latents, ropes, pieces, expanded, full)
    )
    reach = sum(x.shape[0] for x in (*latents, *pieces))
    whole = sum(x.shape[0] for x in latents)
    together = pl.pallas_call(
        functools.partial(mid_kernel, sets, rest),
        in_specs=[VMEM] * 2 + [SMEM] + [VMEM] * (2 * len(latents) + len(pieces)),
        out_specs=VMEM,
        out_shape=jax.ShapeDtypeStruct((reach, wide), bf16),
        compiler_params=grant(by_column, by_column, *latents, *ropes, *pieces, *pieces, *latents),
        name="mid",
    )(gain, by_column, prompt_length, *latents, *ropes, *pieces)

    swapped = []
    for r in range(1, sub_size):
        pairs = [(s, (s + r) % sub_size) for s in range(sub_size)]
        swapped.append(lax.ppermute(together, "sub", pairs))

    parts = [[e for by_core in sets for e in by_core], rest]
    needs = [
        tuple(any(j == c for edges in part for _, j in edges) for part in parts)
        for c in range(ctx_size)
    ]
    levels = [(u, [c for c in range(ctx_size) if needs[c] == u]) for u in sorted(set(needs))]
    takers = [c for c in range(ctx_size) if needs[c][0]]
    fetched, early = pl.pallas_call(
        functools.partial(grow_kernel, heads, takers),
        in_specs=[VMEM] * 5 + [SMEM],
        out_specs=[VMEM] * 2,
        out_shape=[
            jax.ShapeDtypeStruct((reach, up_weight.shape[1]), bf16),
            jax.ShapeDtypeStruct((heads, rows, 2 * rows), jnp.float32),
        ],
        compiler_params=pltpu.CompilerParams(
            vmem_limit_bytes=4 * MIB
            + 2 * (up_weight.size + reach * (wide + up_weight.shape[1]))
            + 2 * (full.size + expanded.size + payload.size)
            + 8 * heads * rows * rows
        ),
        name="grow",
        cost_estimate=pl.CostEstimate(
            flops=2 * reach * width * up_weight.shape[1],
            bytes_accessed=2 * (up_weight.size + reach * up_weight.shape[1]),
            transcendentals=0,
        ),
    )(together, up_weight, full, payload, expanded, prompt_length)

    total = rows + sub_size * reach
    held = 8 * heads * rows * rows + 2 * (up_weight.size + (reach + 2 * rows) * up_weight.shape[1] + total * wide)
    scratch = 8 * total * (NOPE + VDIM) * 2 + 24 * rows * total + 2 * rows * heads * VDIM
    return pl.pallas_call(
        functools.partial(attend_kernel, heads, whole, levels),
        in_specs=[VMEM] * (7 + len(swapped)) + [SMEM],
        out_specs=ANY,
        out_shape=jax.ShapeDtypeStruct((rows, heads * VDIM), bf16),
        scratch_shapes=[
            pltpu.VMEM((rows, WIDE), bf16),
            pltpu.VMEM((4, len(swapped), reach, 2 * (NOPE + VDIM)), bf16),
            pltpu.VMEM((4, rows, total), jnp.float32),
            pltpu.VMEM((4, rows, total), bf16),
            pltpu.VMEM((rows, heads * VDIM), bf16),
            pltpu.SemaphoreType.DMA((OUT_COPIES,)),
        ],
        compiler_params=pltpu.CompilerParams(vmem_limit_bytes=6 * MIB + held + scratch),
        name="attend",
        cost_estimate=pl.CostEstimate(
            flops=2 * total * (width + 2 * rows) * up_weight.shape[1],
            bytes_accessed=2 * (up_weight.size + 3 * rows * up_weight.shape[1]),
            transcendentals=heads * rows * total,
        ),
    )(full, payload, expanded, up_weight, together, fetched, early, *swapped, prompt_length)


def solution(mesh):
    placed = (
        P(("parts", "ctx"), ("head", "sub")),
        P(("parts", "ctx"), None),
        P(("parts", "ctx"), None),
        P(),
        P(None, ("head", "sub")),
        P("parts"),
    )
    step = jax.shard_map(
        functools.partial(per_device, mesh.shape["ctx"], mesh.shape["sub"]),
        mesh=mesh,
        in_specs=placed,
        out_specs=P(("parts", "ctx"), ("head", "sub")),
        check_vma=False,
    )
    if len(plan(mesh.shape["ctx"], mesh.shape["sub"])[0]) > 1:
        return step
    return step
```

```python
import functools
import math

import jax
import jax.numpy as jnp
import numpy as np
from jax import lax
from jax.experimental import pallas as pl
from jax.experimental.pallas import tpu as pltpu
from jax.sharding import PartitionSpec as P

ROPE = 64
NOPE = 128
VDIM = 128
WIDE = 128
FULL = 256
MASKED = -1e30
MIB = 1024 * 1024
PACK_FLOPS = 4 * 10**9
OUT_COPIES = 4
EXPONENT = math.log2(math.e) / math.sqrt(NOPE + ROPE)

VMEM = pl.BlockSpec(memory_space=pltpu.VMEM)
SMEM = pl.BlockSpec(memory_space=pltpu.SMEM)
HBM = pl.BlockSpec(memory_space=pltpu.HBM)
ANY = pl.BlockSpec(memory_space=pl.ANY)


def tables(positions):
    half = ROPE // 2
    frequency = np.float32(10000.0) ** (-np.arange(half, dtype=np.float32) / np.float32(half))
    angles = np.arange(positions, dtype=np.float32)[:, None] * frequency.astype(np.float32)
    cosines, sines = np.cos(angles), np.sin(angles)
    rows = np.concatenate([cosines, cosines, -sines, sines], 1).astype(np.float32)
    columns = np.concatenate([cosines, sines], 1).T.astype(np.float32)
    return rows, np.ascontiguousarray(columns)


def normalise(latent, gain):
    wide = latent.astype(jnp.float32)
    mean = jnp.mean(wide * wide, -1, keepdims=True)
    return (wide * lax.rsqrt(mean + 1e-06) * gain).astype(jnp.bfloat16)


def last_tile(rope, table):
    half = ROPE // 2
    keys = rope.astype(jnp.float32)
    low, high = keys[:half], keys[half:]
    cosines, sines = table[:half], table[half:]
    zeros = jnp.zeros((WIDE - ROPE, rope.shape[1]), jnp.float32)
    rotated = [low * cosines - high * sines, low * sines + high * cosines, zeros]
    return jnp.concatenate(rotated, 0).T.astype(jnp.bfloat16)


def masked_tile(tile, allowed):
    lane = lax.broadcasted_iota(jnp.int32, tile.shape, 1)
    token = lax.broadcasted_iota(jnp.int32, tile.shape, 0)
    bias = jnp.where((lane == ROPE) & ~allowed(token), MASKED, 0.0)
    return tile + bias.astype(jnp.bfloat16)


def pack_kernel(
    latent_hbm,
    rope_hbm,
    gain_hbm,
    tables_hbm,
    payload,
    piece,
    latent,
    rope,
    gain,
    table,
    arrived,
):
    rows, width = latent.shape
    ctx, sub = lax.axis_index("ctx"), lax.axis_index("sub")
    copies = [
        pltpu.make_async_copy(source, target, arrived.at[k])
        for k, (source, target) in enumerate(
            [
                (latent_hbm, latent),
                (gain_hbm, gain),
                (rope_hbm, rope),
                (tables_hbm.at[ctx], table),
            ]
        )
    ]
    for copy in copies:
        copy.start()
    for copy in copies:
        copy.wait()
    normed = normalise(latent[...], gain[...])
    extra = last_tile(rope[...], table[...])
    payload[:, :width] = normed
    payload[:, width:] = extra
    size = piece.shape[0]
    for k in range(rows // size):

        @pl.when(sub == k)
        def _():
            piece[:, :width] = normed[k * size : (k + 1) * size]
            piece[:, width:] = extra[k * size : (k + 1) * size]


def mid_kernel(sources, piece_sources, gain, tables, length, *rest):
    count = len(sources)
    latents, ropes, pieces = rest[:count], rest[count : 2 * count], rest[2 * count : -1]
    together = rest[-1]
    ctx, sub = lax.axis_index("ctx"), lax.axis_index("sub")

    def origin(source):
        picked = [
            jnp.where((sub == s) & (ctx == j), i + 1, 0)
            for s, edges in enumerate(source)
            for i, j in edges
        ]
        return sum(picked) - 1

    def allowed(start, there):
        return lambda token: (start + token < length[0]) & there

    at = 0
    for latent, rope, source in zip(latents, ropes, sources, strict=True):
        rows, width = latent.shape
        shard = origin(source)
        start = jnp.maximum(shard, 0)
        together[at : at + rows, :width] = normalise(latent[...], gain[...])
        together[at : at + rows, width:] = masked_tile(
            last_tile(rope[...], tables[start]), allowed(start * rows, shard >= 0)
        )
        at += rows
    for piece, edges in zip(pieces, piece_sources, strict=True):
        size, width = piece.shape[0], piece.shape[1] - WIDE
        cores = lax.axis_size("sub")
        shard = origin([edges] * cores)
        together[at : at + size, :width] = piece[:, :width]
        together[at : at + size, width:] = masked_tile(
            piece[:, width:], allowed((shard * cores + sub) * size, shard >= 0)
        )
        at += size


def grow_kernel(step, together, weight, grown):
    width = weight.shape[0]

    @pl.when(lax.axis_index("ctx") > 0)
    def _():
        for k in range(weight.shape[1] // step):
            at = slice(k * step, (k + 1) * step)
            grown[:, at] = jnp.dot(
                together[:, :width], weight[:, at], preferred_element_type=jnp.float32
            ).astype(jnp.bfloat16)


def own_kernel(heads, queries, payload, weight, tables_hbm, expanded, full, table, arrived):
    copy = pltpu.make_async_copy(tables_hbm.at[lax.axis_index("ctx")], table, arrived)
    copy.start()
    copy.wait()
    rows = queries.shape[0]
    width = weight.shape[0]
    cosines = jnp.concatenate([table[:, :ROPE]] * 2, 1)
    sines = jnp.concatenate([table[:, ROPE:]] * 2, 1)
    lane = lax.broadcasted_iota(jnp.int32, (rows, 2 * ROPE), 1)
    lower = lane % ROPE < ROPE // 2
    tail = (lax.broadcasted_iota(jnp.int32, (rows, FULL - NOPE - ROPE), 1) == 0).astype(
        jnp.float32
    ).astype(jnp.bfloat16)
    each = NOPE + ROPE
    for i in range(heads // 2):
        pair = queries[:, 2 * each * i : 2 * each * (i + 1)]
        ropes = jnp.concatenate([pair[:, NOPE:each], pair[:, each + NOPE :]], 1).astype(jnp.float32)
        turned = jnp.where(
            lower, pltpu.roll(ropes, 2 * ROPE - ROPE // 2, 1), pltpu.roll(ropes, ROPE // 2, 1)
        )
        ropes = (ropes * cosines + turned * sines).astype(jnp.bfloat16)
        for e in range(2):
            at = FULL * (2 * i + e)
            full[:, at : at + NOPE] = pair[:, each * e : each * e + NOPE]
            full[:, at + NOPE : at + FULL] = jnp.concatenate(
                [ropes[:, ROPE * e : ROPE * (e + 1)], tail], 1
            )
    columns = NOPE + VDIM
    for i in range(heads // 2):
        at = slice(2 * columns * i, 2 * columns * (i + 1))
        expanded[:, at] = jnp.dot(
            payload[:, :width], weight[:, at], preferred_element_type=jnp.float32
        ).astype(jnp.bfloat16)


def attend_kernel(heads, sets, levels, full, own, expanded, weight, together, fetched, *rest):
    swapped = rest[:-8]
    length, out_hbm, last_own, grown, scores, weights, out, sent = rest[-8:]
    rows = full.shape[0]
    width = weight.shape[0]
    columns = NOPE + VDIM
    ctx = lax.axis_index("ctx")
    row = lax.broadcasted_iota(jnp.int32, (rows, rows), 0)
    causal = lax.broadcasted_iota(jnp.int32, (rows, rows), 1) <= row
    live = ctx * rows + lax.broadcasted_iota(jnp.int32, (rows, 1), 0) < length[0]
    last_own[...] = masked_tile(own[:, width:], lambda token: ctx * rows + token < length[0])
    stage, buffers = 2, 4
    block = VDIM * heads // OUT_COPIES

    def leave(k):
        at = pl.ds(k * block, block)
        return pltpu.make_async_copy(out.at[:, at], out_hbm.at[:, at], sent.at[k])

    def run(used, high):
        every = together.shape[0]
        both = ((0, sets), (sets, every))
        spans = [span for span, use in zip(both, used, strict=True) if use]
        extent = slice(spans[0][0], spans[-1][1]) if spans else slice(0, 0)
        total = rows + sum(end - begin for begin, end in spans) * (1 + len(swapped))

        def rows_of(own_part, direct_part, swapped_part):
            found = [own_part()]
            for begin, end in spans:
                found.append(direct_part(slice(begin, end)))
                for r in range(len(swapped)):
                    found.append(swapped_part(r, slice(begin, end)))
            return found[0] if len(found) == 1 else jnp.concatenate(found, 0)

        def grow(i):
            at = slice(2 * columns * i, 2 * columns * (i + 1))
            for r, ref in enumerate(swapped):
                if spans:
                    grown[i % 4, r, extent] = jnp.dot(
                        ref[extent, :width], weight[:, at], preferred_element_type=jnp.float32
                    ).astype(jnp.bfloat16)

        def column(h, begin, end):
            i, e = divmod(h, 2)
            return rows_of(
                lambda: expanded[:, columns * h + begin : columns * h + end],
                lambda piece: fetched[piece, columns * h + begin : columns * h + end],
                lambda r, piece: grown[i % 4, r, piece, columns * e + begin : columns * e + end],
            )

        def score(h):
            last = rows_of(
                lambda: last_own[...],
                lambda piece: together[piece, width:],
                lambda r, piece: swapped[r][piece, width:],
            )
            found = lax.dot_general(
                full[:high, FULL * h : FULL * (h + 1)],
                jnp.concatenate([column(h, 0, NOPE), last], 1),
                (((1,), (1,)), ((), ())),
                preferred_element_type=jnp.float32,
            )
            scores[h % buffers, :high, :rows] = jnp.where(causal[:high], found[:, :rows], MASKED)
            if total > rows:
                scores[h % buffers, :high, rows:total] = found[:, rows:]

        def soften(h):
            found = scores[h % buffers, :high, :total]
            top = jnp.max(found, 1, keepdims=True)
            raw = jnp.exp2(found * EXPONENT - top * EXPONENT)
            weights[h % buffers, :high, :total] = raw.astype(jnp.bfloat16)
            return jnp.sum(raw, 1, keepdims=True)

        def mix(h, total_h):
            mixed = jnp.dot(
                weights[h % buffers, :high, :total],
                column(h, NOPE, columns),
                preferred_element_type=jnp.float32,
            )
            at = slice(VDIM * h, VDIM * (h + 1))
            out[:high, at] = jnp.where(live[:high], mixed / total_h, 0.0).astype(jnp.bfloat16)
            if high < rows:
                out[high:, at] = jnp.zeros((rows - high, VDIM), jnp.bfloat16)
            if (h + 1) % (heads // OUT_COPIES) == 0:
                leave(h // (heads // OUT_COPIES)).start()

        totals = {}
        steps = heads // stage
        grow(0)
        for t in range(steps + 2):
            if t + 1 < heads // 2:
                grow(t + 1)
            for h in range(stage * t, stage * (t + 1)):
                if t < steps:
                    score(h)
            for h in range(stage * (t - 1), stage * t):
                if 0 <= t - 1 < steps:
                    totals[h] = soften(h)
            for h in range(stage * (t - 2), stage * (t - 1)):
                if 0 <= t - 2 < steps:
                    mix(h, totals.pop(h))

    left = length[0] - ctx * rows

    @pl.when(left <= 0)
    def _():
        out[...] = jnp.zeros_like(out)
        for k in range(OUT_COPIES):
            leave(k).start()

    for used, places in levels:
        here = functools.reduce(jnp.logical_or, [ctx == c for c in places])
        bounds = [0, rows // 2, rows * 3 // 4, rows] if all(used) else [0, rows]
        for low, high in zip(bounds[:-1], bounds[1:], strict=True):
            fits = (left > low) if high == rows else (left > low) & (left <= high)

            @pl.when(here & fits)
            def _():
                run(used, high)

    for k in range(OUT_COPIES):
        leave(k).wait()


def plan(shards, cores):
    colours = []
    for distance in range(shards - 1, 0, -1):
        for source in range(shards - distance):
            target = source + distance
            for colour in colours:
                if all(source != i and target != j for i, j in colour):
                    colour.append((source, target))
                    break
            else:
                colours.append([(source, target)])
    whole = len(colours) // cores * cores
    sets = [colours[k : k + cores] for k in range(0, whole, cores)]
    return sets, colours[whole:]


def in_hbm(x):
    return pltpu.with_memory_space_constraint(x, pltpu.HBM)


def grant(*arrays):
    return pltpu.CompilerParams(vmem_limit_bytes=4 * MIB + 2 * sum(x.size for x in arrays))


def per_device(
    ctx_size, sub_size, queries, latent, rope_keys, latent_gain, up_weight, prompt_length
):
    rows, width = latent.shape
    heads = up_weight.shape[1] // (NOPE + VDIM)
    by_row, by_column = tables(ctx_size * rows)
    by_row = jnp.asarray(by_row.reshape(ctx_size, rows, 2 * ROPE))
    by_column = jnp.asarray(by_column.reshape(ROPE, ctx_size, rows).transpose(1, 0, 2))
    gain = latent_gain.reshape(1, width)
    turned = rope_keys.T
    bf16 = jnp.bfloat16
    wide = width + WIDE

    cores = ("ctx", "sub")
    sets, rest = plan(ctx_size, sub_size)

    def send(data, by_core):
        pairs = [
            (i * sub_size + s, j * sub_size + s) for s, edges in enumerate(by_core) for i, j in edges
        ]
        return lax.ppermute(data, cores, pairs)

    latents = [send(latent, by_core) for by_core in sets]
    ropes = [send(turned, by_core) for by_core in sets]

    payload, piece = pl.pallas_call(
        pack_kernel,
        in_specs=[HBM] * 4,
        out_specs=[VMEM] * 2,
        out_shape=[
            jax.ShapeDtypeStruct((rows, wide), bf16),
            jax.ShapeDtypeStruct((rows // sub_size, wide), bf16),
        ],
        scratch_shapes=[
            pltpu.VMEM((rows, width), bf16),
            pltpu.VMEM((ROPE, rows), bf16),
            pltpu.VMEM((1, width), jnp.float32),
            pltpu.VMEM((ROPE, rows), jnp.float32),
            pltpu.SemaphoreType.DMA((4,)),
        ],
        cost_estimate=pl.CostEstimate(
            flops=PACK_FLOPS, bytes_accessed=8 * rows * width, transcendentals=0
        ),
        compiler_params=grant(),
        name="pack",
    )(in_hbm(latent), in_hbm(turned), in_hbm(gain), in_hbm(by_column))

    pieces = [send(piece, [edges] * sub_size) for edges in rest]

    expanded, full = pl.pallas_call(
        functools.partial(own_kernel, heads),
        in_specs=[VMEM] * 3 + [ANY],
        out_specs=[VMEM] * 2,
        out_shape=[
            jax.ShapeDtypeStruct((rows, up_weight.shape[1]), bf16),
            jax.ShapeDtypeStruct((rows, heads * FULL), bf16),
        ],
        scratch_shapes=[pltpu.VMEM((rows, 2 * ROPE), jnp.float32), pltpu.SemaphoreType.DMA],
        compiler_params=grant(queries, up_weight, payload, up_weight[:rows], up_weight[:rows]),
        name="own",
        cost_estimate=pl.CostEstimate(
            flops=2 * rows * width * up_weight.shape[1],
            bytes_accessed=2 * (queries.size + up_weight.size + 2 * rows * up_weight.shape[1]),
            transcendentals=0,
        ),
    )(queries, payload, up_weight, by_row)

    expanded, prompt_length = lax.optimization_barrier((expanded, prompt_length))
    latents, ropes, pieces, expanded, full = lax.optimization_barrier(
        (latents, ropes, pieces, expanded, full)
    )
    reach = sum(x.shape[0] for x in (*latents, *pieces))
    whole = sum(x.shape[0] for x in latents)
    together = pl.pallas_call(
        functools.partial(mid_kernel, sets, rest),
        in_specs=[VMEM] * 2 + [SMEM] + [VMEM] * (2 * len(latents) + len(pieces)),
        out_specs=VMEM,
        out_shape=jax.ShapeDtypeStruct((reach, wide), bf16),
        compiler_params=grant(by_column, by_column, *latents, *ropes, *pieces, *pieces, *latents),
        name="mid",
    )(gain, by_column, prompt_length, *latents, *ropes, *pieces)

    swapped = []
    for r in range(1, sub_size):
        pairs = [(s, (s + r) % sub_size) for s in range(sub_size)]
        swapped.append(lax.ppermute(together, "sub", pairs))

    fetched = pl.pallas_call(
        functools.partial(grow_kernel, 4 * (NOPE + VDIM)),
        in_specs=[VMEM] * 2,
        out_specs=VMEM,
        out_shape=jax.ShapeDtypeStruct((reach, up_weight.shape[1]), bf16),
        compiler_params=pltpu.CompilerParams(
            vmem_limit_bytes=4 * MIB
            + 2 * (up_weight.size + reach * (wide + up_weight.shape[1]))
        ),
        name="grow",
        cost_estimate=pl.CostEstimate(
            flops=2 * reach * width * up_weight.shape[1],
            bytes_accessed=2 * (up_weight.size + reach * up_weight.shape[1]),
            transcendentals=0,
        ),
    )(together, up_weight)

    parts = [[e for by_core in sets for e in by_core], rest]
    needs = [
        tuple(any(j == c for edges in part for _, j in edges) for part in parts)
        for c in range(ctx_size)
    ]
    levels = [(u, [c for c in range(ctx_size) if needs[c] == u]) for u in sorted(set(needs))]
    total = rows + sub_size * reach
    held = 2 * (up_weight.size + (reach + 2 * rows) * up_weight.shape[1] + total * wide)
    scratch = 8 * total * (NOPE + VDIM) * 2 + 24 * rows * total + 2 * rows * heads * VDIM
    return pl.pallas_call(
        functools.partial(attend_kernel, heads, whole, levels),
        in_specs=[VMEM] * (6 + len(swapped)) + [SMEM],
        out_specs=ANY,
        out_shape=jax.ShapeDtypeStruct((rows, heads * VDIM), bf16),
        scratch_shapes=[
            pltpu.VMEM((rows, WIDE), bf16),
            pltpu.VMEM((4, len(swapped), reach, 2 * (NOPE + VDIM)), bf16),
            pltpu.VMEM((4, rows, total), jnp.float32),
            pltpu.VMEM((4, rows, total), bf16),
            pltpu.VMEM((rows, heads * VDIM), bf16),
            pltpu.SemaphoreType.DMA((OUT_COPIES,)),
        ],
        compiler_params=pltpu.CompilerParams(vmem_limit_bytes=6 * MIB + held + scratch),
        name="attend",
        cost_estimate=pl.CostEstimate(
            flops=2 * total * (width + 2 * rows) * up_weight.shape[1],
            bytes_accessed=2 * (up_weight.size + 3 * rows * up_weight.shape[1]),
            transcendentals=heads * rows * total,
        ),
    )(full, payload, expanded, up_weight, together, fetched, *swapped, prompt_length)


def solution(mesh):
    placed = (
        P(("parts", "ctx"), ("head", "sub")),
        P(("parts", "ctx"), None),
        P(("parts", "ctx"), None),
        P(),
        P(None, ("head", "sub")),
        P("parts"),
    )
    step = jax.shard_map(
        functools.partial(per_device, mesh.shape["ctx"], mesh.shape["sub"]),
        mesh=mesh,
        in_specs=placed,
        out_specs=P(("parts", "ctx"), ("head", "sub")),
        check_vma=False,
    )
    if len(plan(mesh.shape["ctx"], mesh.shape["sub"])[0]) > 1:
        return step
    return step
```
